32 devices in a mesh: dp: 4 (over y, core), blk: 8 (over z, x).
Axes of the slice: x: 2, y: 2, z: 4, core: 2. Of those that a mesh axis runs over, the one named last changes fastest.
Arguments:
- tokens: bfloat16 [4, 3072, 1152], P('dp', 'blk'), may hold values from -6 to 6
- condition: bfloat16 [4, 12, 1152], P('dp'), may hold values from -6 to 6
- cotangent: bfloat16 [4, 3072, 1152], P('dp', 'blk'), may hold values from -6 to 6
- segments: int32 [4, 3072], P('dp', 'blk'), may hold values from 0 to 11, as said below
- kept_patch: int32 [4, 3072], P('dp', 'blk'), may hold values from 0 to 1023, as said below
- res_class: int32 [4, 12], P('dp'), may hold values from 0 to 1, as said below
- pack_order: int32 [4, 12], P('dp'), may hold values from 0 to 11, as said below
- ada_weight: bfloat16 [1152, 6912], P(('dp', 'blk')), may hold values from -0.1875 to 0.1875
- ada_bias: bfloat16 [6912], P(('dp', 'blk')), may hold values from -3 to 3
- qkv_weight: bfloat16 [1152, 3456], P(('dp', 'blk')), may hold values from -0.1875 to 0.1875
- query_bias: bfloat16 [1152], P(('dp', 'blk')), may hold values from -3 to 3
- value_bias: bfloat16 [1152], P(('dp', 'blk')), may hold values from -3 to 3
- proj_weight: bfloat16 [1152, 1152], P(('dp', 'blk')), may hold values from -0.875 to 0.875
- proj_bias: bfloat16 [1152], P(('dp', 'blk')), may hold values from -3 to 3
- hidden_weight: bfloat16 [1152, 4608], P(('dp', 'blk')), may hold values from -0.1875 to 0.1875
- hidden_bias: bfloat16 [4608], P(('dp', 'blk')), may hold values from -3 to 3
- output_weight: bfloat16 [4608, 1152], P(('dp', 'blk')), may hold values from -0.09375 to 0.09375
- output_bias: bfloat16 [1152], P(('dp', 'blk')), may hold values from -3 to 3
Outputs:
- block_out: bfloat16 [4, 3072, 1152], P('dp', 'blk')
- grad_tokens: float32 [4, 3072, 1152], P('dp', 'blk')
- grad_condition: float32 [4, 12, 1152], P('dp')
- grad_ada_weight: float32 [1152, 6912], P(('dp', 'blk'))
- grad_ada_bias: float32 [6912], P(('dp', 'blk'))
- grad_qkv_weight: float32 [1152, 3456], P(('dp', 'blk'))
- grad_query_bias: float32 [1152], P(('dp', 'blk'))
- grad_value_bias: float32 [1152], P(('dp', 'blk'))
- grad_proj_weight: float32 [1152, 1152], P(('dp', 'blk'))
- grad_proj_bias: float32 [1152], P(('dp', 'blk'))
- grad_hidden_weight: float32 [1152, 4608], P(('dp', 'blk'))
- grad_hidden_bias: float32 [4608], P(('dp', 'blk'))
- grad_output_weight: float32 [4608, 1152], P(('dp', 'blk'))
- grad_output_bias: float32 [1152], P(('dp', 'blk'))
The draws below stay inside these ranges and needn't reach their ends.
Inputs may be any that keep to these rules, and one draw needn't show every extreme that they name: `segments`: in each row segment numbers never fall, run through 0 to 11, and segment s holds 512 consecutive tokens if res_class of image pack_order[row, s] is 1, else 128. `res_class`: each row has 4 images of class 1 and 8 of class 0. `pack_order`: each row is a permutation of the row's image numbers. `kept_patch`: within an image the indices are distinct and increasing and lie in its grid of side 32 or 16 by its class; an image keeps half its grid.
All inputs are finite; a program needn't handle non-finite values.
Results may differ from the reference program's by a relative error of at most 0.02.
Values may be sent and summed in bfloat16 or wider, within the bound.
No kernel may reach another device: no remote copies, remote signals or barrier semaphores. Data moves between devices by JAX's collectives and lax.ppermute only.
A program may use at most 256 MiB of HBM per device.

```python
import jax
import jax.numpy as jnp
from jax import lax

MODEL_DIM = 1152
HEADS = 16
FF = 4608
BIG_SIDE = 32
SMALL_SIDE = 16
TOK_DEV = 384
BIG_LEN = 512
SMALL_LEN = 128
PACKED_ROWS = 4
PACKED_ROW_LEN = 3072
GROUPS = 4
SEGS = 12


def choose_patches(patch_key, grid_size, count_kept):
    grid_cells = BIG_SIDE * BIG_SIDE
    shuffled = jax.random.permutation(patch_key, grid_cells).astype(jnp.int32)
    ranking = (shuffled >= grid_size).astype(jnp.int32) * grid_cells + jnp.arange(grid_cells, dtype=jnp.int32)
    picked = shuffled[jnp.argsort(ranking)][:BIG_LEN]
    picked = jnp.where(jnp.arange(BIG_LEN, dtype=jnp.int32) < count_kept, picked, grid_cells)
    return jnp.sort(picked).astype(jnp.int32)


def layout_row(row_key):
    key_big, key_order, key_patch = jax.random.split(row_key, 3)
    big_image = (jax.random.permutation(key_big, SEGS) < GROUPS).astype(jnp.int32)
    placing = jax.random.permutation(key_order, SEGS).astype(jnp.int32)
    seg_big = big_image[placing]
    lengths = jnp.where(seg_big == 1, BIG_LEN, SMALL_LEN).astype(jnp.int32)
    starts = (jnp.cumsum(lengths) - lengths).astype(jnp.int32)
    token_positions = jnp.arange(PACKED_ROW_LEN, dtype=jnp.int32)
    seg_ids = (jnp.sum((starts[None, :] <= token_positions[:, None]).astype(jnp.int32), axis=1) - 1).astype(jnp.int32)
    offsets = (token_positions - starts[seg_ids]).astype(jnp.int32)
    grid_sizes = jnp.where(seg_big == 1, BIG_SIDE * BIG_SIDE, SMALL_SIDE * SMALL_SIDE).astype(jnp.int32)
    seg_keys = jax.random.split(key_patch, SEGS)
    patch_table = jax.vmap(choose_patches)(seg_keys, grid_sizes, lengths)
    retained_index = patch_table[seg_ids, offsets]
    return (big_image, placing, seg_ids, retained_index)


def all_rows(key):
    row_keys = jax.random.split(jax.random.fold_in(key, 11), PACKED_ROWS)
    return jax.vmap(layout_row)(row_keys)


def draw_segments(key, part):
    return all_rows(key)[2]


def draw_kept_patch(key, part):
    return all_rows(key)[3]


def draw_res_class(key, part):
    return all_rows(key)[0]


def draw_pack_order(key, part):
    return all_rows(key)[1]


def steps_of(own_key, shape, cuts, least, largest):
    factor_of, own = 1.0, jax.random.fold_in(own_key, 6)
    for axis_at, parts in cuts:
        heights = jnp.exp(jax.random.uniform(jax.random.fold_in(own, axis_at), (parts,), jnp.float32, least / len(cuts), largest / len(cuts)))
        factor_of = factor_of * jnp.repeat(heights, shape[axis_at] // parts).reshape([-1 if axis == axis_at else 1 for axis in range(len(shape))])
    return factor_of


def centred(own_key, extent, scale, limit, cuts=(), held_as=jnp.bfloat16):
    drawn = scale * jax.random.normal(own_key, extent, jnp.float32)
    if cuts:
        drawn = drawn * steps_of(own_key, extent, cuts, -0.22, 0.18)
    return jnp.clip(drawn, -limit, limit).astype(held_as)


def setup_inputs(seed: int = 0) -> dict:
    key_list = jax.random.split(jax.random.key(seed), 19)
    return {
        "tokens": centred(key_list[0], (PACKED_ROWS, PACKED_ROW_LEN, MODEL_DIM), 1.0, 6.0, ((0, 4), (1, 8))),
        "condition": centred(key_list[1], (PACKED_ROWS, SEGS, MODEL_DIM), 1.0, 6.0, ((0, 4),)),
        "cotangent": centred(key_list[2], (PACKED_ROWS, PACKED_ROW_LEN, MODEL_DIM), 1.0, 6.0, ((0, 4), (1, 8))),
        "segments": draw_segments(jax.random.fold_in(key_list[18], 71), 0),
        "kept_patch": draw_kept_patch(jax.random.fold_in(key_list[18], 71), 0),
        "res_class": draw_res_class(jax.random.fold_in(key_list[18], 71), 0),
        "pack_order": draw_pack_order(jax.random.fold_in(key_list[18], 71), 0),
        "ada_weight": centred(key_list[7], (MODEL_DIM, 6 * MODEL_DIM), MODEL_DIM ** -0.5, 0.1875, ((0, 32),)),
        "ada_bias": centred(key_list[8], (6 * MODEL_DIM,), 0.5, 3.0, ((0, 32),)),
        "qkv_weight": centred(key_list[9], (MODEL_DIM, 3 * MODEL_DIM), MODEL_DIM ** -0.5, 0.1875, ((0, 32),)),
        "query_bias": centred(key_list[10], (MODEL_DIM,), 0.5, 3.0, ((0, 32),)),
        "value_bias": centred(key_list[11], (MODEL_DIM,), 0.5, 3.0, ((0, 32),)),
        "proj_weight": centred(key_list[12], (MODEL_DIM, MODEL_DIM), (max(MODEL_DIM // 24, 4)) ** -0.5, 0.875, ((0, 32),)),
        "proj_bias": centred(key_list[13], (MODEL_DIM,), 0.5, 3.0, ((0, 32),)),
        "hidden_weight": centred(key_list[14], (MODEL_DIM, FF), MODEL_DIM ** -0.5, 0.1875, ((0, 32),)),
        "hidden_bias": centred(key_list[15], (FF,), 0.5, 3.0, ((0, 32),)),
        "output_weight": centred(key_list[16], (FF, MODEL_DIM), FF ** -0.5, 0.09375, ((0, 32),)),
        "output_bias": centred(key_list[17], (MODEL_DIM,), 0.5, 3.0, ((0, 32),)),
    }


@jax.custom_vjp
def low(v):
    return lax.optimization_barrier(v.astype(jnp.bfloat16)).astype(jnp.float32)

@jax.custom_vjp
def low_back(v):
    return v

def low_keep(v):
    return (low(v), None)

def low_pass(kept, grad):
    return (grad,)

def back_keep(v):
    return (v, None)

def back_low(kept, grad):
    return (low(grad),)
low.defvjp(low_keep, low_pass)
low_back.defvjp(back_keep, back_low)

def product(left, right):
    return jnp.dot(left, right, precision=lax.Precision.HIGHEST)

def place_code(retained_index, big_token, model_width):
    grid_side = jnp.where(big_token, BIG_SIDE, SMALL_SIDE).astype(jnp.int32)
    row_pos = (retained_index.astype(jnp.int32) // grid_side).astype(jnp.int32)
    col_pos = (retained_index.astype(jnp.int32) - row_pos * grid_side).astype(jnp.int32)
    quarter = model_width // 4
    frequency = 1.0 / 10000.0 ** (jnp.arange(quarter, dtype=jnp.float32) / quarter)
    across = col_pos.astype(jnp.float32)[:, None] * frequency[None, :]
    downward = row_pos.astype(jnp.float32)[:, None] * frequency[None, :]
    return jnp.concatenate([jnp.sin(across), jnp.cos(across), jnp.sin(downward), jnp.cos(downward)], axis=1)

def layer_norm(values_in):
    centered = values_in - lax.optimization_barrier(jnp.mean(values_in, axis=1, keepdims=True))
    spread = lax.optimization_barrier(jnp.mean(centered * centered, axis=1, keepdims=True))
    return centered * lax.rsqrt(spread + 1e-06)

def attention_row(queries, key_rows, value_rows, segment):
    length = queries.shape[0]
    rows_block = TOK_DEV
    while rows_block * 2 <= 1024 and length % (rows_block * 2) == 0:
        rows_block = rows_block * 2
    blocks = length // rows_block
    score_scale = (MODEL_DIM // HEADS) ** (-0.5)

    def one_block(pieces):
        query_block, seg_block = pieces
        scores = low_back(jnp.einsum('qhd,khd->hqk', query_block, key_rows, precision=lax.Precision.HIGHEST) * score_scale)
        allowed = (seg_block[:, None] == segment[None, :])[None]
        scores = jnp.where(allowed, scores, -1e+30)
        weights_soft = low(jax.nn.softmax(scores, axis=-1))
        return jnp.einsum('hqk,khd->qhd', weights_soft, value_rows, precision=lax.Precision.HIGHEST)
    result = lax.map(jax.checkpoint(one_block), (queries.reshape(blocks, rows_block, HEADS, MODEL_DIM // HEADS), segment.reshape(blocks, rows_block)))
    return result.reshape(length, MODEL_DIM)

def block_forward(params, tokens_row, cond_row, seg_row, kept_row, class_row, order_row):
    ada_weight, ada_bias, qkv_weight, query_bias, value_bias, proj_weight, proj_bias, hidden_weight, hidden_bias, output_weight, output_bias = params
    seg_cond = cond_row[order_row]
    seg_big = class_row[order_row]
    modulation = product(low(jax.nn.silu(seg_cond)), ada_weight) + ada_bias
    per_token = modulation[seg_row]
    shift_attn, scale_attn, gate_attn, shift_mlp, scale_mlp, gate_mlp = jnp.split(per_token, 6, axis=1)
    hidden = tokens_row + place_code(kept_row, seg_big[seg_row] == 1, MODEL_DIM)
    attn_in = low(layer_norm(hidden) * (1.0 + scale_attn) + shift_attn)
    projected = product(attn_in, qkv_weight)
    heads_shape = (hidden.shape[0], HEADS, MODEL_DIM // HEADS)
    queries = low(low_back(projected[:, :MODEL_DIM] + query_bias)).reshape(heads_shape)
    key_rows = low(low_back(projected[:, MODEL_DIM:2 * MODEL_DIM])).reshape(heads_shape)
    value_rows = low(low_back(projected[:, 2 * MODEL_DIM:] + value_bias)).reshape(heads_shape)
    attended = low(low_back(attention_row(queries, key_rows, value_rows, seg_row)))
    branch = low_back(product(attended, proj_weight) + proj_bias)
    after_attn = hidden + gate_attn * branch
    mlp_in = low(layer_norm(after_attn) * (1.0 + scale_mlp) + shift_mlp)
    upper_pre = low_back(product(mlp_in, hidden_weight) + hidden_bias)
    activated = low(jax.nn.gelu(upper_pre, approximate=True))
    lower_out = low_back(product(activated, output_weight) + output_bias)
    return after_attn + gate_mlp * lower_out

def reference(tokens, condition, cotangent, segments, kept_patch, res_class, pack_order, ada_weight, ada_bias, qkv_weight, query_bias, value_bias, proj_weight, proj_bias, hidden_weight, hidden_bias, output_weight, output_bias):
    params = tuple((weight.astype(jnp.float32) for weight in (ada_weight, ada_bias, qkv_weight, query_bias, value_bias, proj_weight, proj_bias, hidden_weight, hidden_bias, output_weight, output_bias)))

    def one_row(running, row_data):
        tokens_row, cond_row, cot_row, seg_row, kept_row, class_row, order_row = row_data

        def apply_row(params_in, input_tokens, cond_in):
            return block_forward(params_in, input_tokens, cond_in, seg_row, kept_row, class_row, order_row)
        out_row, pullback = jax.vjp(apply_row, params, tokens_row, cond_row)
        row_grads, grad_tokens_row, grad_cond_row = pullback(cot_row)
        running = jax.tree.map(jnp.add, running, row_grads)
        return (running, (out_row.astype(jnp.bfloat16), grad_tokens_row, grad_cond_row))
    zero_grads = jax.tree.map(jnp.zeros_like, params)
    summed, outputs = lax.scan(one_row, zero_grads, (tokens.astype(jnp.float32), condition.astype(jnp.float32), cotangent.astype(jnp.float32), segments, kept_patch, res_class, pack_order))
    block_out, grad_tokens, grad_condition = outputs
    return (block_out, grad_tokens, grad_condition, summed[0], summed[1], summed[2], summed[3], summed[4], summed[5], summed[6], summed[7], summed[8], summed[9], summed[10])
```

```python
import jax
import jax.numpy as jnp
from jax import lax
from jax.experimental import pallas as pl
from jax.experimental.pallas import tpu as pltpu
from jax.sharding import PartitionSpec as P

HEADS = 16
BIG_SIDE = 32
SMALL_SIDE = 16
BIG_LEN = 512
SMALL_LEN = 128
BLOCK = 128

BF = jnp.bfloat16
F32 = jnp.float32
HIGHEST = lax.Precision.HIGHEST
VMEM_LIMIT = 60 * 1024 * 1024


def cost(us):
    return pl.CostEstimate(flops=int(us * 1.1e9), transcendentals=0, bytes_accessed=1024)


def dot_nn(a, b):
    return lax.dot_general(a, b, (((1,), (0,)), ((), ())), preferred_element_type=F32)


def dot_nt(a, b):
    return lax.dot_general(a, b, (((1,), (1,)), ((), ())), preferred_element_type=F32)


def dot_tn(a, b):
    return lax.dot_general(a, b, (((0,), (0,)), ((), ())), preferred_element_type=F32)


def swap(v, axis, bit):
    count = lax.axis_size(axis)
    return lax.ppermute(v, axis, [(i, i ^ bit) for i in range(count)])


def swap_exact(v, bit, exact):
    at = v.shape[0] - exact
    high = lax.reduce_precision(v, 8, 7)
    rest = lax.reduce_precision(v[at:] - high[at:], 8, 7)
    got = swap(jnp.concatenate([high, rest], axis=0).astype(BF), "blk", bit).astype(F32)
    return jnp.concatenate([got[:at], got[at : v.shape[0]] + got[v.shape[0] :]], axis=0)


def dp_gather(v):
    core, y = lax.axis_index("dp") % 2, lax.axis_index("dp") // 2
    other = swap(v, "dp", 1)
    pair = jnp.stack([jnp.where(core == 0, v, other), jnp.where(core == 0, other, v)])
    across = swap(pair, "dp", 2)
    return jnp.concatenate([jnp.where(y == 0, pair, across), jnp.where(y == 0, across, pair)])


def pair_up(v, axis, bit_value, bit):
    got = swap(v, axis, bit)
    return jnp.concatenate(
        [jnp.where(bit_value == 0, v, got), jnp.where(bit_value == 0, got, v)], axis=0
    )


def gather_line(shard, z):
    line = pair_up(pair_up(shard, "blk", z // 2, 4), "blk", z % 2, 2)
    return line.reshape(4, *shard.shape)


def gather_cross(line, x, y):
    _, n, width = line.shape
    first = line[:, : n // 2].reshape(-1, width)
    last = line[:, n // 2 :].reshape(-1, width)
    return pair_up(first, "blk", x, 1), pair_up(last, "dp", y, 2)


def gather_wide(first, last, x, y):
    return pair_up(first, "dp", y, 2), pair_up(last, "blk", x, 1)


def both_cores(first, last):
    return first, last, swap(first, "dp", 1), swap(last, "dp", 1)


def unpack_weight(core, parts, rows, groups, name):
    width = parts[0].shape[1]
    half = len(groups) // 2
    n_out = max(o for o, _ in groups) + 1
    widths = [(max(c for o, c in groups if o == k) + 1) * width for k in range(n_out)]

    def body(core_ref, a_own, b_own, a_oth, b_oth, *outs):
        dp = pl.program_id(0)
        for a_ref, b_ref, own in ((a_own, b_own, True), (a_oth, b_oth, False)):

            @pl.when((dp % 2 == core_ref[0]) == own)
            def _(a_ref=a_ref, b_ref=b_ref):
                for z in range(4):
                    for x in range(2):
                        at = (z * 2 + x) * rows
                        for g, (o, c) in enumerate(groups):
                            ref = a_ref if g < half else b_ref
                            start = ((x * 4 + z_place(z)) * half + g % half) * rows
                            columns = slice(c * width, (c + 1) * width)
                            if g < half:
                                outs[o][at : at + rows, columns] = ref[start : start + rows, :]
                            else:
                                outs[o][at : at + rows, columns] = ref[x, 0][
                                    (z_place(z) * half + g % half)
                                    * rows : (z_place(z) * half + g % half + 1)
                                    * rows,
                                    :,
                                ]

    chunk = 8 * half * rows
    by_y = pl.BlockSpec((chunk, width), lambda i, c: (i // 2, 0))
    by_x = pl.BlockSpec((2, 1, chunk // 2, width), lambda i, c: (0, i // 2, 0, 0))
    turned = [p.reshape(2, 2, chunk // 2, width) for p in (parts[1], parts[3])]
    return pl.pallas_call(
        body,
        grid_spec=pltpu.PrefetchScalarGridSpec(
            num_scalar_prefetch=1,
            grid=(4,),
            in_specs=[by_y, by_x, by_y, by_x],
            out_specs=[pl.BlockSpec((8 * rows, w), lambda i, c: (i, 0)) for w in widths],
        ),
        out_shape=[jax.ShapeDtypeStruct((32 * rows, w), BF) for w in widths],
        compiler_params=pltpu.CompilerParams(vmem_limit_bytes=VMEM_LIMIT),
        cost_estimate=cost(10),
        name=name,
    )(core, parts[0], turned[0], parts[2], turned[1])


def unpack_rows(core, parts, rows, name):
    width = parts[0].shape[1]
    half = rows // 2

    def body(core_ref, a_own, b_own, a_oth, b_oth, out):
        dp = pl.program_id(0)
        for a_ref, b_ref, own in ((a_own, b_own, True), (a_oth, b_oth, False)):

            @pl.when((dp % 2 == core_ref[0]) == own)
            def _(a_ref=a_ref, b_ref=b_ref):
                for z in range(4):
                    for x in range(2):
                        at = (z * 2 + x) * rows
                        start = (x * 4 + z_place(z)) * half
                        out[at : at + half, :] = a_ref[start : start + half, :]
                        start = z_place(z) * half
                        out[at + half : at + rows, :] = b_ref[x, 0][start : start + half, :]

    by_y = pl.BlockSpec((8 * half, width), lambda i, c: (i // 2, 0))
    by_x = pl.BlockSpec((2, 1, 4 * half, width), lambda i, c: (0, i // 2, 0, 0))
    turned = [p.reshape(2, 2, 4 * half, width) for p in (parts[1], parts[3])]
    return pl.pallas_call(
        body,
        grid_spec=pltpu.PrefetchScalarGridSpec(
            num_scalar_prefetch=1,
            grid=(4,),
            in_specs=[by_y, by_x, by_y, by_x],
            out_specs=pl.BlockSpec((8 * rows, width), lambda i, c: (i, 0)),
        ),
        out_shape=jax.ShapeDtypeStruct((32 * rows, width), BF),
        compiler_params=pltpu.CompilerParams(vmem_limit_bytes=VMEM_LIMIT),
        cost_estimate=cost(10),
        name=name,
    )(core, parts[0], turned[0], parts[2], turned[1])


def z_place(z):
    return z % 2 * 2 + z // 2


def chip_grads(lefts, rights, products, orders, turned, shape, name):
    tokens, width = shape
    parts = [own.shape[0] // 2 if turned else own.shape[1] for own, _ in lefts]
    height = [
        sum(n for _, _, _, pieces in products for _, n, out, _ in pieces if out == o)
        for o in range(len(orders))
    ]
    n_left, n_right = len(lefts), len(rights)
    product_of = dot_nn if turned else dot_tn

    def body(*refs):
        lefts_own, lefts_oth = refs[:n_left], refs[n_left : 2 * n_left]
        rights_own = refs[2 * n_left : 2 * n_left + n_right]
        rights_oth = refs[2 * n_left + n_right : 2 * n_left + 2 * n_right]
        outs, acc = refs[2 * n_left + 2 * n_right : -1], refs[-1]
        y = pl.program_id(0)
        for li, ri, chunk, pieces in products:
            acc[: 8 * chunk, :] = product_of(
                lefts_own[li][...], rights_own[ri][...]
            ) + product_of(lefts_oth[li][...], rights_oth[ri][...])
            for j in range(8):
                z, x = j // 2, j % 2
                for start, n, out, at in pieces:
                    value = acc[j * chunk + start : j * chunk + start + n, :].astype(BF)
                    if orders[out] == "yxz":
                        row = (x * 4 + z_place(z)) * height[out] + at
                        outs[out][row : row + n, :] = value
                    else:
                        for yy in range(2):
                            row = ((x * 2 + yy) * 4 + z_place(z)) * height[out] + at

                            @pl.when(y == yy)
                            def _(row=row, value=value, out=out, n=n):
                                outs[out][row : row + n, :] = value

    left_specs = [
        pl.BlockSpec((p, tokens) if turned else (tokens, p), lambda i: (i, 0)) for p in parts
    ]
    right_specs = [
        pl.BlockSpec((tokens, width), lambda i, r=r, k=k: (r, k)) for _, _, r, k in rights
    ]
    out_specs, out_shape = [], []
    for order, h in zip(orders, height):
        if order == "yxz":
            out_specs.append(pl.BlockSpec((8 * h, width), lambda i: (i, 0)))
        else:
            out_specs.append(pl.BlockSpec((16 * h, width), lambda i: (0, 0)))
        out_shape.append(jax.ShapeDtypeStruct((16 * h, width), BF))
    total = sum(16 * h for h in height)
    return pl.pallas_call(
        body,
        grid=(2,),
        in_specs=left_specs * 2 + right_specs * 2,
        out_specs=out_specs,
        out_shape=out_shape,
        scratch_shapes=[pltpu.VMEM((max(parts), width), F32)],
        compiler_params=pltpu.CompilerParams(vmem_limit_bytes=VMEM_LIMIT),
        cost_estimate=cost(10),
        name=name,
    )(
        *[own for own, _ in lefts],
        *[oth for _, oth in lefts],
        *[r[0] for r in rights],
        *[r[1] for r in rights],
    )


def split_by(v, bit):
    both = v.reshape(2, v.shape[0] // 2, v.shape[1])
    return (
        lax.dynamic_index_in_dim(both, 1 - bit, 0, keepdims=False),
        lax.dynamic_index_in_dim(both, bit, 0, keepdims=False),
    )


def add(a, b):
    return a.astype(F32) + b.astype(F32)


def send(halves, axis, bit):
    sent, kept = halves
    return kept, swap(sent, axis, bit)


def joined(pair):
    return add(*pair).astype(BF)


def side_by_side(v_a, v_b):
    shape = (4, 1, v_a.shape[0] // 4, v_a.shape[1])
    return jnp.concatenate([v_a.reshape(shape), v_b.reshape(shape)], axis=1).reshape(
        2 * v_a.shape[0], v_a.shape[1]
    )


def head_window(h, size):
    first = h * size // 128
    last = ((h + 1) * size - 1) // 128
    return first * 128, (last + 1) * 128, h * size - first * 128


def lane_mask(shape, start, size):
    lane = lax.broadcasted_iota(jnp.int32, shape, 1)
    return (lane >= start) & (lane < start + size)


def attend_forward(info, queries, keys, values, heads):
    tokens, width = queries.shape[0] // 3, queries.shape[1]
    size = width // heads
    scale = size**-0.5
    blocks = tokens // BLOCK

    def body(info_ref, q_ref, k_ref, v_ref, o_ref, lse_ref):
        def one_block(i, carry):
            row = pl.multiple_of(i * BLOCK, BLOCK)
            start = pl.multiple_of(info_ref[i], BLOCK)

            def run(length):
                lse_all = jnp.zeros((BLOCK, 128), F32)
                for h in range(heads):
                    lo, hi, off = head_window(h, size)
                    q = q_ref[pl.ds(row, BLOCK), lo:hi]
                    mask = lane_mask(q.shape, off, size)
                    q = jnp.where(mask, q, jnp.zeros_like(q))
                    k = k_ref[pl.ds(start, length), lo:hi]
                    v = v_ref[pl.ds(start, length), lo:hi]
                    s = dot_nt(q, k) * scale
                    peak = jnp.max(s, axis=1, keepdims=True)
                    p = jnp.exp(s - peak)
                    total = jnp.sum(p, axis=1, keepdims=True)
                    o = (dot_nn(p.astype(BF), v) * (1.0 / total)).astype(BF)
                    if off == 0:
                        o_ref[pl.ds(row, BLOCK), lo:hi] = o
                    else:
                        o_ref[pl.ds(row, BLOCK), lo:hi] = jnp.where(
                            mask, o, o_ref[pl.ds(row, BLOCK), lo:hi]
                        )
                    lse_all = jnp.where(
                        lane_mask(lse_all.shape, h, 1), peak + jnp.log(total), lse_all
                    )
                lse_ref[pl.ds(row, BLOCK), :] = lse_all

            @pl.when(info_ref[blocks + i] == 1)
            def _():
                run(BIG_LEN)

            @pl.when(info_ref[blocks + i] == 0)
            def _():
                run(SMALL_LEN)

            return carry

        lax.fori_loop(0, blocks, one_block, 0)

    return pl.pallas_call(
        body,
        grid_spec=pltpu.PrefetchScalarGridSpec(
            num_scalar_prefetch=1,
            grid=(1,),
            in_specs=[
                pl.BlockSpec((tokens, width), lambda i, s: (1, 0)),
                pl.BlockSpec((3 * tokens, width), lambda i, s: (0, 0)),
                pl.BlockSpec((3 * tokens, width), lambda i, s: (0, 0)),
            ],
            out_specs=[
                pl.BlockSpec((tokens, width), lambda i, s: (0, 0)),
                pl.BlockSpec((tokens, 128), lambda i, s: (0, 0)),
            ],
        ),
        out_shape=[
            jax.ShapeDtypeStruct((tokens, width), BF),
            jax.ShapeDtypeStruct((tokens, 128), F32),
        ],
        compiler_params=pltpu.CompilerParams(vmem_limit_bytes=VMEM_LIMIT),
        cost_estimate=cost(15),
        name="attend_forward",
    )(info, queries, keys, values)


def backward_pairs(q_ref, g_ref, k_ref, v_ref, dk, dv, heads, size):
    scale = size**-0.5
    width = heads * size

    def term(row, lane):
        at = [width + lane + 2 * heads * k for k in range(3)]
        return sum(g_ref[pl.ds(row, BLOCK), i : i + 1].astype(F32) for i in at)

    def pairs(row, start, length, at, dq, dq_at):
        for h in range(heads):
            lo, hi, off = head_window(h, size)
            q = q_ref[pl.ds(row, BLOCK), lo:hi]
            mask = lane_mask(q.shape, off, size)
            q = jnp.where(mask, q, jnp.zeros_like(q))
            g = g_ref[pl.ds(row, BLOCK), lo:hi]
            g = jnp.where(mask, g, jnp.zeros_like(g))
            k = k_ref[pl.ds(start, length), lo:hi]
            v = v_ref[pl.ds(start, length), lo:hi]
            lse, delta = term(row, h), term(row, heads + h)
            p = jnp.exp(dot_nt(q, k) * scale - lse)
            ds = (p * (dot_nt(g, v) - delta)).astype(BF)
            dv[pl.ds(at, length), lo:hi] += dot_tn(p.astype(BF), g)
            dk[pl.ds(at, length), lo:hi] += dot_tn(ds, q)
            if dq is not None:
                part = dot_nn(ds, k)
                dq[pl.ds(dq_at, BLOCK), lo:hi] += jnp.where(mask, part, jnp.zeros_like(part))

    return pairs


def attend_backward_own(info, queries, keys, values, grads, heads):
    tokens, width = grads.shape[0], queries.shape[1]
    size = width // heads
    scale = size**-0.5
    blocks = tokens // BLOCK

    def body(info_ref, q_ref, k_ref, v_ref, g_ref, dq_ref, dk_ref, dv_ref, dq, dk, dv):
        dq[...] = jnp.zeros_like(dq)
        dk[...] = jnp.zeros_like(dk)
        dv[...] = jnp.zeros_like(dv)
        pairs = backward_pairs(q_ref, g_ref, k_ref, v_ref, dk, dv, heads, size)

        def own_block(i, carry):
            row = pl.multiple_of(i * BLOCK, BLOCK)
            start = pl.multiple_of(info_ref[i], BLOCK)

            @pl.when(info_ref[blocks + i] == 1)
            def _():
                pairs(row, start, BIG_LEN, start, dq, row)

            @pl.when(info_ref[blocks + i] == 0)
            def _():
                pairs(row, start, SMALL_LEN, start, dq, row)

            return carry

        lax.fori_loop(0, blocks, own_block, 0)
        dq_ref[...] = (dq[...] * scale).astype(BF)
        dk_ref[...] = dk[tokens : 2 * tokens, :]
        dv_ref[...] = dv[tokens : 2 * tokens, :]

    full = pl.BlockSpec((3 * tokens, width), lambda i, s: (0, 0))
    own = pl.BlockSpec((tokens, width), lambda i, s: (0, 0))
    return pl.pallas_call(
        body,
        grid_spec=pltpu.PrefetchScalarGridSpec(
            num_scalar_prefetch=1,
            grid=(1,),
            in_specs=[pl.BlockSpec((tokens, width), lambda i, s: (1, 0)), full, full, pl.BlockSpec((tokens, width + 128), lambda i, s: (0, 0))],
            out_specs=[own] * 3,
            scratch_shapes=[
                pltpu.VMEM((tokens, width), F32),
                pltpu.VMEM((3 * tokens, width), F32),
                pltpu.VMEM((3 * tokens, width), F32),
            ],
        ),
        out_shape=[
            jax.ShapeDtypeStruct((tokens, width), BF),
            jax.ShapeDtypeStruct((tokens, width), F32),
            jax.ShapeDtypeStruct((tokens, width), F32),
        ],
        compiler_params=pltpu.CompilerParams(vmem_limit_bytes=VMEM_LIMIT),
        cost_estimate=cost(24),
        name="attend_backward_own",
    )(info, queries, keys, values, grads)


def attend_backward_other(info, queries, keys, values, g_near, g_far, dk_own, dv_own, heads):
    tokens, width = g_near.shape[0], queries.shape[1]
    size = width // heads
    scale = size**-0.5
    blocks = tokens // BLOCK

    def body(
        info_ref, q_near, q_far, k_ref, v_ref, gn, gf, dk_in, dv_in, out_ref, dk, dv
    ):
        dk[...] = dk_in[...]
        dv[...] = dv_in[...]
        for side, (q_ref, g_ref) in enumerate(((q_near, gn), (q_far, gf))):
            pairs = backward_pairs(q_ref, g_ref, k_ref, v_ref, dk, dv, heads, size)

            def one(t, carry, pairs=pairs, side=side):
                a, own = t // blocks, t % blocks

                @pl.when(info_ref[a + 2 * blocks * side] == info_ref[blocks + own])
                def _():
                    at = pl.multiple_of(own * BLOCK, BLOCK)
                    pairs(pl.multiple_of(a * BLOCK, BLOCK), at, BLOCK, at, None, 0)

                return carry

            lax.fori_loop(0, blocks * blocks, one, 0)
        out_ref[:, :width] = (dk[...] * scale).astype(BF)
        out_ref[:, width:] = dv[...].astype(BF)

    own = pl.BlockSpec((tokens, width), lambda i, s: (0, 0))
    near = pl.BlockSpec((tokens, width), lambda i, s: (2 - 2 * s[3 * blocks], 0))
    far = pl.BlockSpec((tokens, width), lambda i, s: (2 * s[3 * blocks], 0))
    middle = pl.BlockSpec((tokens, width), lambda i, s: (1, 0))
    wide = pl.BlockSpec((tokens, width + 128), lambda i, s: (0, 0))
    return pl.pallas_call(
        body,
        grid_spec=pltpu.PrefetchScalarGridSpec(
            num_scalar_prefetch=1,
            grid=(1,),
            in_specs=[near, far, middle, middle, wide, wide, own, own],
            out_specs=pl.BlockSpec((tokens, 2 * width), lambda i, s: (0, 0)),
            scratch_shapes=[pltpu.VMEM((tokens, width), F32), pltpu.VMEM((tokens, width), F32)],
        ),
        out_shape=jax.ShapeDtypeStruct((tokens, 2 * width), BF),
        compiler_params=pltpu.CompilerParams(vmem_limit_bytes=VMEM_LIMIT),
        cost_estimate=cost(22),
        name="attend_backward_other",
    )(info, queries, queries, keys, values, g_near, g_far, dk_own, dv_own)


def layer_norm(v):
    centered = v - jnp.mean(v, axis=1, keepdims=True)
    spread = jnp.mean(centered * centered, axis=1, keepdims=True)
    inverse = lax.rsqrt(spread + 1e-06)
    return centered * inverse, inverse


def norm_back(grad_in, normed, inverse):
    mean_grad = jnp.mean(grad_in, axis=1, keepdims=True)
    mean_proj = jnp.mean(grad_in * normed, axis=1, keepdims=True)
    return inverse * (grad_in - mean_grad - normed * mean_proj)


def column_sum(v):
    return jnp.sum(v.astype(F32), axis=0, keepdims=True)


def whole(shape, dtype=None):
    return pl.BlockSpec(shape, lambda *_: (0,) * len(shape))


def store_turned(core, value, keep_ref, send_ref):
    turned = value.astype(F32).T.astype(BF)
    part = turned.shape[0] // 4
    for c in range(2):

        @pl.when(core == c)
        def _():
            for y in range(2):
                keep_ref[y * part : (y + 1) * part, :] = turned[
                    (2 * y + c) * part : (2 * y + c + 1) * part, :
                ]
                send_ref[y * part : (y + 1) * part, :] = turned[
                    (2 * y + 1 - c) * part : (2 * y + 2 - c) * part, :
                ]


def attention_input(core, parts, places, table, mods):
    tokens, width = parts[0].shape
    blocks = tokens // BLOCK

    def body(core_ref, near, own, far, place_ref, table_ref, mod_ref, in_ref, hid_ref, keep, send):
        steps = lax.broadcasted_iota(jnp.int32, (BIG_SIDE, BLOCK), 0)
        flip = core_ref[1]
        bases = (2 * blocks * (1 - flip), blocks, 2 * blocks * flip)
        for source, base in zip((near, own, far), bases):
            for i in range(blocks):
                b = base + i
                at = pl.ds(pl.multiple_of(b * BLOCK, BLOCK), BLOCK)
                place = jnp.concatenate(
                    [
                        lax.dot_general(
                            (steps == place_ref[r : r + 1, at]).astype(F32),
                            table_ref[...],
                            (((0,), (0,)), ((), ())),
                            precision=HIGHEST,
                            preferred_element_type=F32,
                        )
                        for r in range(2)
                    ],
                    axis=1,
                )
                hidden = source[i * BLOCK : (i + 1) * BLOCK, :].astype(F32) + place
                normed, _ = layer_norm(hidden)
                value = (
                    normed * (1.0 + mod_ref[pl.ds(b, 1), width : 2 * width])
                    + mod_ref[pl.ds(b, 1), :width]
                )
                in_ref[at, :] = value.astype(BF)
                if source is own:
                    hid_ref[i * BLOCK : (i + 1) * BLOCK, :] = hidden
        store_turned(core_ref[0], in_ref[tokens : 2 * tokens, :], keep, send)

    half = jax.ShapeDtypeStruct((width // 2, tokens), BF)
    return pl.pallas_call(
        body,
        grid_spec=pltpu.PrefetchScalarGridSpec(
            num_scalar_prefetch=1,
            grid=(1,),
            in_specs=[whole((tokens, width))] * 3
            + [whole(places.shape), whole(table.shape), whole(mods.shape)],
            out_specs=[
                whole((3 * tokens, width)),
                whole((tokens, width)),
                whole(half.shape),
                whole(half.shape),
            ],
        ),
        out_shape=[
            jax.ShapeDtypeStruct((3 * tokens, width), BF),
            jax.ShapeDtypeStruct((tokens, width), F32),
            half,
            half,
        ],
        compiler_params=pltpu.CompilerParams(vmem_limit_bytes=VMEM_LIMIT),
        cost_estimate=cost(10),
        name="attention_input",
    )(core, *parts, places, table, mods)


def after_attention(core, attn_low, proj, proj_bias, hidden, mods):
    tokens, width = hidden.shape
    blocks = tokens // BLOCK

    def body(
        core_ref, low, w_ref, b_ref, hid, mod, branch, after, mlp_in, keep_m, keep_a, send
    ):
        for b in range(blocks):
            rows = slice(b * BLOCK, (b + 1) * BLOCK)
            value = dot_nn(low[rows, :], w_ref[...]) + b_ref[0:1, :]
            branch[rows, :] = value
            done = hid[rows, :] + mod[b : b + 1, 2 * width : 3 * width] * value
            after[rows, :] = done
            normed, _ = layer_norm(done)
            mlp_in[rows, :] = (
                normed * (1.0 + mod[b : b + 1, 4 * width : 5 * width])
                + mod[b : b + 1, 3 * width : 4 * width]
            ).astype(BF)
        store_turned(core_ref[0], mlp_in[...], keep_m, send.at[: width // 2, :])
        store_turned(core_ref[0], low[...], keep_a, send.at[width // 2 :, :])

    half = jax.ShapeDtypeStruct((width // 2, tokens), BF)
    full = jax.ShapeDtypeStruct((tokens, width), F32)
    return pl.pallas_call(
        body,
        grid_spec=pltpu.PrefetchScalarGridSpec(
            num_scalar_prefetch=1,
            grid=(1,),
            in_specs=[
                whole((tokens, width)),
                whole((width, width)),
                whole((8, width)),
                whole((tokens, width)),
                whole(mods.shape),
            ],
            out_specs=[whole((tokens, width))] * 3 + [whole(half.shape)] * 2 + [whole((width, tokens))],
        ),
        out_shape=[full, full, jax.ShapeDtypeStruct((tokens, width), BF)] + [half] * 2
        + [jax.ShapeDtypeStruct((width, tokens), BF)],
        compiler_params=pltpu.CompilerParams(vmem_limit_bytes=VMEM_LIMIT),
        cost_estimate=cost(8),
        name="after_attention",
    )(core, attn_low, proj, proj_bias, hidden, mods)


def feed_forward_up(order, mlp_in, hidden_w, hidden_b):
    tokens, width = mlp_in.shape

    def body(order_ref, x, wh, bh, keep, send, slope):
        t = pl.program_id(0)
        up = dot_nn(x[...], wh[...]) + bh[0:1, :]
        square = up * up
        wave = jnp.tanh(0.7978845608028654 * up * (1.0 + 0.044715 * square))
        act = (0.5 * up * (1.0 + wave)).astype(BF)
        slope[...] = (
            0.5 * (1.0 + wave)
            + 0.5 * up * (1.0 - wave * wave) * 0.7978845608028654 * (1.0 + 0.134145 * square)
        ).astype(BF)

        @pl.when(t < 2)
        def _():
            send[...] = act

        @pl.when(t >= 2)
        def _():
            keep[...] = act

    return pl.pallas_call(
        body,
        grid_spec=pltpu.PrefetchScalarGridSpec(
            num_scalar_prefetch=1,
            grid=(4,),
            in_specs=[
                whole((tokens, width)),
                pl.BlockSpec((width, width), lambda t, o: (0, o[t])),
                pl.BlockSpec((8, width), lambda t, o: (0, o[t])),
            ],
            out_specs=[
                pl.BlockSpec((tokens, width), lambda t, o: (jnp.maximum(t - 2, 0), 0)),
                pl.BlockSpec((tokens, width), lambda t, o: (jnp.minimum(t, 1), 0)),
                pl.BlockSpec((tokens, width), lambda t, o: (0, o[t])),
            ],
        ),
        out_shape=[
            jax.ShapeDtypeStruct((2 * tokens, width), BF),
            jax.ShapeDtypeStruct((3 * tokens, width), BF),
            jax.ShapeDtypeStruct((tokens, 4 * width), BF),
        ],
        compiler_params=pltpu.CompilerParams(vmem_limit_bytes=VMEM_LIMIT),
        cost_estimate=cost(1),
        name="feed_forward_up",
    )(order, mlp_in, hidden_w, hidden_b)


def feed_forward_down(order, keep, send, output_w, output_b, after, cotangent, mods):
    tokens, width = after.shape
    blocks = tokens // BLOCK

    def body(order_ref, keep_ref, send_ref, wo, bo, after_ref, cot, mod, low, out, sums, acc):
        t = pl.program_id(0)

        @pl.when(t == 0)
        def _():
            acc[...] = dot_nn(send_ref[...], wo[...])

        @pl.when(t == 1)
        def _():
            acc[...] += dot_nn(send_ref[...], wo[...])

        @pl.when(t >= 2)
        def _():
            acc[...] += dot_nn(keep_ref[...], wo[...])

        @pl.when(t == 3)
        def _():
            sums[...] = jnp.zeros_like(sums)
            for b in range(blocks):
                rows = slice(b * BLOCK, (b + 1) * BLOCK)
                gate = mod[b : b + 1, 5 * width : 6 * width]
                lower = acc[rows, :] + bo[0:1, :]
                g = cot[rows, :].astype(F32)
                out[rows, :] = (after_ref[rows, :] + gate * lower).astype(BF)
                low[rows, :] = (g * gate).astype(BF)
                sums[b : b + 1, :] = column_sum(g * lower)
            sums[blocks : blocks + 1, :] = column_sum(low[...])

    row = whole((tokens, width))
    return pl.pallas_call(
        body,
        grid_spec=pltpu.PrefetchScalarGridSpec(
            num_scalar_prefetch=1,
            grid=(4,),
            in_specs=[
                pl.BlockSpec((tokens, width), lambda t, o: (jnp.maximum(t - 2, 0), 0)),
                pl.BlockSpec((tokens, width), lambda t, o: (jnp.minimum(t, 1), 0)),
                pl.BlockSpec((width, width), lambda t, o: (o[t], 0)),
                whole((8, width)),
                row,
                row,
                whole(mods.shape),
            ],
            out_specs=[
                pl.BlockSpec((tokens, width), lambda t, o: (2, 0)),
                row,
                whole((8, width)),
            ],
            scratch_shapes=[pltpu.VMEM((tokens, width), F32)],
        ),
        out_shape=[
            jax.ShapeDtypeStruct((3 * tokens, width), BF),
            jax.ShapeDtypeStruct((tokens, width), BF),
            jax.ShapeDtypeStruct((8, width), F32),
        ],
        input_output_aliases={2: 0},
        compiler_params=pltpu.CompilerParams(vmem_limit_bytes=VMEM_LIMIT),
        cost_estimate=cost(12),
        name="feed_forward_down",
    )(order, keep, send, output_w, output_b, after, cotangent, mods)


def feed_forward_back(
    act_and_lower, slope, hidden_w, output_w, proj, after, branch, attn_low, lse, cotangent, mods, heads
):
    tokens, width = after.shape
    blocks = tokens // BLOCK
    size = width // heads

    def body(
        gl,
        sl,
        wh,
        wo,
        wp,
        after_ref,
        br,
        low,
        lse_ref,
        cot,
        mod,
        gu,
        ga,
        gat,
        up_sums,
        sums,
        acc,
    ):
        t = pl.program_id(0)
        up = (dot_nt(gl[...], wo[...]) * sl[...].astype(F32)).astype(BF)
        gu[:, pl.ds(pl.multiple_of(t * width, 128), width)] = up
        up_sums[...] = jnp.broadcast_to(column_sum(up), up_sums.shape)
        part = dot_nt(up, wh[...])

        @pl.when(t == 0)
        def _():
            acc[...] = part

        @pl.when(t > 0)
        def _():
            acc[...] += part

        @pl.when(t == 3)
        def _():
            sums[...] = jnp.zeros_like(sums)
            head = lax.broadcasted_iota(jnp.int32, (width, 128), 0)
            first = (lax.broadcasted_iota(jnp.int32, (width, 128), 1) - heads) * size
            pick = ((head >= first) & (head < first + size)).astype(BF)
            total = jnp.zeros((1, width), F32)
            for b in range(blocks):
                rows = slice(b * BLOCK, (b + 1) * BLOCK)
                gin = acc[rows, :]
                normed, inverse = layer_norm(after_ref[rows, :])
                value = cot[rows, :].astype(F32) + norm_back(
                    gin * (1.0 + mod[b : b + 1, 4 * width : 5 * width]), normed, inverse
                )
                ga[rows, :] = value
                sums[b : b + 1, :width] = column_sum(value * br[rows, :])
                sums[b : b + 1, width : 2 * width] = column_sum(gin)
                sums[b : b + 1, 2 * width : 3 * width] = column_sum(gin * normed)
                low_branch = (value * mod[b : b + 1, 2 * width : 3 * width]).astype(BF)
                gu[rows, 4 * width :] = low_branch
                total = total + column_sum(low_branch)
                grad = dot_nt(low_branch, wp[...]).astype(BF)
                gat[rows, :width] = grad
                product = grad.astype(F32) * low[rows, :].astype(F32)
                high = product.astype(BF)
                rest = (product - high.astype(F32)).astype(BF)
                value = lse_ref[rows, :] + dot_nn(high, pick) + dot_nn(rest, pick)
                terms = jnp.zeros((BLOCK, 128), F32)
                for k in range(3):
                    term = value.astype(BF).astype(F32)
                    terms = terms + (pltpu.roll(term, 2 * heads * k, axis=1) if k else term)
                    value = value - term
                gat[rows, width:] = terms.astype(BF)
            sums[blocks : blocks + 1, :width] = total

    row = whole((tokens, width))
    return pl.pallas_call(
        body,
        grid=(4,),
        in_specs=[
            pl.BlockSpec((tokens, width), lambda t: (2, 0)),
            pl.BlockSpec((tokens, width), lambda t: (0, t)),
            pl.BlockSpec((width, width), lambda t: (0, t)),
            pl.BlockSpec((width, width), lambda t: (t, 0)),
            whole((width, width)),
            row,
            row,
            row,
            whole((tokens, 128)),
            row,
            whole(mods.shape),
        ],
        out_specs=[
            whole((tokens, 5 * width)),
            row,
            whole((tokens, width + 128)),
            pl.BlockSpec((8, width), lambda t: (0, t)),
            whole((8, 3 * width)),
        ],
        out_shape=[
            jax.ShapeDtypeStruct((tokens, 5 * width), BF),
            jax.ShapeDtypeStruct((tokens, width), F32),
            jax.ShapeDtypeStruct((tokens, width + 128), BF),
            jax.ShapeDtypeStruct((8, 4 * width), F32),
            jax.ShapeDtypeStruct((8, 3 * width), F32),
        ],
        scratch_shapes=[pltpu.VMEM((tokens, width), F32)],
        compiler_params=pltpu.CompilerParams(vmem_limit_bytes=VMEM_LIMIT),
        cost_estimate=cost(24),
        name="feed_forward_back",
    )(
        act_and_lower,
        slope,
        hidden_w,
        output_w,
        proj,
        after,
        branch,
        attn_low,
        lse,
        cotangent,
        mods,
    )


def input_gradient(grads, qkv, hidden, grad_after, mods):
    tokens, width = hidden.shape
    blocks = tokens // BLOCK

    def body(gq, gkv, w_ref, hid, ga, mod, out, sums):
        sums[...] = jnp.zeros_like(sums)
        for b in range(blocks):
            rows = slice(b * BLOCK, (b + 1) * BLOCK)
            gin = (
                dot_nt(gq[rows, :], w_ref[:, :width])
                + dot_nt(gkv[rows, :], w_ref[:, width:])
            )
            normed, inverse = layer_norm(hid[rows, :])
            out[rows, :] = ga[rows, :] + norm_back(
                gin * (1.0 + mod[b : b + 1, width : 2 * width]), normed, inverse
            )
            sums[b : b + 1, :width] = column_sum(gin)
            sums[b : b + 1, width : 2 * width] = column_sum(gin * normed)
        sums[blocks : blocks + 1, :width] = column_sum(gq[...])
        sums[blocks : blocks + 1, width : 2 * width] = column_sum(gkv[:, width:])

    row = whole((tokens, width))
    return pl.pallas_call(
        body,
        grid=(1,),
        in_specs=[row, whole((tokens, 2 * width)), whole(qkv.shape), row, row, whole(mods.shape)],
        out_specs=[row, whole((8, 2 * width))],
        out_shape=[
            jax.ShapeDtypeStruct((tokens, width), F32),
            jax.ShapeDtypeStruct((8, 2 * width), F32),
        ],
        compiler_params=pltpu.CompilerParams(vmem_limit_bytes=VMEM_LIMIT),
        cost_estimate=cost(14),
        name="input_gradient",
    )(*grads, qkv, hidden, grad_after, mods)


def halo(v, fast, after=None):
    count = lax.axis_size("blk")
    if not fast:
        right = lax.ppermute(v, "blk", [(i + 1, i) for i in range(count - 1)])
        return right, lax.ppermute(v, "blk", [(i, i + 1) for i in range(count - 1)])
    near = swap(v, "blk", 1)
    if after is not None:
        near, _ = lax.optimization_barrier((near, after))
    return near, lax.ppermute(near, "blk", halo_hops())


def halo_hops():
    count = lax.axis_size("blk")
    return [(i, i + 2) for i in range(0, count - 2, 2)] + [(i + 2, i) for i in range(1, count - 2, 2)]


def halo_flip(fast):
    return lax.axis_index("blk") % 2 if fast else jnp.int32(0)


def place_table(width):
    quarter = width // 4
    frequency = 1.0 / 10000.0 ** (jnp.arange(quarter, dtype=F32) / quarter)
    angle = jnp.arange(BIG_SIDE, dtype=F32)[:, None] * frequency[None, :]
    return jnp.concatenate([jnp.sin(angle), jnp.cos(angle)], axis=1)


def put_slices(pieces, at, total):
    out = []
    for piece, whole in zip(pieces, total):
        out.append(
            lax.dynamic_update_slice_in_dim(
                jnp.zeros((whole,), F32), piece.astype(F32), at * piece.shape[0], 0
            )
        )
    return jnp.concatenate(out)


def per_device(
    tokens,
    condition,
    cotangent,
    segments,
    kept_patch,
    res_class,
    pack_order,
    ada_weight,
    ada_bias,
    qkv_weight,
    query_bias,
    value_bias,
    proj_weight,
    proj_bias,
    hidden_weight,
    hidden_bias,
    output_weight,
    output_bias,
):
    tokens_dev, width = tokens.shape[1], tokens.shape[2]
    segs = condition.shape[1]
    size_dp, size_blk = lax.axis_size("dp"), lax.axis_size("blk")
    own_dp, own_blk = lax.axis_index("dp"), lax.axis_index("blk")
    own_dev = own_dp * size_blk + own_blk
    count = size_dp * size_blk
    rows = width // count
    barrier = lax.optimization_barrier
    fast = size_dp == 4 and size_blk == 8 and rows % 4 == 0
    everyone = ("dp", "blk")
    blocks = tokens_dev // BLOCK

    first = jnp.concatenate(
        [qkv_weight[:, g * width : (g + 1) * width] for g in range(3)] + [proj_weight], axis=0
    )
    second = jnp.concatenate(
        [hidden_weight[:, g * width : (g + 1) * width] for g in range(4)] + [output_weight], axis=0
    )
    x, z = own_blk % 2, own_blk // 2
    core, y = own_dp % 2, own_dp // 2
    image_ids = jnp.arange(segs, dtype=jnp.int32)
    pick_image = pack_order[0][:, None] == image_ids[None, :]
    seg_cond = jnp.dot(pick_image.astype(BF), condition[0], preferred_element_type=F32)
    seg_big = jnp.sum(jnp.where(pick_image, res_class[0][None, :], 0), axis=1)
    seg_len = jnp.where(seg_big == 1, BIG_LEN, SMALL_LEN).astype(jnp.int32)
    earlier = image_ids[None, :] < image_ids[:, None]
    seg_start = jnp.sum(jnp.where(earlier, seg_len[None, :], 0), axis=1)
    window_start = (own_blk - 1) * tokens_dev
    block_pos = window_start + BLOCK * jnp.arange(3 * blocks, dtype=jnp.int32)
    block_seg = jnp.sum((seg_start[None, :] <= block_pos[:, None]).astype(jnp.int32), axis=1) - 1
    block_seg = jnp.clip(block_seg, 0, segs - 1)
    block_pick = block_seg[:, None] == image_ids[None, :]
    block_big = jnp.sum(jnp.where(block_pick, seg_big[None, :], 0), axis=1)
    block_start = jnp.sum(jnp.where(block_pick, seg_start[None, :], 0), axis=1) - window_start
    inside = (block_pos >= 0) & (block_pos < size_blk * tokens_dev)
    block_id = jnp.where(inside, block_seg, -1)
    block_start = jnp.clip(block_start, 0, 3 * tokens_dev - BLOCK)
    own_pick = block_pick[blocks : 2 * blocks].astype(F32)

    silu_cond, silu_pull = jax.vjp(jax.nn.silu, seg_cond)
    silu_low = silu_cond.astype(BF)
    if fast:
        silu_all = dp_gather(silu_low).reshape(4 * segs, width)
    else:
        silu_all = lax.all_gather(silu_low, "dp", axis=0, tiled=True)
    silu_own = lax.dynamic_slice_in_dim(silu_all.T, own_dev * rows, rows, axis=0)
    partial_mod = dot_tn(silu_own, ada_weight).reshape(size_dp, segs, 6 * width)
    bias_rows = put_slices(
        (query_bias, value_bias, proj_bias, hidden_bias, output_bias, ada_bias),
        own_dev,
        (width, width, width, 4 * width, width, 6 * width),
    )
    bias_rows = jnp.pad(bias_rows, (0, 24 * width - bias_rows.shape[0])).reshape(1, 4, 6 * width)
    partial_mod = jnp.concatenate(
        [partial_mod, jnp.broadcast_to(bias_rows, (size_dp, 4, 6 * width))], axis=1
    )
    if fast:
        by_core = partial_mod.reshape(2, 2, segs + 4, 6 * width)
        sent = lax.dynamic_index_in_dim(by_core, 1 - core, 1, keepdims=False)
        kept = lax.dynamic_index_in_dim(by_core, core, 1, keepdims=False)
        kept = kept + swap(sent, "dp", 1)
        sent = lax.dynamic_index_in_dim(kept, 1 - y, 0, keepdims=False).astype(BF)
        kept = lax.dynamic_index_in_dim(kept, y, 0, keepdims=False)
        row_mod = kept + swap(sent, "dp", 2).astype(F32)
        for bit in (1, 2, 4):
            low = row_mod.astype(BF)
            row_mod = low.astype(F32) + swap(low, "blk", bit).astype(F32)
    else:
        row_mod = lax.psum_scatter(partial_mod, "dp", scatter_dimension=0, tiled=True)[0]
        row_mod = lax.psum(row_mod, "blk")
    if fast:
        core_only = core.reshape(1).astype(jnp.int32)
        first_line = gather_line(first, z)
        first_line, second_shard = barrier((first_line, second[: 4 * rows]))
        first_halves = gather_cross(first_line, x, y)
        second_pair = pair_up(second_shard, "blk", z // 2, 4)
        first_halves, second_pair = barrier((first_halves, second_pair))
        first_halves = gather_wide(*first_halves, x, y)
        second_line = pair_up(second_pair, "blk", z % 2, 2).reshape(4, 4 * rows, width)
    else:
        first_all = lax.all_gather(first, everyone, axis=0, tiled=True)
        second_all = lax.all_gather(second, everyone, axis=0, tiled=True)
        groups = first_all.reshape(count, 4, rows, width).transpose(1, 0, 2, 3)
        groups = groups.reshape(4, width, width)
        full_qkv = jnp.concatenate([groups[0], groups[1], groups[2]], axis=1)
        full_proj = groups[3]
        pair = second_all.reshape(count, 8 * rows, width)
        hid = pair[:, : 4 * rows].reshape(count, 4, rows, width).transpose(0, 2, 1, 3)
        full_hidden = hid.reshape(width, 4 * width)
        full_output = pair[:, 4 * rows :].reshape(4 * width, width)
    bias_flat = row_mod[segs:].reshape(-1)
    full_query_bias = bias_flat[:width]
    full_value_bias = bias_flat[width : 2 * width]
    full_proj_bias = bias_flat[2 * width : 3 * width]
    full_hidden_bias = bias_flat[3 * width : 7 * width]
    full_output_bias = bias_flat[7 * width : 8 * width]
    modulation = row_mod[:segs] + bias_flat[8 * width : 14 * width][None, :]
    block_pick = jnp.pad(block_pick.astype(F32), ((0, 16 - 3 * blocks), (0, 0)))
    mods = jnp.dot(block_pick, modulation, precision=HIGHEST)
    own_mods = mods[blocks : blocks + 8]

    big = jnp.broadcast_to(block_big[:, None], (3 * blocks, BLOCK)).reshape(-1) == 1
    flip = halo_flip(fast)
    kept_near, kept_far = halo(kept_patch[0], fast)
    kept_all = jnp.concatenate(
        [
            jnp.where(flip == 0, kept_far, kept_near),
            kept_patch[0],
            jnp.where(flip == 0, kept_near, kept_far),
        ]
    )
    row_pos = jnp.where(big, kept_all // BIG_SIDE, kept_all // SMALL_SIDE)
    col_pos = kept_all - row_pos * jnp.where(big, BIG_SIDE, SMALL_SIDE)
    places = jnp.concatenate(
        [col_pos[None], row_pos[None], jnp.zeros((6, 3 * tokens_dev), jnp.int32)], axis=0
    )
    own_tokens, _ = barrier((tokens[0], kept_near))
    tokens_near, tokens_far = halo(own_tokens, fast, second_pair if fast else None)
    core = core if fast else jnp.int32(0)
    core_arg = jnp.stack([core, flip]).astype(jnp.int32)
    attn_in_all, hidden, attn_in_keep, attn_in_send = attention_input(
        core_arg, (tokens_near, tokens[0], tokens_far), places, place_table(width), mods
    )

    if fast:
        attn_in_all, first_halves, second_line, third_shard = barrier(
            (attn_in_all, first_halves, second_line, second[4 * rows :])
        )
        first_parts = both_cores(*first_halves)
        second_halves = gather_cross(second_line, x, y)
        third_pair = pair_up(third_shard, "blk", z // 2, 4)
        first_parts, second_halves, third_pair = barrier((first_parts, second_halves, third_pair))
        second_halves = gather_wide(*second_halves, x, y)
        third_line = pair_up(third_pair, "blk", z % 2, 2).reshape(4, 4 * rows, width)
        full_qkv, full_proj = unpack_weight(
            core_only,
            first_parts,
            rows,
            [(0, 0), (0, 1), (0, 2), (1, 0)],
            "unpack_first",
        )
    queries = (dot_nn(attn_in_all, full_qkv[:, :width]) + full_query_bias).astype(BF)
    keys = dot_nn(attn_in_all, full_qkv[:, width : 2 * width]).astype(BF)
    values = (dot_nn(attn_in_all, full_qkv[:, 2 * width :]) + full_value_bias).astype(BF)
    own = slice(tokens_dev, 2 * tokens_dev)
    forward_info = jnp.concatenate(
        [block_start[blocks : 2 * blocks], block_big[blocks : 2 * blocks]]
    ).astype(jnp.int32)
    left_id, own_id, right_id = jnp.split(block_id, 3)
    backward_info = jnp.concatenate(
        [
            jnp.where(flip == 0, right_id, left_id),
            own_id,
            jnp.where(flip == 0, left_id, right_id),
            flip[None],
        ]
    ).astype(jnp.int32)
    if fast:
        queries, second_halves, third_line = barrier((queries, second_halves, third_line))
        second_parts = both_cores(*second_halves)
        third_halves = gather_cross(third_line, x, y)
    attn_low, lse = attend_forward(forward_info, queries, keys, values, HEADS)

    def eight(v):
        return jnp.broadcast_to(v[None, :], (8, v.shape[0]))

    if fast:
        attn_low, second_parts, third_halves = barrier((attn_low, second_parts, third_halves))
        third_halves = gather_wide(*third_halves, x, y)
    branch, after_attn, mlp_in, mlp_keep, low_keep, mlp_low_send = after_attention(
        core_arg, attn_low, full_proj, eight(full_proj_bias), hidden, own_mods
    )
    if fast:
        (full_hidden,) = unpack_weight(
            core_only,
            second_parts,
            rows,
            [(0, 0), (0, 1), (0, 2), (0, 3)],
            "unpack_hidden",
        )
        attn_in_send, mlp_low_send, ada_rows = barrier((attn_in_send, mlp_low_send, ada_weight))
        attn_in_oth, mlp_low_oth = swap(attn_in_send, "dp", 1), swap(mlp_low_send, "dp", 1)
        mlp_in, attn_in_oth, mlp_low_oth = lax.optimization_barrier(
            (mlp_in, attn_in_oth, mlp_low_oth)
        )
    order = jnp.stack([1 - core, 3 - core, core, 2 + core]).astype(jnp.int32)
    act_keep, act_send, slope = feed_forward_up(order, mlp_in, full_hidden, eight(full_hidden_bias))
    if fast:
        act_keep, third_halves = barrier((act_keep, third_halves))
        full_output = unpack_rows(core_only, both_cores(*third_halves), 4 * rows, "unpack_output")
        full_output, ada_rows = barrier((full_output, ada_rows))
        ada_rows = pair_up(ada_rows[None], "dp", core, 1)
    act_and_lower, block_out, lower_sums = feed_forward_down(
        order,
        act_keep,
        act_send,
        full_output,
        eight(full_output_bias),
        after_attn,
        cotangent[0],
        own_mods,
    )

    shape = (tokens_dev, width)
    orders = ["yxz", "xyz"]
    if fast:
        act_and_lower, ada_pair = barrier((act_and_lower, ada_rows))
        act_and_lower_oth = swap(act_and_lower, "dp", 1)
    grad_upper, grad_after, grad_attn, upper_sums, branch_sums = feed_forward_back(
        act_and_lower,
        slope,
        full_hidden,
        full_output,
        full_proj,
        after_attn,
        branch,
        attn_low,
        lse,
        cotangent[0],
        own_mods,
        HEADS,
    )

    def to_segments(sums):
        return lax.dot_general(
            own_pick, sums[:blocks], (((0,), (0,)), ((), ())), precision=HIGHEST
        )

    def early_message():
        bias = jnp.concatenate(
            [
                branch_sums[blocks, :width],
                upper_sums[0],
                lower_sums[blocks],
                jnp.zeros((2 * width,), F32),
            ]
        )
        return jnp.concatenate(
            [
                to_segments(jnp.concatenate([branch_sums, lower_sums], axis=1)),
                bias.reshape(2, 4 * width),
            ],
            axis=0,
        )

    def late_message(sums):
        return jnp.concatenate([to_segments(sums), sums[blocks : blocks + 1]], axis=0)

    if not fast:
        grad_near, grad_far = halo(grad_attn, fast)
    else:

        def half_1(group):
            return split_by(group[0], y), split_by(group[1], x)

        def step_1(halves):
            return send(halves[0], "dp", 2), send(halves[1], "blk", 1)

        def half_2(got):
            return split_by(joined(got[0]), x), split_by(joined(got[1]), y)

        def step_2(halves):
            return send(halves[0], "blk", 1), send(halves[1], "dp", 2)

        def half_3(got):
            return split_by(side_by_side(joined(got[0]), joined(got[1])), z % 2)

        def step_3(halves):
            return send(halves, "blk", 2)

        def half_4(got):
            return split_by(joined(got), z // 2)

        def step_4(halves):
            return send(halves, "blk", 4)

        early = early_message()
        act_keep, grad_upper, grad_attn, early, act_and_lower_oth, ada_pair = barrier(
            (act_keep, grad_upper, grad_attn, early, act_and_lower_oth, ada_pair)
        )
        ada_got = swap(ada_pair, "dp", 2)
        grad_upper_oth = swap(grad_upper, "dp", 1)
        early_got = swap_exact(early, 1, 2)
        grad_near = swap(grad_attn, "blk", 1)
        third = chip_grads(
            [(act_keep, act_and_lower_oth)],
            [(act_and_lower, act_and_lower_oth, 2, 0)],
            [(0, 0, 4 * rows, [(0, 2 * rows, 0, 0), (2 * rows, 2 * rows, 1, 0)])],
            orders,
            False,
            shape,
            "grad_output_weight",
        )

        mlp_keep, third, grad_upper_oth, early, early_got = barrier(
            (mlp_keep, half_1(third), grad_upper_oth, early, early_got)
        )
        third = step_1(third)
        early = early + early_got
        early_got = swap_exact(early, 2, 2)
        second = chip_grads(
            [(mlp_keep, mlp_low_oth)],
            [(grad_upper, grad_upper_oth, 0, g) for g in range(4)],
            [(0, g, rows, [(0, rows, g // 2, g % 2 * rows)]) for g in range(4)],
            orders,
            True,
            shape,
            "grad_hidden_weight",
        )

        grad_attn, second, grad_near, early, early_got = barrier(
            (grad_attn, half_1(second), grad_near, early, early_got)
        )
        grad_far = lax.ppermute(grad_near, "blk", halo_hops())
        early = early + early_got
        early_got = swap_exact(early, 4, 2)
    grad_q, grad_k_own, grad_v_own = attend_backward_own(
        forward_info, queries, keys, values, grad_attn, HEADS
    )
    if fast:
        grad_q, third, grad_far, early, early_got, ada_got = barrier(
            (grad_q, third, grad_far, early, early_got, ada_got)
        )
        grad_q_oth = swap(grad_q, "dp", 1)
        second = step_1(second)
        third = step_2(half_2(third))

        attn_in_keep, grad_q_oth = barrier((attn_in_keep, grad_q_oth))
        early_row = early + early_got
        early_pair = pair_up(early_row[None], "dp", core, 1)
        first = chip_grads(
            [(attn_in_keep, attn_in_oth), (low_keep, mlp_low_oth[width // 2 :])],
            [(grad_q, grad_q_oth, 0, 0), (grad_upper, grad_upper_oth, 0, 4)],
            [(0, 0, rows, [(0, rows, 0, 0)]), (1, 1, rows, [(0, rows, 1, 0)])],
            orders,
            True,
            shape,
            "grad_query_weight",
        )

        grad_near, first, early_pair = barrier((grad_near, half_1(first), early_pair))
        early_all = pair_up(early_pair, "dp", y, 2)
    grad_kv = attend_backward_other(
        backward_info,
        queries,
        keys,
        values,
        grad_near,
        grad_far,
        grad_k_own,
        grad_v_own,
        HEADS,
    )
    if fast:
        grad_kv, hidden, second, third, first, early_all = barrier(
            (grad_kv, hidden, second, third, first, early_all)
        )
        grad_kv_oth = swap(grad_kv, "dp", 1)
        first = step_1(first)
        third = step_3(half_3(third))
    grad_tokens, input_sums = input_gradient(
        (grad_q, grad_kv), full_qkv, hidden, grad_after, own_mods
    )
    if fast:
        late = late_message(input_sums)
        attn_in_keep, grad_kv_oth, third, first, late = barrier(
            (attn_in_keep, grad_kv_oth, third, first, late)
        )
        second = step_2(half_2(second))
        third = step_4(half_4(third))
        late_got = swap_exact(late, 1, 1)
        last = chip_grads(
            [(attn_in_keep, attn_in_oth)],
            [(grad_kv, grad_kv_oth, 0, 0), (grad_kv, grad_kv_oth, 0, 1)],
            [(0, 0, rows, [(0, rows, 0, 0)]), (0, 1, rows, [(0, rows, 1, 0)])],
            orders,
            True,
            shape,
            "grad_key_weight",
        )

        last, second, late, late_got = barrier((half_1(last), second, late, late_got))
        last = step_1(last)
        second = step_3(half_3(second))
        late = late + late_got
        late_got = swap_exact(late, 2, 1)

        last, second, third, late, late_got = barrier((last, second, third, late, late_got))
        third_sum = add(*third)
        first = step_2(half_2(first))
        second = step_4(half_4(second))
        late = late + late_got
        late_got = swap_exact(late, 4, 1)

        last, first, second, late, late_got = barrier((last, first, second, late, late_got))
        second_sum = add(*second)
        last = step_2(half_2(last))
        first = step_3(half_3(first))
        late_row = late + late_got
        ada_rows = jnp.concatenate(
            [jnp.where(y == 0, ada_pair, ada_got), jnp.where(y == 0, ada_got, ada_pair)], axis=0
        ).reshape(4 * rows, 6 * width)
        own_row = jnp.concatenate([late_row[:segs], early_row[:segs]], axis=1)
        row_high = lax.reduce_precision(own_row, 8, 7)
        row_rest = (own_row - row_high).astype(BF)
        part = dot_nt(ada_rows, row_high.astype(BF)) + dot_nt(ada_rows, row_rest)
        part = pair_up(part[None], "blk", z // 2, 4)
        late_pair = pair_up(late_row[None], "dp", core, 1)

        last, first, part, late_pair = barrier((last, first, part, late_pair))
        last = step_3(half_3(last))
        first = step_4(half_4(first))
        part = pair_up(part[None], "blk", z % 2, 2)
        late_all = pair_up(late_pair, "dp", y, 2)

        last, first, part, late_all = barrier((last, first, part, late_all))
        first_sum = add(*first)
        last = step_4(half_4(last))
        part = pair_up(part[None], "blk", x, 1)
        last_sum = add(*last)

    if not fast:
        early_row, late_row = (
            lax.psum(v, "blk") for v in (early_message(), late_message(input_sums))
        )
        early_all, late_all = (
            lax.all_gather(v, "dp", axis=0, tiled=False) for v in (early_row, late_row)
        )
    mod_all = jnp.concatenate([late_all[:, :segs], early_all[:, :segs]], axis=2)
    mod_all = mod_all.reshape(-1, 6 * width)
    early_bias = jnp.sum(early_all[:, segs:], axis=0).reshape(-1)
    late_bias = jnp.sum(late_all[:, segs:], axis=0).reshape(-1)

    def take(v, n):
        return lax.dynamic_slice_in_dim(v, own_dev * n, n)

    grad_query_bias = take(late_bias[:width], rows)
    grad_value_bias = take(late_bias[width:], rows)
    grad_proj_bias = take(early_bias[:width], rows)
    grad_hidden_bias = take(early_bias[width : 5 * width], 4 * rows)
    grad_output_bias = take(early_bias[5 * width : 6 * width], rows)
    grad_ada_bias = take(jnp.sum(mod_all, axis=0), 6 * rows)
    mod_high = mod_all.astype(BF)
    mod_rest = (mod_all - mod_high.astype(F32)).astype(BF)
    grad_ada_weight = dot_nn(silu_own, mod_high) + dot_nn(silu_own, mod_rest)
    if fast:
        part = part.reshape(2, 2, 2, 4, rows, segs).transpose(5, 3, 2, 1, 0, 4)
        own_silu = part.reshape(segs, width)
    else:
        silu_grad = dot_nt(ada_weight, mod_high) + dot_nt(ada_weight, mod_rest)
        silu_rows = lax.all_gather(silu_grad, everyone, axis=0, tiled=True)
        own_silu = lax.dynamic_slice_in_dim(silu_rows, own_dp * segs, segs, axis=1).T
    grad_seg_cond = silu_pull(own_silu)[0]
    grad_image = lax.dot_general(
        pick_image.astype(F32), grad_seg_cond, (((0,), (0,)), ((), ())), precision=HIGHEST
    )

    if fast:
        grad_qkv_weight = jnp.concatenate(
            [first_sum[:rows], last_sum[:rows], last_sum[rows:]], axis=1
        )
        grad_proj_weight = first_sum[rows:]
        grad_hidden_weight = jnp.concatenate(
            [second_sum[g * rows : (g + 1) * rows] for g in range(4)], axis=1
        )
        grad_output_weight = third_sum
    else:

        def scattered(left_t, right):
            product = dot_nn(left_t, right).astype(BF)
            product = lax.psum_scatter(product, "dp", scatter_dimension=0, tiled=True)
            return lax.psum_scatter(product, "blk", scatter_dimension=0, tiled=True).astype(F32)

        def in_order(keep, send):
            both = jnp.stack([keep.reshape(2, -1, tokens_dev), send.reshape(2, -1, tokens_dev)], axis=1)
            return both.reshape(-1, tokens_dev)

        attn_in_t = in_order(attn_in_keep, attn_in_send)
        mlp_send, low_send = mlp_low_send[: width // 2], mlp_low_send[width // 2 :]
        grad_qkv_weight = scattered(attn_in_t, jnp.concatenate([grad_q, grad_kv], axis=1))
        grad_proj_weight = scattered(in_order(low_keep, low_send), grad_upper[:, 4 * width :])
        grad_hidden_weight = scattered(in_order(mlp_keep, mlp_send), grad_upper[:, : 4 * width])
        act_send = act_and_lower[: 2 * tokens_dev]
        grad_lower = act_and_lower[2 * tokens_dev :]
        act = jnp.stack(
            [act_keep.reshape(2, tokens_dev, width), act_send.reshape(2, tokens_dev, width)], axis=1
        ).reshape(4, tokens_dev, width)
        act_t = act.transpose(0, 2, 1).reshape(4 * width, tokens_dev)
        grad_output_weight = scattered(act_t, grad_lower)
    return (
        block_out[None],
        grad_tokens[None],
        grad_image[None],
        grad_ada_weight,
        grad_ada_bias,
        grad_qkv_weight,
        grad_query_bias,
        grad_value_bias,
        grad_proj_weight,
        grad_proj_bias,
        grad_hidden_weight,
        grad_hidden_bias,
        grad_output_weight,
        grad_output_bias,
    )


def solution(mesh):
    row = P("dp", "blk", None)
    ints = P("dp", "blk")
    image = P("dp", None)
    matrix = P(("dp", "blk"), None)
    vector = P(("dp", "blk"))
    return jax.shard_map(
        per_device,
        mesh=mesh,
        in_specs=(
            row,
            P("dp", None, None),
            row,
            ints,
            ints,
            image,
            image,
            matrix,
            vector,
            matrix,
            vector,
            vector,
            matrix,
            vector,
            matrix,
            vector,
            matrix,
            vector,
        ),
        out_specs=(
            row,
            row,
            P("dp", None, None),
            matrix,
            vector,
            matrix,
            vector,
            vector,
            matrix,
            vector,
            matrix,
            vector,
            matrix,
            vector,
        ),
        check_vma=False,
    )
```

```python
import jax
import jax.numpy as jnp
from jax import lax
from jax.experimental import pallas as pl
from jax.experimental.pallas import tpu as pltpu
from jax.sharding import PartitionSpec as P

HEADS = 16
BIG_SIDE = 32
SMALL_SIDE = 16
BIG_LEN = 512
SMALL_LEN = 128
BLOCK = 128

BF = jnp.bfloat16
F32 = jnp.float32
HIGHEST = lax.Precision.HIGHEST
VMEM_LIMIT = 60 * 1024 * 1024


def cost(us):
    return pl.CostEstimate(flops=int(us * 1.1e9), transcendentals=0, bytes_accessed=1024)


def dot_nn(a, b):
    return lax.dot_general(a, b, (((1,), (0,)), ((), ())), preferred_element_type=F32)


def dot_nt(a, b):
    return lax.dot_general(a, b, (((1,), (1,)), ((), ())), preferred_element_type=F32)


def dot_tn(a, b):
    return lax.dot_general(a, b, (((0,), (0,)), ((), ())), preferred_element_type=F32)


def swap(v, axis, bit):
    count = lax.axis_size(axis)
    return lax.ppermute(v, axis, [(i, i ^ bit) for i in range(count)])


def swap_exact(v, bit, exact):
    at = v.shape[0] - exact
    high = lax.reduce_precision(v, 8, 7)
    rest = lax.reduce_precision(v[at:] - high[at:], 8, 7)
    got = swap(jnp.concatenate([high, rest], axis=0).astype(BF), "blk", bit).astype(F32)
    return jnp.concatenate([got[:at], got[at : v.shape[0]] + got[v.shape[0] :]], axis=0)


def dp_gather(v):
    core, y = lax.axis_index("dp") % 2, lax.axis_index("dp") // 2
    other = swap(v, "dp", 1)
    pair = jnp.stack([jnp.where(core == 0, v, other), jnp.where(core == 0, other, v)])
    across = swap(pair, "dp", 2)
    return jnp.concatenate([jnp.where(y == 0, pair, across), jnp.where(y == 0, across, pair)])


def pair_up(v, axis, bit_value, bit):
    got = swap(v, axis, bit)
    return jnp.concatenate(
        [jnp.where(bit_value == 0, v, got), jnp.where(bit_value == 0, got, v)], axis=0
    )


def gather_line(shard, z):
    line = pair_up(pair_up(shard, "blk", z // 2, 4), "blk", z % 2, 2)
    return line.reshape(4, *shard.shape)


def gather_cross(line, x, y):
    _, n, width = line.shape
    first = line[:, : n // 2].reshape(-1, width)
    last = line[:, n // 2 :].reshape(-1, width)
    return pair_up(first, "blk", x, 1), pair_up(last, "dp", y, 2)


def gather_wide(first, last, x, y):
    return pair_up(first, "dp", y, 2), pair_up(last, "blk", x, 1)


def both_cores(first, last):
    return first, last, swap(first, "dp", 1), swap(last, "dp", 1)


def unpack_weight(core, parts, rows, groups, name):
    width = parts[0].shape[1]
    half = len(groups) // 2
    n_out = max(o for o, _ in groups) + 1
    widths = [(max(c for o, c in groups if o == k) + 1) * width for k in range(n_out)]

    def body(core_ref, a_own, b_own, a_oth, b_oth, *outs):
        dp = pl.program_id(0)
        for a_ref, b_ref, own in ((a_own, b_own, True), (a_oth, b_oth, False)):

            @pl.when((dp % 2 == core_ref[0]) == own)
            def _(a_ref=a_ref, b_ref=b_ref):
                for z in range(4):
                    for x in range(2):
                        at = (z * 2 + x) * rows
                        for g, (o, c) in enumerate(groups):
                            ref = a_ref if g < half else b_ref
                            start = ((x * 4 + z_place(z)) * half + g % half) * rows
                            columns = slice(c * width, (c + 1) * width)
                            if g < half:
                                outs[o][at : at + rows, columns] = ref[start : start + rows, :]
                            else:
                                outs[o][at : at + rows, columns] = ref[x, 0][
                                    (z_place(z) * half + g % half)
                                    * rows : (z_place(z) * half + g % half + 1)
                                    * rows,
                                    :,
                                ]

    chunk = 8 * half * rows
    by_y = pl.BlockSpec((chunk, width), lambda i, c: (i // 2, 0))
    by_x = pl.BlockSpec((2, 1, chunk // 2, width), lambda i, c: (0, i // 2, 0, 0))
    turned = [p.reshape(2, 2, chunk // 2, width) for p in (parts[1], parts[3])]
    return pl.pallas_call(
        body,
        grid_spec=pltpu.PrefetchScalarGridSpec(
            num_scalar_prefetch=1,
            grid=(4,),
            in_specs=[by_y, by_x, by_y, by_x],
            out_specs=[pl.BlockSpec((8 * rows, w), lambda i, c: (i, 0)) for w in widths],
        ),
        out_shape=[jax.ShapeDtypeStruct((32 * rows, w), BF) for w in widths],
        compiler_params=pltpu.CompilerParams(vmem_limit_bytes=VMEM_LIMIT),
        cost_estimate=cost(10),
        name=name,
    )(core, parts[0], turned[0], parts[2], turned[1])


def unpack_rows(core, parts, rows, name):
    width = parts[0].shape[1]
    half = rows // 2

    def body(core_ref, a_own, b_own, a_oth, b_oth, out):
        dp = pl.program_id(0)
        for a_ref, b_ref, own in ((a_own, b_own, True), (a_oth, b_oth, False)):

            @pl.when((dp % 2 == core_ref[0]) == own)
            def _(a_ref=a_ref, b_ref=b_ref):
                for z in range(4):
                    for x in range(2):
                        at = (z * 2 + x) * rows
                        start = (x * 4 + z_place(z)) * half
                        out[at : at + half, :] = a_ref[start : start + half, :]
                        start = z_place(z) * half
                        out[at + half : at + rows, :] = b_ref[x, 0][start : start + half, :]

    by_y = pl.BlockSpec((8 * half, width), lambda i, c: (i // 2, 0))
    by_x = pl.BlockSpec((2, 1, 4 * half, width), lambda i, c: (0, i // 2, 0, 0))
    turned = [p.reshape(2, 2, 4 * half, width) for p in (parts[1], parts[3])]
    return pl.pallas_call(
        body,
        grid_spec=pltpu.PrefetchScalarGridSpec(
            num_scalar_prefetch=1,
            grid=(4,),
            in_specs=[by_y, by_x, by_y, by_x],
            out_specs=pl.BlockSpec((8 * rows, width), lambda i, c: (i, 0)),
        ),
        out_shape=jax.ShapeDtypeStruct((32 * rows, width), BF),
        compiler_params=pltpu.CompilerParams(vmem_limit_bytes=VMEM_LIMIT),
        cost_estimate=cost(10),
        name=name,
    )(core, parts[0], turned[0], parts[2], turned[1])


def z_place(z):
    return z % 2 * 2 + z // 2


def chip_grads(bits, lefts, rights, products, orders, turned, shape, name):
    tokens, width = shape
    parts = [own.shape[0] // 2 if turned else own.shape[1] for own, _ in lefts]
    height = [
        sum(n for _, _, _, pieces in products for _, n, out, _ in pieces if out == o)
        for o in range(len(orders))
    ]
    n_left, n_right = len(lefts), len(rights)
    product_of = dot_nn if turned else dot_tn

    def body(bits_ref, *refs):
        lefts_own, lefts_oth = refs[:n_left], refs[n_left : 2 * n_left]
        rights_own = refs[2 * n_left : 2 * n_left + n_right]
        rights_oth = refs[2 * n_left + n_right : 2 * n_left + 2 * n_right]
        outs, acc = refs[2 * n_left + 2 * n_right : -1], refs[-1]
        keep = pl.program_id(0)
        y = jnp.where(keep == 1, bits_ref[1], 1 - bits_ref[1])
        for li, ri, chunk, pieces in products:
            acc[: 8 * chunk, :] = product_of(
                lefts_own[li][...], rights_own[ri][...]
            ) + product_of(lefts_oth[li][...], rights_oth[ri][...])
            for j in range(8):
                z, x = j // 2, j % 2
                for start, n, out, at in pieces:
                    value = acc[j * chunk + start : j * chunk + start + n, :].astype(BF)
                    if orders[out] == "yxz":
                        row = (x * 4 + z_place(z)) * height[out] + at
                        chosen = keep
                    else:
                        row = z_place(z) * height[out] + at
                        chosen = jnp.where(bits_ref[0] == x, 1, 0)
                    for k in range(2):

                        @pl.when(chosen == k)
                        def _(row=row, value=value, out=out, n=n, k=k):
                            ref = outs[2 * out + k]
                            if orders[out] == "yxz":
                                ref[row : row + n, :] = value
                            else:
                                ref[y, row : row + n, :] = value

    left_specs = [
        pl.BlockSpec(
            (p, tokens) if turned else (tokens, p), lambda i, b: (jnp.where(i == 1, b[1], 1 - b[1]), 0)
        )
        for p in parts
    ]
    right_specs = [
        pl.BlockSpec((tokens, width), lambda i, b, r=r, k=k: (r, k)) for _, _, r, k in rights
    ]
    out_specs, out_shape = [], []
    for order, h in zip(orders, height):
        half = (8 * h, width) if order == "yxz" else (2, 4 * h, width)
        out_specs += [whole(half)] * 2
        out_shape += [jax.ShapeDtypeStruct(half, BF)] * 2
    total = sum(16 * h for h in height)
    results = pl.pallas_call(
        body,
        grid_spec=pltpu.PrefetchScalarGridSpec(
            num_scalar_prefetch=1,
            grid=(2,),
            in_specs=left_specs * 2 + right_specs * 2,
            out_specs=out_specs,
            scratch_shapes=[pltpu.VMEM((max(parts), width), F32)],
        ),
        out_shape=out_shape,
        compiler_params=pltpu.CompilerParams(vmem_limit_bytes=VMEM_LIMIT),
        cost_estimate=cost(10),
        name=name,
    )(
        bits,
        *[own for own, _ in lefts],
        *[oth for _, oth in lefts],
        *[r[0] for r in rights],
        *[r[1] for r in rights],
    )
    return [
        tuple(v.reshape(-1, width) for v in results[2 * k : 2 * k + 2]) for k in range(len(orders))
    ]


def split_by(v, bit):
    both = v.reshape(2, v.shape[0] // 2, v.shape[1])
    return (
        lax.dynamic_index_in_dim(both, 1 - bit, 0, keepdims=False),
        lax.dynamic_index_in_dim(both, bit, 0, keepdims=False),
    )


def add(a, b):
    return a.astype(F32) + b.astype(F32)


def send(halves, axis, bit):
    sent, kept = halves
    return kept, swap(sent, axis, bit)


COLUMNS = 1152


def stage_call(body, bits, operands, rows_out, name):
    width = operands[0].shape[1]
    return pl.pallas_call(
        body,
        grid_spec=pltpu.PrefetchScalarGridSpec(
            num_scalar_prefetch=1,
            grid=(width // COLUMNS,),
            in_specs=[pl.BlockSpec((v.shape[0], COLUMNS), lambda i, b: (0, i)) for v in operands],
            out_specs=[pl.BlockSpec((n, COLUMNS), lambda i, b: (0, i)) for n in rows_out],
        ),
        out_shape=[jax.ShapeDtypeStruct((n, width), BF) for n in rows_out],
        compiler_params=pltpu.CompilerParams(vmem_limit_bytes=VMEM_LIMIT),
        cost_estimate=cost(2),
        name=name,
    )(bits, *operands)


def add_and_cut(bits, a, b):
    n = a[0].shape[0] // 2

    def body(bits_ref, a_own, a_got, b_own, b_got, a_sent, a_kept, b_sent, b_kept):
        for own, got, sent, kept, bit in (
            (a_own, a_got, a_sent, a_kept, bits_ref[0]),
            (b_own, b_got, b_sent, b_kept, bits_ref[1]),
        ):
            there = pl.ds(pl.multiple_of((1 - bit) * n, 16), n)
            here = pl.ds(pl.multiple_of(bit * n, 16), n)
            sent[...] = add(own[there, :], got[there, :]).astype(BF)
            kept[...] = add(own[here, :], got[here, :]).astype(BF)

    a_sent, a_kept, b_sent, b_kept = stage_call(body, bits, [*a, *b], [n] * 4, "add_and_cut")
    return (a_sent, a_kept), (b_sent, b_kept)


def add_and_cut_z(bits, a, b):
    h = a[0].shape[0] // 4

    def body(bits_ref, a_own, a_got, b_own, b_got, sent, kept):
        for even in range(2):

            @pl.when(bits_ref[2] == even)
            def _():
                for ref, low in ((sent, 1 - even), (kept, even)):
                    for k in range(2):
                        rows = slice((low * 2 + k) * h, (low * 2 + k + 1) * h)
                        ref[k * 2 * h : k * 2 * h + h, :] = add(
                            a_own[rows, :], a_got[rows, :]
                        ).astype(BF)
                        ref[k * 2 * h + h : (k + 1) * 2 * h, :] = add(
                            b_own[rows, :], b_got[rows, :]
                        ).astype(BF)

    return tuple(stage_call(body, bits, [*a, *b], [4 * h] * 2, "add_and_cut_z"))


def add_and_cut_last(bits, got):
    n = got[0].shape[0] // 2

    def body(bits_ref, own, other, sent, kept):
        for high in range(2):

            @pl.when(bits_ref[3] == high)
            def _():
                there, here = slice((1 - high) * n, (2 - high) * n), slice(high * n, (high + 1) * n)
                sent[...] = add(own[there, :], other[there, :]).astype(BF)
                kept[...] = add(own[here, :], other[here, :]).astype(BF)

    return tuple(stage_call(body, bits, [*got], [n] * 2, "add_and_cut_last"))


def head_window(h, size):
    first = h * size // 128
    last = ((h + 1) * size - 1) // 128
    return first * 128, (last + 1) * 128, h * size - first * 128


def lane_mask(shape, start, size):
    lane = lax.broadcasted_iota(jnp.int32, shape, 1)
    return (lane >= start) & (lane < start + size)


def attend_forward(info, queries, keys, values, heads):
    tokens, width = queries.shape[0] // 3, queries.shape[1]
    size = width // heads
    scale = size**-0.5
    blocks = tokens // BLOCK

    def body(info_ref, q_ref, k_ref, v_ref, o_ref, full_ref, lse_ref):
        def one_block(i, carry):
            row = pl.multiple_of(i * BLOCK, BLOCK)
            start = pl.multiple_of(info_ref[i], BLOCK)

            def run(length):
                lse_all = jnp.zeros((BLOCK, 128), F32)
                for h in range(heads):
                    lo, hi, off = head_window(h, size)
                    q = q_ref[pl.ds(row, BLOCK), lo:hi]
                    mask = lane_mask(q.shape, off, size)
                    q = jnp.where(mask, q, jnp.zeros_like(q))
                    k = k_ref[pl.ds(start, length), lo:hi]
                    v = v_ref[pl.ds(start, length), lo:hi]
                    s = dot_nt(q, k) * scale
                    peak = jnp.max(s, axis=1, keepdims=True)
                    p = jnp.exp(s - peak)
                    total = jnp.sum(p, axis=1, keepdims=True)
                    o = dot_nn(p.astype(BF), v) * (1.0 / total)
                    if off == 0:
                        full_ref[pl.ds(row, BLOCK), lo:hi] = o
                    else:
                        full_ref[pl.ds(row, BLOCK), lo:hi] = jnp.where(
                            mask, o, full_ref[pl.ds(row, BLOCK), lo:hi]
                        )
                    lse_all = jnp.where(
                        lane_mask(lse_all.shape, h, 1), peak + jnp.log(total), lse_all
                    )
                lse_ref[pl.ds(row, BLOCK), :] = lse_all

            @pl.when(info_ref[blocks + i] == 1)
            def _():
                run(BIG_LEN)

            @pl.when(info_ref[blocks + i] == 0)
            def _():
                run(SMALL_LEN)

            return carry

        lax.fori_loop(0, blocks, one_block, 0)
        o_ref[...] = full_ref[...].astype(BF)

    return pl.pallas_call(
        body,
        grid_spec=pltpu.PrefetchScalarGridSpec(
            num_scalar_prefetch=1,
            grid=(1,),
            in_specs=[
                pl.BlockSpec((tokens, width), lambda i, s: (1, 0)),
                pl.BlockSpec((3 * tokens, width), lambda i, s: (0, 0)),
                pl.BlockSpec((3 * tokens, width), lambda i, s: (0, 0)),
            ],
            out_specs=[
                pl.BlockSpec((tokens, width), lambda i, s: (0, 0)),
                pl.BlockSpec((tokens, width), lambda i, s: (0, 0)),
                pl.BlockSpec((tokens, 128), lambda i, s: (0, 0)),
            ],
        ),
        out_shape=[
            jax.ShapeDtypeStruct((tokens, width), BF),
            jax.ShapeDtypeStruct((tokens, width), F32),
            jax.ShapeDtypeStruct((tokens, 128), F32),
        ],
        compiler_params=pltpu.CompilerParams(vmem_limit_bytes=VMEM_LIMIT),
        cost_estimate=cost(15),
        name="attend_forward",
    )(info, queries, keys, values)


def backward_pairs(q_ref, g_ref, k_ref, v_ref, dk, dv, heads, size):
    scale = size**-0.5
    width = heads * size

    def term(row, lane):
        at = [width + lane + 2 * heads * k for k in range(3)]
        return sum(g_ref[pl.ds(row, BLOCK), i : i + 1].astype(F32) for i in at)

    def pairs(row, start, length, at, dq, dq_at):
        for h in range(heads):
            lo, hi, off = head_window(h, size)
            q = q_ref[pl.ds(row, BLOCK), lo:hi]
            mask = lane_mask(q.shape, off, size)
            q = jnp.where(mask, q, jnp.zeros_like(q))
            g = g_ref[pl.ds(row, BLOCK), lo:hi]
            g = jnp.where(mask, g, jnp.zeros_like(g))
            k = k_ref[pl.ds(start, length), lo:hi]
            v = v_ref[pl.ds(start, length), lo:hi]
            lse, delta = term(row, h), term(row, heads + h)
            p = jnp.exp(dot_nt(q, k) * scale - lse)
            ds = (p * (dot_nt(g, v) - delta)).astype(BF)
            dv[pl.ds(at, length), lo:hi] += dot_tn(p.astype(BF), g)
            dk[pl.ds(at, length), lo:hi] += dot_tn(ds, q)
            if dq is not None:
                part = dot_nn(ds, k)
                dq[pl.ds(dq_at, BLOCK), lo:hi] += jnp.where(mask, part, jnp.zeros_like(part))

    return pairs


def attend_backward_own(info, queries, keys, values, grads, heads):
    tokens, width = grads.shape[0], queries.shape[1]
    size = width // heads
    scale = size**-0.5
    blocks = tokens // BLOCK

    def body(info_ref, q_ref, k_ref, v_ref, g_ref, dq_ref, dk_ref, dv_ref, dq, dk, dv):
        dq[...] = jnp.zeros_like(dq)
        dk[...] = jnp.zeros_like(dk)
        dv[...] = jnp.zeros_like(dv)
        pairs = backward_pairs(q_ref, g_ref, k_ref, v_ref, dk, dv, heads, size)

        def own_block(i, carry):
            row = pl.multiple_of(i * BLOCK, BLOCK)
            start = pl.multiple_of(info_ref[i], BLOCK)

            @pl.when(info_ref[blocks + i] == 1)
            def _():
                pairs(row, start, BIG_LEN, start, dq, row)

            @pl.when(info_ref[blocks + i] == 0)
            def _():
                pairs(row, start, SMALL_LEN, start, dq, row)

            return carry

        lax.fori_loop(0, blocks, own_block, 0)
        dq_ref[...] = (dq[...] * scale).astype(BF)
        dk_ref[...] = dk[tokens : 2 * tokens, :]
        dv_ref[...] = dv[tokens : 2 * tokens, :]

    full = pl.BlockSpec((3 * tokens, width), lambda i, s: (0, 0))
    own = pl.BlockSpec((tokens, width), lambda i, s: (0, 0))
    return pl.pallas_call(
        body,
        grid_spec=pltpu.PrefetchScalarGridSpec(
            num_scalar_prefetch=1,
            grid=(1,),
            in_specs=[pl.BlockSpec((tokens, width), lambda i, s: (1, 0)), full, full, pl.BlockSpec((tokens, width + 128), lambda i, s: (0, 0))],
            out_specs=[own] * 3,
            scratch_shapes=[
                pltpu.VMEM((tokens, width), F32),
                pltpu.VMEM((3 * tokens, width), F32),
                pltpu.VMEM((3 * tokens, width), F32),
            ],
        ),
        out_shape=[
            jax.ShapeDtypeStruct((tokens, width), BF),
            jax.ShapeDtypeStruct((tokens, width), F32),
            jax.ShapeDtypeStruct((tokens, width), F32),
        ],
        compiler_params=pltpu.CompilerParams(vmem_limit_bytes=VMEM_LIMIT),
        cost_estimate=cost(24),
        name="attend_backward_own",
    )(info, queries, keys, values, grads)


def attend_backward_other(info, queries, keys, values, g_near, g_far, dk_own, dv_own, heads):
    tokens, width = g_near.shape[0], queries.shape[1]
    size = width // heads
    scale = size**-0.5
    blocks = tokens // BLOCK

    def body(
        info_ref, q_near, q_far, k_ref, v_ref, gn, gf, dk_in, dv_in, out_ref, dk, dv
    ):
        dk[...] = dk_in[...]
        dv[...] = dv_in[...]
        for side, (q_ref, g_ref) in enumerate(((q_near, gn), (q_far, gf))):
            pairs = backward_pairs(q_ref, g_ref, k_ref, v_ref, dk, dv, heads, size)

            def one(t, carry, pairs=pairs, side=side):
                a, own = t // blocks, t % blocks

                @pl.when(info_ref[a + 2 * blocks * side] == info_ref[blocks + own])
                def _():
                    at = pl.multiple_of(own * BLOCK, BLOCK)
                    pairs(pl.multiple_of(a * BLOCK, BLOCK), at, BLOCK, at, None, 0)

                return carry

            lax.fori_loop(0, blocks * blocks, one, 0)
        out_ref[:, :width] = (dk[...] * scale).astype(BF)
        out_ref[:, width:] = dv[...].astype(BF)

    own = pl.BlockSpec((tokens, width), lambda i, s: (0, 0))
    near = pl.BlockSpec((tokens, width), lambda i, s: (2 - 2 * s[3 * blocks], 0))
    far = pl.BlockSpec((tokens, width), lambda i, s: (2 * s[3 * blocks], 0))
    middle = pl.BlockSpec((tokens, width), lambda i, s: (1, 0))
    wide = pl.BlockSpec((tokens, width + 128), lambda i, s: (0, 0))
    return pl.pallas_call(
        body,
        grid_spec=pltpu.PrefetchScalarGridSpec(
            num_scalar_prefetch=1,
            grid=(1,),
            in_specs=[near, far, middle, middle, wide, wide, own, own],
            out_specs=pl.BlockSpec((tokens, 2 * width), lambda i, s: (0, 0)),
            scratch_shapes=[pltpu.VMEM((tokens, width), F32), pltpu.VMEM((tokens, width), F32)],
        ),
        out_shape=jax.ShapeDtypeStruct((tokens, 2 * width), BF),
        compiler_params=pltpu.CompilerParams(vmem_limit_bytes=VMEM_LIMIT),
        cost_estimate=cost(22),
        name="attend_backward_other",
    )(info, queries, queries, keys, values, g_near, g_far, dk_own, dv_own)


def layer_norm(v):
    centered = v - jnp.mean(v, axis=1, keepdims=True)
    spread = jnp.mean(centered * centered, axis=1, keepdims=True)
    inverse = lax.rsqrt(spread + 1e-06)
    return centered * inverse, inverse


def norm_back(grad_in, normed, inverse):
    mean_grad = jnp.mean(grad_in, axis=1, keepdims=True)
    mean_proj = jnp.mean(grad_in * normed, axis=1, keepdims=True)
    return inverse * (grad_in - mean_grad - normed * mean_proj)


def column_sum(v):
    return jnp.sum(v.astype(F32), axis=0, keepdims=True)


def whole(shape, dtype=None):
    return pl.BlockSpec(shape, lambda *_: (0,) * len(shape))


def store_turned(core, value, keep_ref, send_ref):
    turned = value.astype(F32).T.astype(BF)
    part = turned.shape[0] // 4
    for c in range(2):

        @pl.when(core == c)
        def _():
            for y in range(2):
                keep_ref[y * part : (y + 1) * part, :] = turned[
                    (2 * y + c) * part : (2 * y + c + 1) * part, :
                ]
                send_ref[y * part : (y + 1) * part, :] = turned[
                    (2 * y + 1 - c) * part : (2 * y + 2 - c) * part, :
                ]


def attention_input(core, parts, places, table, mods):
    tokens, width = parts[0].shape
    blocks = tokens // BLOCK

    def body(core_ref, near, own, far, place_ref, table_ref, mod_ref, in_ref, hid_ref, keep, send):
        steps = lax.broadcasted_iota(jnp.int32, (BIG_SIDE, BLOCK), 0)
        flip = core_ref[1]
        bases = (2 * blocks * (1 - flip), blocks, 2 * blocks * flip)
        for source, base in zip((near, own, far), bases):
            for i in range(blocks):
                b = base + i
                at = pl.ds(pl.multiple_of(b * BLOCK, BLOCK), BLOCK)
                place = jnp.concatenate(
                    [
                        lax.dot_general(
                            (steps == place_ref[r : r + 1, at]).astype(F32),
                            table_ref[...],
                            (((0,), (0,)), ((), ())),
                            precision=HIGHEST,
                            preferred_element_type=F32,
                        )
                        for r in range(2)
                    ],
                    axis=1,
                )
                hidden = source[i * BLOCK : (i + 1) * BLOCK, :].astype(F32) + place
                normed, _ = layer_norm(hidden)
                value = (
                    normed * (1.0 + mod_ref[pl.ds(b, 1), width : 2 * width])
                    + mod_ref[pl.ds(b, 1), :width]
                )
                in_ref[at, :] = value.astype(BF)
                if source is own:
                    hid_ref[i * BLOCK : (i + 1) * BLOCK, :] = hidden
        store_turned(core_ref[0], in_ref[tokens : 2 * tokens, :], keep, send)

    half = jax.ShapeDtypeStruct((width // 2, tokens), BF)
    return pl.pallas_call(
        body,
        grid_spec=pltpu.PrefetchScalarGridSpec(
            num_scalar_prefetch=1,
            grid=(1,),
            in_specs=[whole((tokens, width))] * 3
            + [whole(places.shape), whole(table.shape), whole(mods.shape)],
            out_specs=[
                whole((3 * tokens, width)),
                whole((tokens, width)),
                whole(half.shape),
                whole(half.shape),
            ],
        ),
        out_shape=[
            jax.ShapeDtypeStruct((3 * tokens, width), BF),
            jax.ShapeDtypeStruct((tokens, width), F32),
            half,
            half,
        ],
        compiler_params=pltpu.CompilerParams(vmem_limit_bytes=VMEM_LIMIT),
        cost_estimate=cost(10),
        name="attention_input",
    )(core, *parts, places, table, mods)


def after_attention(core, attn_low, proj, proj_bias, hidden, mods):
    tokens, width = hidden.shape
    blocks = tokens // BLOCK

    def body(
        core_ref, low, w_ref, b_ref, hid, mod, branch, after, mlp_in, keep_m, keep_a, send
    ):
        for b in range(blocks):
            rows = slice(b * BLOCK, (b + 1) * BLOCK)
            value = dot_nn(low[rows, :], w_ref[...]) + b_ref[0:1, :]
            branch[rows, :] = value
            done = hid[rows, :] + mod[b : b + 1, 2 * width : 3 * width] * value
            after[rows, :] = done
            normed, _ = layer_norm(done)
            mlp_in[rows, :] = (
                normed * (1.0 + mod[b : b + 1, 4 * width : 5 * width])
                + mod[b : b + 1, 3 * width : 4 * width]
            ).astype(BF)
        store_turned(core_ref[0], mlp_in[...], keep_m, send.at[: width // 2, :])
        store_turned(core_ref[0], low[...], keep_a, send.at[width // 2 :, :])

    half = jax.ShapeDtypeStruct((width // 2, tokens), BF)
    full = jax.ShapeDtypeStruct((tokens, width), F32)
    return pl.pallas_call(
        body,
        grid_spec=pltpu.PrefetchScalarGridSpec(
            num_scalar_prefetch=1,
            grid=(1,),
            in_specs=[
                whole((tokens, width)),
                whole((width, width)),
                whole((8, width)),
                whole((tokens, width)),
                whole(mods.shape),
            ],
            out_specs=[whole((tokens, width))] * 3 + [whole(half.shape)] * 2 + [whole((width, tokens))],
        ),
        out_shape=[full, full, jax.ShapeDtypeStruct((tokens, width), BF)] + [half] * 2
        + [jax.ShapeDtypeStruct((width, tokens), BF)],
        compiler_params=pltpu.CompilerParams(vmem_limit_bytes=VMEM_LIMIT),
        cost_estimate=cost(8),
        name="after_attention",
    )(core, attn_low, proj, proj_bias, hidden, mods)


def feed_forward_up(order, mlp_in, hidden_w, hidden_b):
    tokens, width = mlp_in.shape

    def body(order_ref, x, wh, bh, keep, send, slope):
        t = pl.program_id(0)
        up = dot_nn(x[...], wh[...]) + bh[0:1, :]
        square = up * up
        wave = jnp.tanh(0.7978845608028654 * up * (1.0 + 0.044715 * square))
        act = (0.5 * up * (1.0 + wave)).astype(BF)
        slope[...] = (
            0.5 * (1.0 + wave)
            + 0.5 * up * (1.0 - wave * wave) * 0.7978845608028654 * (1.0 + 0.134145 * square)
        ).astype(BF)

        @pl.when(t < 2)
        def _():
            send[...] = act

        @pl.when(t >= 2)
        def _():
            keep[...] = act

    return pl.pallas_call(
        body,
        grid_spec=pltpu.PrefetchScalarGridSpec(
            num_scalar_prefetch=1,
            grid=(4,),
            in_specs=[
                whole((tokens, width)),
                pl.BlockSpec((width, width), lambda t, o: (0, o[t])),
                pl.BlockSpec((8, width), lambda t, o: (0, o[t])),
            ],
            out_specs=[
                pl.BlockSpec((tokens, width), lambda t, o: (jnp.maximum(t - 2, 0), 0)),
                pl.BlockSpec((tokens, width), lambda t, o: (jnp.minimum(t, 1), 0)),
                pl.BlockSpec((tokens, width), lambda t, o: (0, o[t])),
            ],
        ),
        out_shape=[
            jax.ShapeDtypeStruct((2 * tokens, width), BF),
            jax.ShapeDtypeStruct((2 * tokens, width), BF),
            jax.ShapeDtypeStruct((tokens, 4 * width), BF),
        ],
        compiler_params=pltpu.CompilerParams(vmem_limit_bytes=VMEM_LIMIT),
        cost_estimate=cost(14),
        name="feed_forward_up",
    )(order, mlp_in, hidden_w, hidden_b)


def feed_forward_down(order, keep, send, output_w, output_b, after, cotangent, mods):
    tokens, width = after.shape
    blocks = tokens // BLOCK

    def body(order_ref, keep_ref, send_ref, wo, bo, after_ref, cot, mod, low, out, sums, acc):
        t = pl.program_id(0)

        @pl.when(t == 0)
        def _():
            acc[...] = dot_nn(send_ref[...], wo[...])

        @pl.when(t == 1)
        def _():
            acc[...] += dot_nn(send_ref[...], wo[...])

        @pl.when(t >= 2)
        def _():
            acc[...] += dot_nn(keep_ref[...], wo[...])

        @pl.when(t == 3)
        def _():
            sums[...] = jnp.zeros_like(sums)
            for b in range(blocks):
                rows = slice(b * BLOCK, (b + 1) * BLOCK)
                gate = mod[b : b + 1, 5 * width : 6 * width]
                lower = acc[rows, :] + bo[0:1, :]
                g = cot[rows, :].astype(F32)
                out[rows, :] = (after_ref[rows, :] + gate * lower).astype(BF)
                low[rows, :] = (g * gate).astype(BF)
                sums[b : b + 1, :] = column_sum(g * lower)
            sums[blocks : blocks + 1, :] = column_sum(low[...])

    row = whole((tokens, width))
    return pl.pallas_call(
        body,
        grid_spec=pltpu.PrefetchScalarGridSpec(
            num_scalar_prefetch=1,
            grid=(4,),
            in_specs=[
                pl.BlockSpec((tokens, width), lambda t, o: (jnp.maximum(t - 2, 0), 0)),
                pl.BlockSpec((tokens, width), lambda t, o: (jnp.minimum(t, 1), 0)),
                pl.BlockSpec((width, width), lambda t, o: (o[t], 0)),
                whole((8, width)),
                row,
                row,
                whole(mods.shape),
            ],
            out_specs=[
                row,
                row,
                whole((8, width)),
            ],
            scratch_shapes=[pltpu.VMEM((tokens, width), F32)],
        ),
        out_shape=[
            jax.ShapeDtypeStruct((tokens, width), BF),
            jax.ShapeDtypeStruct((tokens, width), BF),
            jax.ShapeDtypeStruct((8, width), F32),
        ],
        compiler_params=pltpu.CompilerParams(vmem_limit_bytes=VMEM_LIMIT),
        cost_estimate=cost(12),
        name="feed_forward_down",
    )(order, keep, send, output_w, output_b, after, cotangent, mods)


def feed_forward_back(
    grad_lower, slope, hidden_w, output_w, proj, after, branch, attended, lse, cotangent, mods, heads
):
    tokens, width = after.shape
    blocks = tokens // BLOCK
    size = width // heads

    def body(
        gl,
        sl,
        wh,
        wo,
        wp,
        after_ref,
        br,
        low,
        lse_ref,
        cot,
        mod,
        gu,
        ga,
        gat,
        up_sums,
        sums,
        acc,
    ):
        t = pl.program_id(0)
        up = (dot_nt(gl[...], wo[...]) * sl[...].astype(F32)).astype(BF)
        gu[:, pl.ds(pl.multiple_of(t * width, 128), width)] = up
        up_sums[...] = jnp.broadcast_to(column_sum(up), up_sums.shape)
        part = dot_nt(up, wh[...])

        @pl.when(t == 0)
        def _():
            acc[...] = part

        @pl.when(t > 0)
        def _():
            acc[...] += part

        @pl.when(t == 3)
        def _():
            sums[...] = jnp.zeros_like(sums)
            head = lax.broadcasted_iota(jnp.int32, (width, 128), 0)
            first = (lax.broadcasted_iota(jnp.int32, (width, 128), 1) - heads) * size
            pick = ((head >= first) & (head < first + size)).astype(BF)
            total = jnp.zeros((1, width), F32)
            for b in range(blocks):
                rows = slice(b * BLOCK, (b + 1) * BLOCK)
                gin = acc[rows, :]
                normed, inverse = layer_norm(after_ref[rows, :])
                value = cot[rows, :].astype(F32) + norm_back(
                    gin * (1.0 + mod[b : b + 1, 4 * width : 5 * width]), normed, inverse
                )
                ga[rows, :] = value
                sums[b : b + 1, :width] = column_sum(value * br[rows, :])
                sums[b : b + 1, width : 2 * width] = column_sum(gin)
                sums[b : b + 1, 2 * width : 3 * width] = column_sum(gin * normed)
                low_branch = (value * mod[b : b + 1, 2 * width : 3 * width]).astype(BF)
                gu[rows, 4 * width :] = low_branch
                total = total + column_sum(low_branch)
                grad = dot_nt(low_branch, wp[...]).astype(BF)
                gat[rows, :width] = grad
                product = grad.astype(F32) * low[rows, :]
                high = product.astype(BF)
                rest = (product - high.astype(F32)).astype(BF)
                value = lse_ref[rows, :] + dot_nn(high, pick) + dot_nn(rest, pick)
                terms = jnp.zeros((BLOCK, 128), F32)
                for k in range(3):
                    term = value.astype(BF).astype(F32)
                    terms = terms + (pltpu.roll(term, 2 * heads * k, axis=1) if k else term)
                    value = value - term
                gat[rows, width:] = terms.astype(BF)
            sums[blocks : blocks + 1, :width] = total

    row = whole((tokens, width))
    return pl.pallas_call(
        body,
        grid=(4,),
        in_specs=[
            row,
            pl.BlockSpec((tokens, width), lambda t: (0, t)),
            pl.BlockSpec((width, width), lambda t: (0, t)),
            pl.BlockSpec((width, width), lambda t: (t, 0)),
            whole((width, width)),
            row,
            row,
            row,
            whole((tokens, 128)),
            row,
            whole(mods.shape),
        ],
        out_specs=[
            whole((tokens, 5 * width)),
            row,
            whole((tokens, width + 128)),
            pl.BlockSpec((8, width), lambda t: (0, t)),
            whole((8, 3 * width)),
        ],
        out_shape=[
            jax.ShapeDtypeStruct((tokens, 5 * width), BF),
            jax.ShapeDtypeStruct((tokens, width), F32),
            jax.ShapeDtypeStruct((tokens, width + 128), BF),
            jax.ShapeDtypeStruct((8, 4 * width), F32),
            jax.ShapeDtypeStruct((8, 3 * width), F32),
        ],
        scratch_shapes=[pltpu.VMEM((tokens, width), F32)],
        compiler_params=pltpu.CompilerParams(vmem_limit_bytes=VMEM_LIMIT),
        cost_estimate=cost(24),
        name="feed_forward_back",
    )(
        grad_lower,
        slope,
        hidden_w,
        output_w,
        proj,
        after,
        branch,
        attended,
        lse,
        cotangent,
        mods,
    )


def input_gradient(grads, qkv, hidden, grad_after, mods):
    tokens, width = hidden.shape
    blocks = tokens // BLOCK

    def body(gq, gkv, w_ref, hid, ga, mod, out, sums):
        sums[...] = jnp.zeros_like(sums)
        for b in range(blocks):
            rows = slice(b * BLOCK, (b + 1) * BLOCK)
            gin = (
                dot_nt(gq[rows, :], w_ref[:, :width])
                + dot_nt(gkv[rows, :], w_ref[:, width:])
            )
            normed, inverse = layer_norm(hid[rows, :])
            out[rows, :] = ga[rows, :] + norm_back(
                gin * (1.0 + mod[b : b + 1, width : 2 * width]), normed, inverse
            )
            sums[b : b + 1, :width] = column_sum(gin)
            sums[b : b + 1, width : 2 * width] = column_sum(gin * normed)
        sums[blocks : blocks + 1, :width] = column_sum(gq[...])
        sums[blocks : blocks + 1, width : 2 * width] = column_sum(gkv[:, width:])

    row = whole((tokens, width))
    return pl.pallas_call(
        body,
        grid=(1,),
        in_specs=[row, whole((tokens, 2 * width)), whole(qkv.shape), row, row, whole(mods.shape)],
        out_specs=[row, whole((8, 2 * width))],
        out_shape=[
            jax.ShapeDtypeStruct((tokens, width), F32),
            jax.ShapeDtypeStruct((8, 2 * width), F32),
        ],
        compiler_params=pltpu.CompilerParams(vmem_limit_bytes=VMEM_LIMIT),
        cost_estimate=cost(14),
        name="input_gradient",
    )(*grads, qkv, hidden, grad_after, mods)


def halo(v, fast, after=None):
    count = lax.axis_size("blk")
    if not fast:
        right = lax.ppermute(v, "blk", [(i + 1, i) for i in range(count - 1)])
        return right, lax.ppermute(v, "blk", [(i, i + 1) for i in range(count - 1)])
    near = swap(v, "blk", 1)
    if after is not None:
        near, _ = lax.optimization_barrier((near, after))
    return near, lax.ppermute(near, "blk", halo_hops())


def halo_hops():
    count = lax.axis_size("blk")
    return [(i, i + 2) for i in range(0, count - 2, 2)] + [(i + 2, i) for i in range(1, count - 2, 2)]


def halo_flip(fast):
    return lax.axis_index("blk") % 2 if fast else jnp.int32(0)


def place_table(width):
    quarter = width // 4
    frequency = 1.0 / 10000.0 ** (jnp.arange(quarter, dtype=F32) / quarter)
    angle = jnp.arange(BIG_SIDE, dtype=F32)[:, None] * frequency[None, :]
    return jnp.concatenate([jnp.sin(angle), jnp.cos(angle)], axis=1)


def put_slices(pieces, at, total):
    out = []
    for piece, whole in zip(pieces, total):
        out.append(
            lax.dynamic_update_slice_in_dim(
                jnp.zeros((whole,), F32), piece.astype(F32), at * piece.shape[0], 0
            )
        )
    return jnp.concatenate(out)


def per_device(
    tokens,
    condition,
    cotangent,
    segments,
    kept_patch,
    res_class,
    pack_order,
    ada_weight,
    ada_bias,
    qkv_weight,
    query_bias,
    value_bias,
    proj_weight,
    proj_bias,
    hidden_weight,
    hidden_bias,
    output_weight,
    output_bias,
):
    tokens_dev, width = tokens.shape[1], tokens.shape[2]
    segs = condition.shape[1]
    size_dp, size_blk = lax.axis_size("dp"), lax.axis_size("blk")
    own_dp, own_blk = lax.axis_index("dp"), lax.axis_index("blk")
    own_dev = own_dp * size_blk + own_blk
    count = size_dp * size_blk
    rows = width // count
    barrier = lax.optimization_barrier
    fast = size_dp == 4 and size_blk == 8 and rows % 4 == 0
    everyone = ("dp", "blk")
    blocks = tokens_dev // BLOCK

    first = jnp.concatenate(
        [qkv_weight[:, g * width : (g + 1) * width] for g in range(3)] + [proj_weight], axis=0
    )
    second = jnp.concatenate(
        [hidden_weight[:, g * width : (g + 1) * width] for g in range(4)] + [output_weight], axis=0
    )
    x, z = own_blk % 2, own_blk // 2
    core, y = own_dp % 2, own_dp // 2
    image_ids = jnp.arange(segs, dtype=jnp.int32)
    pick_image = pack_order[0][:, None] == image_ids[None, :]
    seg_cond = jnp.dot(pick_image.astype(BF), condition[0], preferred_element_type=F32)
    seg_big = jnp.sum(jnp.where(pick_image, res_class[0][None, :], 0), axis=1)
    seg_len = jnp.where(seg_big == 1, BIG_LEN, SMALL_LEN).astype(jnp.int32)
    earlier = image_ids[None, :] < image_ids[:, None]
    seg_start = jnp.sum(jnp.where(earlier, seg_len[None, :], 0), axis=1)
    window_start = (own_blk - 1) * tokens_dev
    block_pos = window_start + BLOCK * jnp.arange(3 * blocks, dtype=jnp.int32)
    block_seg = jnp.sum((seg_start[None, :] <= block_pos[:, None]).astype(jnp.int32), axis=1) - 1
    block_seg = jnp.clip(block_seg, 0, segs - 1)
    block_pick = block_seg[:, None] == image_ids[None, :]
    block_big = jnp.sum(jnp.where(block_pick, seg_big[None, :], 0), axis=1)
    block_start = jnp.sum(jnp.where(block_pick, seg_start[None, :], 0), axis=1) - window_start
    inside = (block_pos >= 0) & (block_pos < size_blk * tokens_dev)
    block_id = jnp.where(inside, block_seg, -1)
    block_start = jnp.clip(block_start, 0, 3 * tokens_dev - BLOCK)
    own_pick = block_pick[blocks : 2 * blocks].astype(F32)

    silu_cond, silu_pull = jax.vjp(jax.nn.silu, seg_cond)
    silu_low = silu_cond.astype(BF)
    if fast:
        silu_all = dp_gather(silu_low).reshape(4 * segs, width)
    else:
        silu_all = lax.all_gather(silu_low, "dp", axis=0, tiled=True)
    silu_own = lax.dynamic_slice_in_dim(silu_all.T, own_dev * rows, rows, axis=0)
    partial_mod = dot_tn(silu_own, ada_weight).reshape(size_dp, segs, 6 * width)
    bias_rows = put_slices(
        (query_bias, value_bias, proj_bias, hidden_bias, output_bias, ada_bias),
        own_dev,
        (width, width, width, 4 * width, width, 6 * width),
    )
    bias_rows = jnp.pad(bias_rows, (0, 24 * width - bias_rows.shape[0])).reshape(1, 4, 6 * width)
    partial_mod = jnp.concatenate(
        [partial_mod, jnp.broadcast_to(bias_rows, (size_dp, 4, 6 * width))], axis=1
    )
    if fast:
        by_core = partial_mod.reshape(2, 2, segs + 4, 6 * width)
        sent = lax.dynamic_index_in_dim(by_core, 1 - core, 1, keepdims=False)
        kept = lax.dynamic_index_in_dim(by_core, core, 1, keepdims=False)
        kept = kept + swap(sent, "dp", 1)
        sent = lax.dynamic_index_in_dim(kept, 1 - y, 0, keepdims=False).astype(BF)
        kept = lax.dynamic_index_in_dim(kept, y, 0, keepdims=False)
        row_mod = kept + swap(sent, "dp", 2).astype(F32)
        row_mod, ada_pair = barrier((row_mod, pair_up(ada_weight[None], "dp", core, 1)))
        ada_got = swap(ada_pair, "dp", 2)
        for bit in (1, 2, 4):
            low = row_mod.astype(BF)
            row_mod = low.astype(F32) + swap(low, "blk", bit).astype(F32)
    else:
        row_mod = lax.psum_scatter(partial_mod, "dp", scatter_dimension=0, tiled=True)[0]
        row_mod = lax.psum(row_mod, "blk")
    if fast:
        core_only = core.reshape(1).astype(jnp.int32)
        first_line = gather_line(first, z)
        first_line, second_shard = barrier((first_line, second[: 4 * rows]))
        first_halves = gather_cross(first_line, x, y)
        second_pair = pair_up(second_shard, "blk", z // 2, 4)
        first_halves, second_pair = barrier((first_halves, second_pair))
        first_halves = gather_wide(*first_halves, x, y)
        second_line = pair_up(second_pair, "blk", z % 2, 2).reshape(4, 4 * rows, width)
    else:
        first_all = lax.all_gather(first, everyone, axis=0, tiled=True)
        second_all = lax.all_gather(second, everyone, axis=0, tiled=True)
        groups = first_all.reshape(count, 4, rows, width).transpose(1, 0, 2, 3)
        groups = groups.reshape(4, width, width)
        full_qkv = jnp.concatenate([groups[0], groups[1], groups[2]], axis=1)
        full_proj = groups[3]
        pair = second_all.reshape(count, 8 * rows, width)
        hid = pair[:, : 4 * rows].reshape(count, 4, rows, width).transpose(0, 2, 1, 3)
        full_hidden = hid.reshape(width, 4 * width)
        full_output = pair[:, 4 * rows :].reshape(4 * width, width)
    bias_flat = row_mod[segs:].reshape(-1)
    full_query_bias = bias_flat[:width]
    full_value_bias = bias_flat[width : 2 * width]
    full_proj_bias = bias_flat[2 * width : 3 * width]
    full_hidden_bias = bias_flat[3 * width : 7 * width]
    full_output_bias = bias_flat[7 * width : 8 * width]
    modulation = row_mod[:segs] + bias_flat[8 * width : 14 * width][None, :]
    block_pick = jnp.pad(block_pick.astype(F32), ((0, 16 - 3 * blocks), (0, 0)))
    mods = jnp.dot(block_pick, modulation, precision=HIGHEST)
    own_mods = mods[blocks : blocks + 8]

    big = jnp.broadcast_to(block_big[:, None], (3 * blocks, BLOCK)).reshape(-1) == 1
    flip = halo_flip(fast)
    kept_near, kept_far = halo(kept_patch[0], fast)
    kept_all = jnp.concatenate(
        [
            jnp.where(flip == 0, kept_far, kept_near),
            kept_patch[0],
            jnp.where(flip == 0, kept_near, kept_far),
        ]
    )
    row_pos = jnp.where(big, kept_all // BIG_SIDE, kept_all // SMALL_SIDE)
    col_pos = kept_all - row_pos * jnp.where(big, BIG_SIDE, SMALL_SIDE)
    places = jnp.concatenate(
        [col_pos[None], row_pos[None], jnp.zeros((6, 3 * tokens_dev), jnp.int32)], axis=0
    )
    own_tokens, _ = barrier((tokens[0], kept_near))
    tokens_near, tokens_far = halo(own_tokens, fast, second_pair if fast else None)
    core = core if fast else jnp.int32(0)
    core_arg = jnp.stack([core, flip]).astype(jnp.int32)
    attn_in_all, hidden, attn_in_keep, attn_in_send = attention_input(
        core_arg, (tokens_near, tokens[0], tokens_far), places, place_table(width), mods
    )

    if fast:
        attn_in_all, first_halves, second_line, third_shard, ada_got = barrier(
            (attn_in_all, first_halves, second_line, second[4 * rows :], ada_got)
        )
        first_parts = both_cores(*first_halves)
        second_halves = gather_cross(second_line, x, y)
        third_pair = pair_up(third_shard, "blk", z // 2, 4)
        first_parts, second_halves, third_pair = barrier((first_parts, second_halves, third_pair))
        second_halves = gather_wide(*second_halves, x, y)
        third_line = pair_up(third_pair, "blk", z % 2, 2).reshape(4, 4 * rows, width)
        full_qkv, full_proj = unpack_weight(
            core_only,
            first_parts,
            rows,
            [(0, 0), (0, 1), (0, 2), (1, 0)],
            "unpack_first",
        )
    queries = (dot_nn(attn_in_all, full_qkv[:, :width]) + full_query_bias).astype(BF)
    keys = dot_nn(attn_in_all, full_qkv[:, width : 2 * width]).astype(BF)
    values = (dot_nn(attn_in_all, full_qkv[:, 2 * width :]) + full_value_bias).astype(BF)
    own = slice(tokens_dev, 2 * tokens_dev)
    forward_info = jnp.concatenate(
        [block_start[blocks : 2 * blocks], block_big[blocks : 2 * blocks]]
    ).astype(jnp.int32)
    left_id, own_id, right_id = jnp.split(block_id, 3)
    backward_info = jnp.concatenate(
        [
            jnp.where(flip == 0, right_id, left_id),
            own_id,
            jnp.where(flip == 0, left_id, right_id),
            flip[None],
        ]
    ).astype(jnp.int32)
    if fast:
        queries, second_halves, third_line = barrier((queries, second_halves, third_line))
        second_parts = both_cores(*second_halves)
        third_halves = gather_cross(third_line, x, y)
    attn_low, attended, lse = attend_forward(forward_info, queries, keys, values, HEADS)

    def eight(v):
        return jnp.broadcast_to(v[None, :], (8, v.shape[0]))

    if fast:
        attn_low, second_parts, third_halves = barrier((attn_low, second_parts, third_halves))
        third_halves = gather_wide(*third_halves, x, y)
    branch, after_attn, mlp_in, mlp_keep, low_keep, mlp_low_send = after_attention(
        core_arg, attn_low, full_proj, eight(full_proj_bias), hidden, own_mods
    )
    if fast:
        (full_hidden,) = unpack_weight(
            core_only,
            second_parts,
            rows,
            [(0, 0), (0, 1), (0, 2), (0, 3)],
            "unpack_hidden",
        )
        attn_in_send, mlp_low_send = barrier((attn_in_send, mlp_low_send))
        attn_in_oth, mlp_low_oth = swap(attn_in_send, "dp", 1), swap(mlp_low_send, "dp", 1)
        mlp_in, attn_in_oth, mlp_low_oth = lax.optimization_barrier(
            (mlp_in, attn_in_oth, mlp_low_oth)
        )
    order = jnp.stack([1 - core, 3 - core, core, 2 + core]).astype(jnp.int32)
    act_keep, act_send, slope = feed_forward_up(order, mlp_in, full_hidden, eight(full_hidden_bias))
    if fast:
        act_keep, third_halves = barrier((act_keep, third_halves))
        third_parts = both_cores(*third_halves)
        act_oth = swap(act_send, "dp", 1)
        full_output = unpack_rows(core_only, third_parts, 4 * rows, "unpack_output")
    grad_lower, block_out, lower_sums = feed_forward_down(
        order,
        act_keep,
        act_send,
        full_output,
        eight(full_output_bias),
        after_attn,
        cotangent[0],
        own_mods,
    )

    shape = (tokens_dev, width)
    orders = ["yxz", "xyz"]
    if fast:
        bits = jnp.stack([x, y, z % 2, z // 2]).astype(jnp.int32)

        def step_1(halves):
            return send(halves[0], "dp", 2), send(halves[1], "blk", 1)

        def step_2(halves):
            return send(halves[0], "blk", 1), send(halves[1], "dp", 2)

        def step_3(halves):
            return send(halves, "blk", 2)

        def step_4(halves):
            return send(halves, "blk", 4)

        def half_2(got):
            return add_and_cut(bits, *got)

        def half_3(got):
            return add_and_cut_z(bits, *got)

        def half_4(got):
            return add_and_cut_last(bits, got)

        act_keep, act_oth, grad_lower_oth = barrier((act_keep, act_oth, swap(grad_lower, "dp", 1)))
        third = chip_grads(
            bits,
            [(act_keep, act_oth)],
            [(grad_lower, grad_lower_oth, 0, 0)],
            [(0, 0, 4 * rows, [(0, 2 * rows, 0, 0), (2 * rows, 2 * rows, 1, 0)])],
            orders,
            False,
            shape,
            "grad_output_weight",
        )
        grad_lower, third = barrier((grad_lower, third))
        third = step_1(third)
    grad_upper, grad_after, grad_attn, upper_sums, branch_sums = feed_forward_back(
        grad_lower,
        slope,
        full_hidden,
        full_output,
        full_proj,
        after_attn,
        branch,
        attended,
        lse,
        cotangent[0],
        own_mods,
        HEADS,
    )

    def to_segments(sums):
        return lax.dot_general(
            own_pick, sums[:blocks], (((0,), (0,)), ((), ())), precision=HIGHEST
        )

    def early_message():
        bias = jnp.concatenate(
            [
                branch_sums[blocks, :width],
                upper_sums[0],
                lower_sums[blocks],
                jnp.zeros((2 * width,), F32),
            ]
        )
        return jnp.concatenate(
            [
                to_segments(jnp.concatenate([branch_sums, lower_sums], axis=1)),
                bias.reshape(2, 4 * width),
            ],
            axis=0,
        )

    def late_message(sums):
        return jnp.concatenate([to_segments(sums), sums[blocks : blocks + 1]], axis=0)

    if not fast:
        grad_near, grad_far = halo(grad_attn, fast)
    else:

        early = early_message()
        grad_attn, grad_upper, third, early = barrier((grad_attn, grad_upper, third, early))
        grad_upper_oth = swap(grad_upper, "dp", 1)
        grad_near = swap(grad_attn, "blk", 1)
        early_got = swap_exact(early, 1, 2)
        third = half_2(third)
    grad_q, grad_k_own, grad_v_own = attend_backward_own(
        forward_info, queries, keys, values, grad_attn, HEADS
    )
    if fast:
        mlp_keep, grad_q, grad_near, grad_upper_oth, early, early_got, third = barrier(
            (mlp_keep, grad_q, grad_near, grad_upper_oth, early, early_got, third)
        )
        grad_far = lax.ppermute(grad_near, "blk", halo_hops())
        grad_q_oth = swap(grad_q, "dp", 1)
        third = step_2(third)
        early = early + early_got
        early_got = swap_exact(early, 2, 2)
        second = chip_grads(
            bits,
            [(mlp_keep, mlp_low_oth)],
            [(grad_upper, grad_upper_oth, 0, g) for g in range(4)],
            [(0, g, rows, [(0, rows, g // 2, g % 2 * rows)]) for g in range(4)],
            orders,
            True,
            shape,
            "grad_hidden_weight",
        )
        attn_in_keep, grad_q_oth, second = barrier((attn_in_keep, grad_q_oth, second))
        first = chip_grads(
            bits,
            [(attn_in_keep, attn_in_oth), (low_keep, mlp_low_oth[width // 2 :])],
            [(grad_q, grad_q_oth, 0, 0), (grad_upper, grad_upper_oth, 0, 4)],
            [(0, 0, rows, [(0, rows, 0, 0)]), (1, 1, rows, [(0, rows, 1, 0)])],
            orders,
            True,
            shape,
            "grad_query_weight",
        )

        grad_far, first, second, third, early, early_got = barrier(
            (grad_far, first, second, third, early, early_got)
        )
        second = step_1(second)
        third = step_3(half_3(third))
        early = early + early_got
        early_got = swap_exact(early, 4, 2)
    grad_kv = attend_backward_other(
        backward_info,
        queries,
        keys,
        values,
        grad_near,
        grad_far,
        grad_k_own,
        grad_v_own,
        HEADS,
    )
    if fast:
        grad_kv, hidden, first, second, third, early, early_got = barrier(
            (grad_kv, hidden, first, second, third, early, early_got)
        )
        first = step_1(first)
        second = step_2(half_2(second))
        third = step_4(half_4(third))
        early_row = early + early_got
    grad_tokens, input_sums = input_gradient(
        (grad_q, grad_kv), full_qkv, hidden, grad_after, own_mods
    )
    if fast:
        late = late_message(input_sums)
        attn_in_keep, grad_kv, first, second, third, late = barrier(
            (attn_in_keep, grad_kv, first, second, third, late)
        )
        grad_kv_oth = swap(grad_kv, "dp", 1)
        late_got = swap_exact(late, 1, 1)
        second = step_3(half_3(second))
        first = step_2(half_2(first))
        third_sum = add(*third)
        last = chip_grads(
            bits,
            [(attn_in_keep, attn_in_oth)],
            [(grad_kv, grad_kv_oth, 0, 0), (grad_kv, grad_kv_oth, 0, 1)],
            [(0, 0, rows, [(0, rows, 0, 0)]), (0, 1, rows, [(0, rows, 1, 0)])],
            orders,
            True,
            shape,
            "grad_key_weight",
        )

        last, first, second, late, late_got, early_row = barrier(
            (last, first, second, late, late_got, early_row)
        )
        last = step_1(last)
        late = late + late_got
        late_got = swap_exact(late, 2, 1)
        second = step_4(half_4(second))
        first = step_3(half_3(first))

        last, first, second, late, late_got, early_row = barrier(
            (last, first, second, late, late_got, early_row)
        )
        late = late + late_got
        late_got = swap_exact(late, 4, 1)
        last = step_2(half_2(last))
        first = step_4(half_4(first))
        early_pair = pair_up(early_row[None], "dp", core, 1)
        second_sum = add(*second)

        last, first, late, late_got, early_pair = barrier((last, first, late, late_got, early_pair))
        late_row = late + late_got
        ada_rows = jnp.concatenate(
            [jnp.where(y == 0, ada_pair, ada_got), jnp.where(y == 0, ada_got, ada_pair)], axis=0
        ).reshape(4 * rows, 6 * width)
        own_row = jnp.concatenate([late_row[:segs], early_row[:segs]], axis=1)
        row_high = lax.reduce_precision(own_row, 8, 7)
        row_rest = (own_row - row_high).astype(BF)
        part = dot_nt(ada_rows, row_high.astype(BF)) + dot_nt(ada_rows, row_rest)
        parts = [part] + [swap(part, "blk", bit) for bit in (2, 4, 6)]
        last = step_3(half_3(last))
        late_pair = pair_up(late_row[None], "dp", core, 1)
        first_sum = add(*first)

        last, parts, late_pair, early_pair = barrier((last, parts, late_pair, early_pair))
        low = [jnp.where(z % 2 == 0, a, b) for a, b in ((parts[0], parts[1]), (parts[2], parts[3]))]
        high = [jnp.where(z % 2 == 0, b, a) for a, b in ((parts[0], parts[1]), (parts[2], parts[3]))]
        line = jnp.stack(
            [
                jnp.where(z // 2 == 0, low[0], low[1]),
                jnp.where(z // 2 == 0, high[0], high[1]),
                jnp.where(z // 2 == 0, low[1], low[0]),
                jnp.where(z // 2 == 0, high[1], high[0]),
            ]
        )
        part = pair_up(line[None], "blk", x, 1)
        last = step_4(half_4(last))
        late_all = pair_up(late_pair, "dp", y, 2)
        early_all = pair_up(early_pair, "dp", y, 2)
        last_sum = add(*last)

    if not fast:
        early_row, late_row = (
            lax.psum(v, "blk") for v in (early_message(), late_message(input_sums))
        )
        early_all, late_all = (
            lax.all_gather(v, "dp", axis=0, tiled=False) for v in (early_row, late_row)
        )
    mod_all = jnp.concatenate([late_all[:, :segs], early_all[:, :segs]], axis=2)
    mod_all = mod_all.reshape(-1, 6 * width)
    early_bias = jnp.sum(early_all[:, segs:], axis=0).reshape(-1)
    late_bias = jnp.sum(late_all[:, segs:], axis=0).reshape(-1)

    def take(v, n):
        return lax.dynamic_slice_in_dim(v, own_dev * n, n)

    grad_query_bias = take(late_bias[:width], rows)
    grad_value_bias = take(late_bias[width:], rows)
    grad_proj_bias = take(early_bias[:width], rows)
    grad_hidden_bias = take(early_bias[width : 5 * width], 4 * rows)
    grad_output_bias = take(early_bias[5 * width : 6 * width], rows)
    grad_ada_bias = take(jnp.sum(mod_all, axis=0), 6 * rows)
    mod_high = mod_all.astype(BF)
    mod_rest = (mod_all - mod_high.astype(F32)).astype(BF)
    grad_ada_weight = dot_nn(silu_own, mod_high) + dot_nn(silu_own, mod_rest)
    if fast:
        part = part.reshape(2, 4, 4, rows, segs).transpose(4, 2, 1, 0, 3)
        own_silu = part.reshape(segs, width)
    else:
        silu_grad = dot_nt(ada_weight, mod_high) + dot_nt(ada_weight, mod_rest)
        silu_rows = lax.all_gather(silu_grad, everyone, axis=0, tiled=True)
        own_silu = lax.dynamic_slice_in_dim(silu_rows, own_dp * segs, segs, axis=1).T
    grad_seg_cond = silu_pull(own_silu)[0]
    grad_image = lax.dot_general(
        pick_image.astype(F32), grad_seg_cond, (((0,), (0,)), ((), ())), precision=HIGHEST
    )

    if fast:
        grad_qkv_weight = jnp.concatenate(
            [first_sum[:rows], last_sum[:rows], last_sum[rows:]], axis=1
        )
        grad_proj_weight = first_sum[rows:]
        grad_hidden_weight = jnp.concatenate(
            [second_sum[g * rows : (g + 1) * rows] for g in range(4)], axis=1
        )
        grad_output_weight = third_sum
    else:

        def scattered(left_t, right):
            product = dot_nn(left_t, right).astype(BF)
            product = lax.psum_scatter(product, "dp", scatter_dimension=0, tiled=True)
            return lax.psum_scatter(product, "blk", scatter_dimension=0, tiled=True).astype(F32)

        def in_order(keep, send):
            both = jnp.stack([keep.reshape(2, -1, tokens_dev), send.reshape(2, -1, tokens_dev)], axis=1)
            return both.reshape(-1, tokens_dev)

        attn_in_t = in_order(attn_in_keep, attn_in_send)
        mlp_send, low_send = mlp_low_send[: width // 2], mlp_low_send[width // 2 :]
        grad_qkv_weight = scattered(attn_in_t, jnp.concatenate([grad_q, grad_kv], axis=1))
        grad_proj_weight = scattered(in_order(low_keep, low_send), grad_upper[:, 4 * width :])
        grad_hidden_weight = scattered(in_order(mlp_keep, mlp_send), grad_upper[:, : 4 * width])
        act = jnp.stack(
            [act_keep.reshape(2, tokens_dev, width), act_send.reshape(2, tokens_dev, width)], axis=1
        ).reshape(4, tokens_dev, width)
        act_t = act.transpose(0, 2, 1).reshape(4 * width, tokens_dev)
        grad_output_weight = scattered(act_t, grad_lower)
    return (
        block_out[None],
        grad_tokens[None],
        grad_image[None],
        grad_ada_weight,
        grad_ada_bias,
        grad_qkv_weight,
        grad_query_bias,
        grad_value_bias,
        grad_proj_weight,
        grad_proj_bias,
        grad_hidden_weight,
        grad_hidden_bias,
        grad_output_weight,
        grad_output_bias,
    )


def solution(mesh):
    row = P("dp", "blk", None)
    ints = P("dp", "blk")
    image = P("dp", None)
    matrix = P(("dp", "blk"), None)
    vector = P(("dp", "blk"))
    return jax.shard_map(
        per_device,
        mesh=mesh,
        in_specs=(
            row,
            P("dp", None, None),
            row,
            ints,
            ints,
            image,
            image,
            matrix,
            vector,
            matrix,
            vector,
            vector,
            matrix,
            vector,
            matrix,
            vector,
            matrix,
            vector,
        ),
        out_specs=(
            row,
            row,
            P("dp", None, None),
            matrix,
            vector,
            matrix,
            vector,
            vector,
            matrix,
            vector,
            matrix,
            vector,
            matrix,
            vector,
        ),
        check_vma=False,
    )
```

```python
import jax
import jax.numpy as jnp
from jax import lax
from jax.experimental import pallas as pl
from jax.experimental.pallas import tpu as pltpu
from jax.sharding import PartitionSpec as P

HEADS = 16
BIG_SIDE = 32
SMALL_SIDE = 16
BIG_LEN = 512
SMALL_LEN = 128
BLOCK = 128

BF = jnp.bfloat16
F32 = jnp.float32
HIGHEST = lax.Precision.HIGHEST
VMEM_LIMIT = 60 * 1024 * 1024


def cost(us):
    return pl.CostEstimate(flops=int(us * 1.1e9), transcendentals=0, bytes_accessed=1024)


def dot_nn(a, b):
    return lax.dot_general(a, b, (((1,), (0,)), ((), ())), preferred_element_type=F32)


def dot_nt(a, b):
    return lax.dot_general(a, b, (((1,), (1,)), ((), ())), preferred_element_type=F32)


def dot_tn(a, b):
    return lax.dot_general(a, b, (((0,), (0,)), ((), ())), preferred_element_type=F32)


def swap(v, axis, bit):
    count = lax.axis_size(axis)
    return lax.ppermute(v, axis, [(i, i ^ bit) for i in range(count)])


def swap_exact(v, bit, exact):
    at = v.shape[0] - exact
    high = lax.reduce_precision(v, 8, 7)
    rest = lax.reduce_precision(v[at:] - high[at:], 8, 7)
    got = swap(jnp.concatenate([high, rest], axis=0).astype(BF), "blk", bit).astype(F32)
    return jnp.concatenate([got[:at], got[at : v.shape[0]] + got[v.shape[0] :]], axis=0)


def dp_gather(v):
    core, y = lax.axis_index("dp") % 2, lax.axis_index("dp") // 2
    other = swap(v, "dp", 1)
    pair = jnp.stack([jnp.where(core == 0, v, other), jnp.where(core == 0, other, v)])
    across = swap(pair, "dp", 2)
    return jnp.concatenate([jnp.where(y == 0, pair, across), jnp.where(y == 0, across, pair)])


def pair_up(v, axis, bit_value, bit):
    got = swap(v, axis, bit)
    return jnp.concatenate(
        [jnp.where(bit_value == 0, v, got), jnp.where(bit_value == 0, got, v)], axis=0
    )


def gather_line(shard, z):
    line = pair_up(pair_up(shard, "blk", z // 2, 4), "blk", z % 2, 2)
    return line.reshape(4, *shard.shape)


def gather_cross(line, x, y):
    _, n, width = line.shape
    first = line[:, : n // 2].reshape(-1, width)
    last = line[:, n // 2 :].reshape(-1, width)
    return pair_up(first, "blk", x, 1), pair_up(last, "dp", y, 2)


def gather_wide(first, last, x, y):
    return pair_up(first, "dp", y, 2), pair_up(last, "blk", x, 1)


def both_cores(first, last):
    return first, last, swap(first, "dp", 1), swap(last, "dp", 1)


def unpack_weight(core, parts, rows, groups, name):
    width = parts[0].shape[1]
    half = len(groups) // 2
    n_out = max(o for o, _ in groups) + 1
    widths = [(max(c for o, c in groups if o == k) + 1) * width for k in range(n_out)]

    def body(core_ref, a_own, b_own, a_oth, b_oth, *outs):
        dp = pl.program_id(0)
        for a_ref, b_ref, own in ((a_own, b_own, True), (a_oth, b_oth, False)):

            @pl.when((dp % 2 == core_ref[0]) == own)
            def _(a_ref=a_ref, b_ref=b_ref):
                for z in range(4):
                    for x in range(2):
                        at = (z * 2 + x) * rows
                        for g, (o, c) in enumerate(groups):
                            ref = a_ref if g < half else b_ref
                            start = ((x * 4 + z_place(z)) * half + g % half) * rows
                            columns = slice(c * width, (c + 1) * width)
                            if g < half:
                                outs[o][at : at + rows, columns] = ref[start : start + rows, :]
                            else:
                                outs[o][at : at + rows, columns] = ref[x, 0][
                                    (z_place(z) * half + g % half)
                                    * rows : (z_place(z) * half + g % half + 1)
                                    * rows,
                                    :,
                                ]

    chunk = 8 * half * rows
    by_y = pl.BlockSpec((chunk, width), lambda i, c: (i // 2, 0))
    by_x = pl.BlockSpec((2, 1, chunk // 2, width), lambda i, c: (0, i // 2, 0, 0))
    turned = [p.reshape(2, 2, chunk // 2, width) for p in (parts[1], parts[3])]
    return pl.pallas_call(
        body,
        grid_spec=pltpu.PrefetchScalarGridSpec(
            num_scalar_prefetch=1,
            grid=(4,),
            in_specs=[by_y, by_x, by_y, by_x],
            out_specs=[pl.BlockSpec((8 * rows, w), lambda i, c: (i, 0)) for w in widths],
        ),
        out_shape=[jax.ShapeDtypeStruct((32 * rows, w), BF) for w in widths],
        compiler_params=pltpu.CompilerParams(vmem_limit_bytes=VMEM_LIMIT),
        cost_estimate=cost(10),
        name=name,
    )(core, parts[0], turned[0], parts[2], turned[1])


def z_place(z):
    return z % 2 * 2 + z // 2


def chip_grads(bits, lefts, rights, products, orders, turned, shape, name):
    tokens, width = shape
    parts = [own.shape[0] // 2 if turned else own.shape[1] for own, _ in lefts]
    height = [
        sum(n for _, _, _, pieces in products for _, n, out, _ in pieces if out == o)
        for o in range(len(orders))
    ]
    n_left, n_right = len(lefts), len(rights)
    product_of = dot_nn if turned else dot_tn

    def body(bits_ref, *refs):
        lefts_own, lefts_oth = refs[:n_left], refs[n_left : 2 * n_left]
        rights_own = refs[2 * n_left : 2 * n_left + n_right]
        rights_oth = refs[2 * n_left + n_right : 2 * n_left + 2 * n_right]
        outs, acc = refs[2 * n_left + 2 * n_right : -1], refs[-1]
        keep = pl.program_id(0)
        y = jnp.where(keep == 1, bits_ref[1], 1 - bits_ref[1])
        for li, ri, chunk, pieces in products:
            acc[: 8 * chunk, :] = product_of(
                lefts_own[li][...], rights_own[ri][...]
            ) + product_of(lefts_oth[li][...], rights_oth[ri][...])
            for j in range(8):
                z, x = j // 2, j % 2
                for start, n, out, at in pieces:
                    value = acc[j * chunk + start : j * chunk + start + n, :].astype(BF)
                    if orders[out] == "yxz":
                        row = (x * 4 + z_place(z)) * height[out] + at
                        chosen = keep
                    else:
                        row = z_place(z) * height[out] + at
                        chosen = jnp.where(bits_ref[0] == x, 1, 0)
                    for k in range(2):

                        @pl.when(chosen == k)
                        def _(row=row, value=value, out=out, n=n, k=k):
                            ref = outs[2 * out + k]
                            if orders[out] == "yxz":
                                ref[row : row + n, :] = value
                            else:
                                ref[y, row : row + n, :] = value

    left_specs = [
        pl.BlockSpec(
            (p, tokens) if turned else (tokens, p), lambda i, b: (jnp.where(i == 1, b[1], 1 - b[1]), 0)
        )
        for p in parts
    ]
    right_specs = [
        pl.BlockSpec((tokens, width), lambda i, b, r=r, k=k: (r, k)) for _, _, r, k in rights
    ]
    out_specs, out_shape = [], []
    for order, h in zip(orders, height):
        half = (8 * h, width) if order == "yxz" else (2, 4 * h, width)
        out_specs += [whole(half)] * 2
        out_shape += [jax.ShapeDtypeStruct(half, BF)] * 2
    total = sum(16 * h for h in height)
    results = pl.pallas_call(
        body,
        grid_spec=pltpu.PrefetchScalarGridSpec(
            num_scalar_prefetch=1,
            grid=(2,),
            in_specs=left_specs * 2 + right_specs * 2,
            out_specs=out_specs,
            scratch_shapes=[pltpu.VMEM((max(parts), width), F32)],
        ),
        out_shape=out_shape,
        compiler_params=pltpu.CompilerParams(vmem_limit_bytes=VMEM_LIMIT),
        cost_estimate=cost(10),
        name=name,
    )(
        bits,
        *[own for own, _ in lefts],
        *[oth for _, oth in lefts],
        *[r[0] for r in rights],
        *[r[1] for r in rights],
    )
    return [
        tuple(v.reshape(-1, width) for v in results[2 * k : 2 * k + 2]) for k in range(len(orders))
    ]


def split_by(v, bit):
    both = v.reshape(2, v.shape[0] // 2, v.shape[1])
    return (
        lax.dynamic_index_in_dim(both, 1 - bit, 0, keepdims=False),
        lax.dynamic_index_in_dim(both, bit, 0, keepdims=False),
    )


def add(a, b):
    return a.astype(F32) + b.astype(F32)


def send(halves, axis, bit):
    sent, kept = halves
    return kept, swap(sent, axis, bit)


def run_together(bits, *tasks):
    width = tasks[0][1][0].shape[1]
    operands = [v for task in tasks for v in task[1]]
    rows_out = [n for task in tasks for n in task[2]]

    def body(bits_ref, *refs):
        ins, outs = refs[: len(operands)], refs[len(operands) :]
        for task in tasks:
            n_in, n_out = len(task[1]), len(task[2])
            task[0](bits_ref, *ins[:n_in], *outs[:n_out])
            ins, outs = ins[n_in:], outs[n_out:]

    results = pl.pallas_call(
        body,
        grid_spec=pltpu.PrefetchScalarGridSpec(
            num_scalar_prefetch=1,
            grid=(1,),
            in_specs=[whole(v.shape) for v in operands],
            out_specs=[whole((n, width)) for n in rows_out],
        ),
        out_shape=[jax.ShapeDtypeStruct((n, width), BF) for n in rows_out],
        compiler_params=pltpu.CompilerParams(vmem_limit_bytes=VMEM_LIMIT),
        cost_estimate=cost(2),
        name="add_and_cut",
    )(bits, *operands)
    found = []
    for task in tasks:
        found.append(task[3](results[: len(task[2])]))
        results = results[len(task[2]) :]
    return found


def add_and_cut(a, b):
    n = a[0].shape[0] // 2

    def body(bits_ref, a_own, a_got, b_own, b_got, a_sent, a_kept, b_sent, b_kept):
        for own, got, sent, kept, bit in (
            (a_own, a_got, a_sent, a_kept, bits_ref[0]),
            (b_own, b_got, b_sent, b_kept, bits_ref[1]),
        ):
            there = pl.ds(pl.multiple_of((1 - bit) * n, 16), n)
            here = pl.ds(pl.multiple_of(bit * n, 16), n)
            sent[...] = add(own[there, :], got[there, :]).astype(BF)
            kept[...] = add(own[here, :], got[here, :]).astype(BF)

    return body, [*a, *b], [n] * 4, lambda r: ((r[0], r[1]), (r[2], r[3]))


def add_and_cut_z(a, b):
    h = a[0].shape[0] // 4

    def body(bits_ref, a_own, a_got, b_own, b_got, sent, kept):
        for even in range(2):

            @pl.when(bits_ref[2] == even)
            def _():
                for ref, low in ((sent, 1 - even), (kept, even)):
                    for k in range(2):
                        rows = slice((low * 2 + k) * h, (low * 2 + k + 1) * h)
                        ref[k * 2 * h : k * 2 * h + h, :] = add(
                            a_own[rows, :], a_got[rows, :]
                        ).astype(BF)
                        ref[k * 2 * h + h : (k + 1) * 2 * h, :] = add(
                            b_own[rows, :], b_got[rows, :]
                        ).astype(BF)

    return body, [*a, *b], [4 * h] * 2, tuple


def add_and_cut_last(got):
    n = got[0].shape[0] // 2

    def body(bits_ref, own, other, sent, kept):
        for high in range(2):

            @pl.when(bits_ref[3] == high)
            def _():
                there, here = slice((1 - high) * n, (2 - high) * n), slice(high * n, (high + 1) * n)
                sent[...] = add(own[there, :], other[there, :]).astype(BF)
                kept[...] = add(own[here, :], other[here, :]).astype(BF)

    return body, [*got], [n] * 2, tuple


def head_window(h, size):
    first = h * size // 128
    last = ((h + 1) * size - 1) // 128
    return first * 128, (last + 1) * 128, h * size - first * 128


def lane_mask(shape, start, size):
    lane = lax.broadcasted_iota(jnp.int32, shape, 1)
    return (lane >= start) & (lane < start + size)


def attend_forward(info, queries, keys, values, heads):
    tokens, width = queries.shape[0] // 3, queries.shape[1]
    size = width // heads
    scale = size**-0.5
    blocks = tokens // BLOCK

    def body(info_ref, q_ref, k_ref, v_ref, o_ref, full_ref, lse_ref):
        def one_block(i, carry):
            row = pl.multiple_of(i * BLOCK, BLOCK)
            start = pl.multiple_of(info_ref[i], BLOCK)

            def run(length):
                lse_all = jnp.zeros((BLOCK, 128), F32)
                for h in range(heads):
                    lo, hi, off = head_window(h, size)
                    q = q_ref[pl.ds(row, BLOCK), lo:hi]
                    mask = lane_mask(q.shape, off, size)
                    q = jnp.where(mask, q, jnp.zeros_like(q))
                    k = k_ref[pl.ds(start, length), lo:hi]
                    v = v_ref[pl.ds(start, length), lo:hi]
                    s = dot_nt(q, k) * scale
                    peak = jnp.max(s, axis=1, keepdims=True)
                    p = jnp.exp(s - peak)
                    total = jnp.sum(p, axis=1, keepdims=True)
                    o = dot_nn(p.astype(BF), v) * (1.0 / total)
                    if off == 0:
                        full_ref[pl.ds(row, BLOCK), lo:hi] = o
                    else:
                        full_ref[pl.ds(row, BLOCK), lo:hi] = jnp.where(
                            mask, o, full_ref[pl.ds(row, BLOCK), lo:hi]
                        )
                    lse_all = jnp.where(
                        lane_mask(lse_all.shape, h, 1), peak + jnp.log(total), lse_all
                    )
                lse_ref[pl.ds(row, BLOCK), :] = lse_all

            @pl.when(info_ref[blocks + i] == 1)
            def _():
                run(BIG_LEN)

            @pl.when(info_ref[blocks + i] == 0)
            def _():
                run(SMALL_LEN)

            return carry

        lax.fori_loop(0, blocks, one_block, 0)
        o_ref[...] = full_ref[...].astype(BF)

    return pl.pallas_call(
        body,
        grid_spec=pltpu.PrefetchScalarGridSpec(
            num_scalar_prefetch=1,
            grid=(1,),
            in_specs=[
                pl.BlockSpec((tokens, width), lambda i, s: (1, 0)),
                pl.BlockSpec((3 * tokens, width), lambda i, s: (0, 0)),
                pl.BlockSpec((3 * tokens, width), lambda i, s: (0, 0)),
            ],
            out_specs=[
                pl.BlockSpec((tokens, width), lambda i, s: (0, 0)),
                pl.BlockSpec((tokens, width), lambda i, s: (0, 0)),
                pl.BlockSpec((tokens, 128), lambda i, s: (0, 0)),
            ],
        ),
        out_shape=[
            jax.ShapeDtypeStruct((tokens, width), BF),
            jax.ShapeDtypeStruct((tokens, width), F32),
            jax.ShapeDtypeStruct((tokens, 128), F32),
        ],
        compiler_params=pltpu.CompilerParams(vmem_limit_bytes=VMEM_LIMIT),
        cost_estimate=cost(15),
        name="attend_forward",
    )(info, queries, keys, values)


def backward_pairs(q_ref, g_ref, k_ref, v_ref, dk, dv, heads, size):
    scale = size**-0.5
    width = heads * size

    def pairs(row, start, length, at, dq, dq_at):
        terms = g_ref[pl.ds(row, BLOCK), width : width + 128].astype(F32).T
        stats = terms[: 2 * heads] + terms[2 * heads : 4 * heads] + terms[4 * heads : 6 * heads]
        for h in range(heads):
            lo, hi, off = head_window(h, size)
            q = q_ref[pl.ds(row, BLOCK), lo:hi]
            mask = lane_mask(q.shape, off, size)
            q = jnp.where(mask, q, jnp.zeros_like(q))
            g = g_ref[pl.ds(row, BLOCK), lo:hi]
            g = jnp.where(mask, g, jnp.zeros_like(g))
            k = k_ref[pl.ds(start, length), lo:hi]
            v = v_ref[pl.ds(start, length), lo:hi]
            p = jnp.exp(dot_nt(k, q) * scale - stats[h : h + 1, :])
            ds = (p * (dot_nt(v, g) - stats[heads + h : heads + h + 1, :])).astype(BF)
            dv[pl.ds(at, length), lo:hi] += dot_nn(p.astype(BF), g)
            dk[pl.ds(at, length), lo:hi] += dot_nn(ds, q)
            if dq is not None:
                part = dot_tn(ds, k)
                dq[pl.ds(dq_at, BLOCK), lo:hi] += jnp.where(mask, part, jnp.zeros_like(part))

    return pairs


def attend_backward_own(info, queries, keys, values, grads, heads):
    tokens, width = grads.shape[0], queries.shape[1]
    size = width // heads
    scale = size**-0.5
    blocks = tokens // BLOCK

    def body(info_ref, q_ref, k_ref, v_ref, g_ref, dq_ref, dk_ref, dv_ref, dq, dk, dv):
        dq[...] = jnp.zeros_like(dq)
        dk[...] = jnp.zeros_like(dk)
        dv[...] = jnp.zeros_like(dv)
        pairs = backward_pairs(q_ref, g_ref, k_ref, v_ref, dk, dv, heads, size)

        def own_block(i, carry):
            row = pl.multiple_of(i * BLOCK, BLOCK)
            start = pl.multiple_of(info_ref[i], BLOCK)

            @pl.when(info_ref[blocks + i] == 1)
            def _():
                pairs(row, start, BIG_LEN, start, dq, row)

            @pl.when(info_ref[blocks + i] == 0)
            def _():
                pairs(row, start, SMALL_LEN, start, dq, row)

            return carry

        lax.fori_loop(0, blocks, own_block, 0)
        dq_ref[...] = (dq[...] * scale).astype(BF)
        dk_ref[...] = dk[tokens : 2 * tokens, :]
        dv_ref[...] = dv[tokens : 2 * tokens, :]

    full = pl.BlockSpec((3 * tokens, width), lambda i, s: (0, 0))
    own = pl.BlockSpec((tokens, width), lambda i, s: (0, 0))
    return pl.pallas_call(
        body,
        grid_spec=pltpu.PrefetchScalarGridSpec(
            num_scalar_prefetch=1,
            grid=(1,),
            in_specs=[pl.BlockSpec((tokens, width), lambda i, s: (1, 0)), full, full, pl.BlockSpec((tokens, width + 128), lambda i, s: (0, 0))],
            out_specs=[own] * 3,
            scratch_shapes=[
                pltpu.VMEM((tokens, width), F32),
                pltpu.VMEM((3 * tokens, width), F32),
                pltpu.VMEM((3 * tokens, width), F32),
            ],
        ),
        out_shape=[
            jax.ShapeDtypeStruct((tokens, width), BF),
            jax.ShapeDtypeStruct((tokens, width), F32),
            jax.ShapeDtypeStruct((tokens, width), F32),
        ],
        compiler_params=pltpu.CompilerParams(vmem_limit_bytes=VMEM_LIMIT),
        cost_estimate=cost(24),
        name="attend_backward_own",
    )(info, queries, keys, values, grads)


def attend_backward_other(info, queries, keys, values, g_near, g_far, dk_own, dv_own, heads):
    tokens, width = g_near.shape[0], queries.shape[1]
    size = width // heads
    scale = size**-0.5
    blocks = tokens // BLOCK

    def body(
        info_ref, q_near, q_far, k_ref, v_ref, gn, gf, dk_in, dv_in, out_ref, dk, dv
    ):
        dk[...] = dk_in[...]
        dv[...] = dv_in[...]
        for side, (q_ref, g_ref) in enumerate(((q_near, gn), (q_far, gf))):
            pairs = backward_pairs(q_ref, g_ref, k_ref, v_ref, dk, dv, heads, size)

            def one(t, carry, pairs=pairs, side=side):
                a, own = t // blocks, t % blocks

                @pl.when(info_ref[a + 2 * blocks * side] == info_ref[blocks + own])
                def _():
                    at = pl.multiple_of(own * BLOCK, BLOCK)
                    pairs(pl.multiple_of(a * BLOCK, BLOCK), at, BLOCK, at, None, 0)

                return carry

            lax.fori_loop(0, blocks * blocks, one, 0)
        out_ref[:, :width] = (dk[...] * scale).astype(BF)
        out_ref[:, width:] = dv[...].astype(BF)

    own = pl.BlockSpec((tokens, width), lambda i, s: (0, 0))
    near = pl.BlockSpec((tokens, width), lambda i, s: (2 - 2 * s[3 * blocks], 0))
    far = pl.BlockSpec((tokens, width), lambda i, s: (2 * s[3 * blocks], 0))
    middle = pl.BlockSpec((tokens, width), lambda i, s: (1, 0))
    wide = pl.BlockSpec((tokens, width + 128), lambda i, s: (0, 0))
    return pl.pallas_call(
        body,
        grid_spec=pltpu.PrefetchScalarGridSpec(
            num_scalar_prefetch=1,
            grid=(1,),
            in_specs=[near, far, middle, middle, wide, wide, own, own],
            out_specs=pl.BlockSpec((tokens, 2 * width), lambda i, s: (0, 0)),
            scratch_shapes=[pltpu.VMEM((tokens, width), F32), pltpu.VMEM((tokens, width), F32)],
        ),
        out_shape=jax.ShapeDtypeStruct((tokens, 2 * width), BF),
        compiler_params=pltpu.CompilerParams(vmem_limit_bytes=VMEM_LIMIT),
        cost_estimate=cost(22),
        name="attend_backward_other",
    )(info, queries, queries, keys, values, g_near, g_far, dk_own, dv_own)


def layer_norm(v):
    centered = v - jnp.mean(v, axis=1, keepdims=True)
    spread = jnp.mean(centered * centered, axis=1, keepdims=True)
    inverse = lax.rsqrt(spread + 1e-06)
    return centered * inverse, inverse


def norm_back(grad_in, normed, inverse):
    mean_grad = jnp.mean(grad_in, axis=1, keepdims=True)
    mean_proj = jnp.mean(grad_in * normed, axis=1, keepdims=True)
    return inverse * (grad_in - mean_grad - normed * mean_proj)


def column_sum(v):
    return jnp.sum(v.astype(F32), axis=0, keepdims=True)


def whole(shape, dtype=None):
    return pl.BlockSpec(shape, lambda *_: (0,) * len(shape))


def store_turned(core, value, keep_ref, send_ref):
    turned = value.astype(F32).T.astype(BF)
    part = turned.shape[0] // 4
    for c in range(2):

        @pl.when(core == c)
        def _():
            for y in range(2):
                keep_ref[y * part : (y + 1) * part, :] = turned[
                    (2 * y + c) * part : (2 * y + c + 1) * part, :
                ]
                send_ref[y * part : (y + 1) * part, :] = turned[
                    (2 * y + 1 - c) * part : (2 * y + 2 - c) * part, :
                ]


def attention_input(core, parts, places, table, mods):
    tokens, width = parts[0].shape
    blocks = tokens // BLOCK

    def body(core_ref, near, own, far, place_ref, table_ref, mod_ref, in_ref, hid_ref, keep, send):
        steps = lax.broadcasted_iota(jnp.int32, (BIG_SIDE, BLOCK), 0)
        flip = core_ref[1]
        bases = (2 * blocks * (1 - flip), blocks, 2 * blocks * flip)
        for source, base in zip((near, own, far), bases):
            for i in range(blocks):
                b = base + i
                at = pl.ds(pl.multiple_of(b * BLOCK, BLOCK), BLOCK)
                place = jnp.concatenate(
                    [
                        lax.dot_general(
                            (steps == place_ref[r : r + 1, at]).astype(F32),
                            table_ref[...],
                            (((0,), (0,)), ((), ())),
                            precision=HIGHEST,
                            preferred_element_type=F32,
                        )
                        for r in range(2)
                    ],
                    axis=1,
                )
                hidden = source[i * BLOCK : (i + 1) * BLOCK, :].astype(F32) + place
                normed, _ = layer_norm(hidden)
                value = (
                    normed * (1.0 + mod_ref[pl.ds(b, 1), width : 2 * width])
                    + mod_ref[pl.ds(b, 1), :width]
                )
                in_ref[at, :] = value.astype(BF)
                if source is own:
                    hid_ref[i * BLOCK : (i + 1) * BLOCK, :] = hidden
        store_turned(core_ref[0], in_ref[tokens : 2 * tokens, :], keep, send)

    half = jax.ShapeDtypeStruct((width // 2, tokens), BF)
    return pl.pallas_call(
        body,
        grid_spec=pltpu.PrefetchScalarGridSpec(
            num_scalar_prefetch=1,
            grid=(1,),
            in_specs=[whole((tokens, width))] * 3
            + [whole(places.shape), whole(table.shape), whole(mods.shape)],
            out_specs=[
                whole((3 * tokens, width)),
                whole((tokens, width)),
                whole(half.shape),
                whole(half.shape),
            ],
        ),
        out_shape=[
            jax.ShapeDtypeStruct((3 * tokens, width), BF),
            jax.ShapeDtypeStruct((tokens, width), F32),
            half,
            half,
        ],
        compiler_params=pltpu.CompilerParams(vmem_limit_bytes=VMEM_LIMIT),
        cost_estimate=cost(10),
        name="attention_input",
    )(core, *parts, places, table, mods)


def after_attention(core, attn_low, proj, proj_bias, hidden, mods):
    tokens, width = hidden.shape
    blocks = tokens // BLOCK

    def body(
        core_ref, low, w_ref, b_ref, hid, mod, branch, after, mlp_in, keep_m, keep_a, send
    ):
        for b in range(blocks):
            rows = slice(b * BLOCK, (b + 1) * BLOCK)
            value = dot_nn(low[rows, :], w_ref[...]) + b_ref[0:1, :]
            branch[rows, :] = value
            done = hid[rows, :] + mod[b : b + 1, 2 * width : 3 * width] * value
            after[rows, :] = done
            normed, _ = layer_norm(done)
            mlp_in[rows, :] = (
                normed * (1.0 + mod[b : b + 1, 4 * width : 5 * width])
                + mod[b : b + 1, 3 * width : 4 * width]
            ).astype(BF)
        store_turned(core_ref[0], mlp_in[...], keep_m, send.at[: width // 2, :])
        store_turned(core_ref[0], low[...], keep_a, send.at[width // 2 :, :])

    half = jax.ShapeDtypeStruct((width // 2, tokens), BF)
    full = jax.ShapeDtypeStruct((tokens, width), F32)
    return pl.pallas_call(
        body,
        grid_spec=pltpu.PrefetchScalarGridSpec(
            num_scalar_prefetch=1,
            grid=(1,),
            in_specs=[
                whole((tokens, width)),
                whole((width, width)),
                whole((8, width)),
                whole((tokens, width)),
                whole(mods.shape),
            ],
            out_specs=[whole((tokens, width))] * 3 + [whole(half.shape)] * 2 + [whole((width, tokens))],
        ),
        out_shape=[full, full, jax.ShapeDtypeStruct((tokens, width), BF)] + [half] * 2
        + [jax.ShapeDtypeStruct((width, tokens), BF)],
        compiler_params=pltpu.CompilerParams(vmem_limit_bytes=VMEM_LIMIT),
        cost_estimate=cost(8),
        name="after_attention",
    )(core, attn_low, proj, proj_bias, hidden, mods)


def feed_forward_up(order, mlp_in, hidden_w, hidden_b):
    tokens, width = mlp_in.shape

    def body(order_ref, x, wh, bh, keep, send, slope):
        t = pl.program_id(0)
        up = dot_nn(x[...], wh[...]) + bh[0:1, :]
        square = up * up
        wave = jnp.tanh(0.7978845608028654 * up * (1.0 + 0.044715 * square))
        act = (0.5 * up * (1.0 + wave)).astype(BF)
        slope[...] = (
            0.5 * (1.0 + wave)
            + 0.5 * up * (1.0 - wave * wave) * 0.7978845608028654 * (1.0 + 0.134145 * square)
        ).astype(BF)

        @pl.when(t < 2)
        def _():
            send[...] = act

        @pl.when(t >= 2)
        def _():
            keep[...] = act

    return pl.pallas_call(
        body,
        grid_spec=pltpu.PrefetchScalarGridSpec(
            num_scalar_prefetch=1,
            grid=(4,),
            in_specs=[
                whole((tokens, width)),
                pl.BlockSpec((width, width), lambda t, o: (0, o[t])),
                pl.BlockSpec((8, width), lambda t, o: (0, o[t])),
            ],
            out_specs=[
                pl.BlockSpec((tokens, width), lambda t, o: (jnp.maximum(t - 2, 0), 0)),
                pl.BlockSpec((tokens, width), lambda t, o: (jnp.minimum(t, 1), 0)),
                pl.BlockSpec((tokens, width), lambda t, o: (0, o[t])),
            ],
        ),
        out_shape=[
            jax.ShapeDtypeStruct((2 * tokens, width), BF),
            jax.ShapeDtypeStruct((2 * tokens, width), BF),
            jax.ShapeDtypeStruct((tokens, 4 * width), BF),
        ],
        compiler_params=pltpu.CompilerParams(vmem_limit_bytes=VMEM_LIMIT),
        cost_estimate=cost(14),
        name="feed_forward_up",
    )(order, mlp_in, hidden_w, hidden_b)


def feed_forward_down(order, keep, send, output_w, output_b, after, cotangent, mods, core=None):
    tokens, width = after.shape
    blocks = tokens // BLOCK
    parts = core is not None

    def body(order_ref, keep_ref, send_ref, *refs):
        t = pl.program_id(0)
        if parts:
            a_own, b_own, a_oth, b_oth, bo, after_ref, cot, mod, low, out, sums, wo, acc = refs
            half = a_own.shape[0] // 8
            for a_ref, b_ref, own in ((a_own, b_own, True), (a_oth, b_oth, False)):

                @pl.when((order_ref[t] % 2 == order_ref[4]) == own)
                def _(a_ref=a_ref, b_ref=b_ref):
                    for z in range(4):
                        for x in range(2):
                            at = (z * 2 + x) * 2 * half
                            start = (x * 4 + z_place(z)) * half
                            wo[at : at + half, :] = a_ref[start : start + half, :]
                            start = z_place(z) * half
                            wo[at + half : at + 2 * half, :] = b_ref[x, 0][start : start + half, :]

        else:
            wo, bo, after_ref, cot, mod, low, out, sums, acc = refs

        @pl.when(t == 0)
        def _():
            acc[...] = dot_nn(send_ref[...], wo[...])

        @pl.when(t == 1)
        def _():
            acc[...] += dot_nn(send_ref[...], wo[...])

        @pl.when(t >= 2)
        def _():
            acc[...] += dot_nn(keep_ref[...], wo[...])

        @pl.when(t == 3)
        def _():
            sums[...] = jnp.zeros_like(sums)
            for b in range(blocks):
                rows = slice(b * BLOCK, (b + 1) * BLOCK)
                gate = mod[b : b + 1, 5 * width : 6 * width]
                lower = acc[rows, :] + bo[0:1, :]
                g = cot[rows, :].astype(F32)
                out[rows, :] = (after_ref[rows, :] + gate * lower).astype(BF)
                low[rows, :] = (g * gate).astype(BF)
                sums[b : b + 1, :] = column_sum(g * lower)
            sums[blocks : blocks + 1, :] = column_sum(low[...])

    row = whole((tokens, width))
    chunk = pl.BlockSpec((width, width), lambda t, o: (o[t], 0))
    if parts:
        size = output_w[0].shape[0] // 2
        by_y = pl.BlockSpec((size, width), lambda t, o: (o[t] // 2, 0))
        by_x = pl.BlockSpec((2, 1, size // 2, width), lambda t, o: (0, o[t] // 2, 0, 0))
        weights = [
            v if k % 2 == 0 else v.reshape(2, 2, size // 2, width) for k, v in enumerate(output_w)
        ]
        weight_specs = [by_y, by_x] * 2
        order = jnp.concatenate([order, core])
    else:
        weights, weight_specs = [output_w], [chunk]
    return pl.pallas_call(
        body,
        grid_spec=pltpu.PrefetchScalarGridSpec(
            num_scalar_prefetch=1,
            grid=(4,),
            in_specs=[
                pl.BlockSpec((tokens, width), lambda t, o: (jnp.maximum(t - 2, 0), 0)),
                pl.BlockSpec((tokens, width), lambda t, o: (jnp.minimum(t, 1), 0)),
                *weight_specs,
                whole((8, width)),
                row,
                row,
                whole(mods.shape),
            ],
            out_specs=[
                row,
                row,
                whole((8, width)),
            ]
            + [chunk] * parts,
            scratch_shapes=[pltpu.VMEM((tokens, width), F32)],
        ),
        out_shape=[
            jax.ShapeDtypeStruct((tokens, width), BF),
            jax.ShapeDtypeStruct((tokens, width), BF),
            jax.ShapeDtypeStruct((8, width), F32),
        ]
        + [jax.ShapeDtypeStruct((4 * width, width), BF)] * parts,
        compiler_params=pltpu.CompilerParams(vmem_limit_bytes=VMEM_LIMIT),
        cost_estimate=cost(12),
        name="feed_forward_down",
    )(order, keep, send, *weights, output_b, after, cotangent, mods)


def feed_forward_back(
    grad_lower, slope, hidden_w, output_w, proj, after, branch, attended, lse, cotangent, mods, heads
):
    tokens, width = after.shape
    blocks = tokens // BLOCK
    size = width // heads

    def body(
        gl,
        sl,
        wh,
        wo,
        wp,
        after_ref,
        br,
        low,
        lse_ref,
        cot,
        mod,
        gu,
        ga,
        gat,
        up_sums,
        sums,
        acc,
    ):
        t = pl.program_id(0)
        up = (dot_nt(gl[...], wo[...]) * sl[...].astype(F32)).astype(BF)
        gu[:, pl.ds(pl.multiple_of(t * width, 128), width)] = up
        up_sums[...] = jnp.broadcast_to(column_sum(up), up_sums.shape)
        part = dot_nt(up, wh[...])

        @pl.when(t == 0)
        def _():
            acc[...] = part

        @pl.when(t > 0)
        def _():
            acc[...] += part

        @pl.when(t == 3)
        def _():
            sums[...] = jnp.zeros_like(sums)
            head = lax.broadcasted_iota(jnp.int32, (width, 128), 0)
            first = (lax.broadcasted_iota(jnp.int32, (width, 128), 1) - heads) * size
            pick = ((head >= first) & (head < first + size)).astype(BF)
            total = jnp.zeros((1, width), F32)
            for b in range(blocks):
                rows = slice(b * BLOCK, (b + 1) * BLOCK)
                gin = acc[rows, :]
                normed, inverse = layer_norm(after_ref[rows, :])
                value = cot[rows, :].astype(F32) + norm_back(
                    gin * (1.0 + mod[b : b + 1, 4 * width : 5 * width]), normed, inverse
                )
                ga[rows, :] = value
                sums[b : b + 1, :width] = column_sum(value * br[rows, :])
                sums[b : b + 1, width : 2 * width] = column_sum(gin)
                sums[b : b + 1, 2 * width : 3 * width] = column_sum(gin * normed)
                low_branch = (value * mod[b : b + 1, 2 * width : 3 * width]).astype(BF)
                gu[rows, 4 * width :] = low_branch
                total = total + column_sum(low_branch)
                grad = dot_nt(low_branch, wp[...]).astype(BF)
                gat[rows, :width] = grad
                product = grad.astype(F32) * low[rows, :]
                high = product.astype(BF)
                rest = (product - high.astype(F32)).astype(BF)
                value = lse_ref[rows, :] + dot_nn(high, pick) + dot_nn(rest, pick)
                terms = jnp.zeros((BLOCK, 128), F32)
                for k in range(3):
                    term = value.astype(BF).astype(F32)
                    terms = terms + (pltpu.roll(term, 2 * heads * k, axis=1) if k else term)
                    value = value - term
                gat[rows, width:] = terms.astype(BF)
            sums[blocks : blocks + 1, :width] = total

    row = whole((tokens, width))
    return pl.pallas_call(
        body,
        grid=(4,),
        in_specs=[
            row,
            pl.BlockSpec((tokens, width), lambda t: (0, t)),
            pl.BlockSpec((width, width), lambda t: (0, t)),
            pl.BlockSpec((width, width), lambda t: (t, 0)),
            whole((width, width)),
            row,
            row,
            row,
            whole((tokens, 128)),
            row,
            whole(mods.shape),
        ],
        out_specs=[
            whole((tokens, 5 * width)),
            row,
            whole((tokens, width + 128)),
            pl.BlockSpec((8, width), lambda t: (0, t)),
            whole((8, 3 * width)),
        ],
        out_shape=[
            jax.ShapeDtypeStruct((tokens, 5 * width), BF),
            jax.ShapeDtypeStruct((tokens, width), F32),
            jax.ShapeDtypeStruct((tokens, width + 128), BF),
            jax.ShapeDtypeStruct((8, 4 * width), F32),
            jax.ShapeDtypeStruct((8, 3 * width), F32),
        ],
        scratch_shapes=[pltpu.VMEM((tokens, width), F32)],
        compiler_params=pltpu.CompilerParams(vmem_limit_bytes=VMEM_LIMIT),
        cost_estimate=cost(24),
        name="feed_forward_back",
    )(
        grad_lower,
        slope,
        hidden_w,
        output_w,
        proj,
        after,
        branch,
        attended,
        lse,
        cotangent,
        mods,
    )


def input_gradient(grads, qkv, hidden, grad_after, mods):
    tokens, width = hidden.shape
    blocks = tokens // BLOCK

    def body(gq, gkv, w_ref, hid, ga, mod, out, sums):
        sums[...] = jnp.zeros_like(sums)
        for b in range(blocks):
            rows = slice(b * BLOCK, (b + 1) * BLOCK)
            gin = (
                dot_nt(gq[rows, :], w_ref[:, :width])
                + dot_nt(gkv[rows, :], w_ref[:, width:])
            )
            normed, inverse = layer_norm(hid[rows, :])
            out[rows, :] = ga[rows, :] + norm_back(
                gin * (1.0 + mod[b : b + 1, width : 2 * width]), normed, inverse
            )
            sums[b : b + 1, :width] = column_sum(gin)
            sums[b : b + 1, width : 2 * width] = column_sum(gin * normed)
        sums[blocks : blocks + 1, :width] = column_sum(gq[...])
        sums[blocks : blocks + 1, width : 2 * width] = column_sum(gkv[:, width:])

    row = whole((tokens, width))
    return pl.pallas_call(
        body,
        grid=(1,),
        in_specs=[row, whole((tokens, 2 * width)), whole(qkv.shape), row, row, whole(mods.shape)],
        out_specs=[row, whole((8, 2 * width))],
        out_shape=[
            jax.ShapeDtypeStruct((tokens, width), F32),
            jax.ShapeDtypeStruct((8, 2 * width), F32),
        ],
        compiler_params=pltpu.CompilerParams(vmem_limit_bytes=VMEM_LIMIT),
        cost_estimate=cost(14),
        name="input_gradient",
    )(*grads, qkv, hidden, grad_after, mods)


def halo(v, fast, after=None):
    count = lax.axis_size("blk")
    if not fast:
        right = lax.ppermute(v, "blk", [(i + 1, i) for i in range(count - 1)])
        return right, lax.ppermute(v, "blk", [(i, i + 1) for i in range(count - 1)])
    near = swap(v, "blk", 1)
    if after is not None:
        near, _ = lax.optimization_barrier((near, after))
    return near, lax.ppermute(near, "blk", halo_hops())


def halo_hops():
    count = lax.axis_size("blk")
    return [(i, i + 2) for i in range(0, count - 2, 2)] + [(i + 2, i) for i in range(1, count - 2, 2)]


def halo_flip(fast):
    return lax.axis_index("blk") % 2 if fast else jnp.int32(0)


def place_table(width):
    quarter = width // 4
    frequency = 1.0 / 10000.0 ** (jnp.arange(quarter, dtype=F32) / quarter)
    angle = jnp.arange(BIG_SIDE, dtype=F32)[:, None] * frequency[None, :]
    return jnp.concatenate([jnp.sin(angle), jnp.cos(angle)], axis=1)


def put_slices(pieces, at, total):
    out = []
    for piece, whole in zip(pieces, total):
        out.append(
            lax.dynamic_update_slice_in_dim(
                jnp.zeros((whole,), F32), piece.astype(F32), at * piece.shape[0], 0
            )
        )
    return jnp.concatenate(out)


def per_device(
    tokens,
    condition,
    cotangent,
    segments,
    kept_patch,
    res_class,
    pack_order,
    ada_weight,
    ada_bias,
    qkv_weight,
    query_bias,
    value_bias,
    proj_weight,
    proj_bias,
    hidden_weight,
    hidden_bias,
    output_weight,
    output_bias,
):
    tokens_dev, width = tokens.shape[1], tokens.shape[2]
    segs = condition.shape[1]
    size_dp, size_blk = lax.axis_size("dp"), lax.axis_size("blk")
    own_dp, own_blk = lax.axis_index("dp"), lax.axis_index("blk")
    own_dev = own_dp * size_blk + own_blk
    count = size_dp * size_blk
    rows = width // count
    barrier = lax.optimization_barrier
    fast = size_dp == 4 and size_blk == 8 and rows % 4 == 0
    everyone = ("dp", "blk")
    blocks = tokens_dev // BLOCK

    first = jnp.concatenate(
        [qkv_weight[:, g * width : (g + 1) * width] for g in range(3)] + [proj_weight], axis=0
    )
    second = jnp.concatenate(
        [hidden_weight[:, g * width : (g + 1) * width] for g in range(4)] + [output_weight], axis=0
    )
    x, z = own_blk % 2, own_blk // 2
    core, y = own_dp % 2, own_dp // 2
    image_ids = jnp.arange(segs, dtype=jnp.int32)
    pick_image = pack_order[0][:, None] == image_ids[None, :]
    seg_cond = jnp.dot(pick_image.astype(BF), condition[0], preferred_element_type=F32)
    seg_big = jnp.sum(jnp.where(pick_image, res_class[0][None, :], 0), axis=1)
    seg_len = jnp.where(seg_big == 1, BIG_LEN, SMALL_LEN).astype(jnp.int32)
    earlier = image_ids[None, :] < image_ids[:, None]
    seg_start = jnp.sum(jnp.where(earlier, seg_len[None, :], 0), axis=1)
    window_start = (own_blk - 1) * tokens_dev
    block_pos = window_start + BLOCK * jnp.arange(3 * blocks, dtype=jnp.int32)
    block_seg = jnp.sum((seg_start[None, :] <= block_pos[:, None]).astype(jnp.int32), axis=1) - 1
    block_seg = jnp.clip(block_seg, 0, segs - 1)
    block_pick = block_seg[:, None] == image_ids[None, :]
    block_big = jnp.sum(jnp.where(block_pick, seg_big[None, :], 0), axis=1)
    block_start = jnp.sum(jnp.where(block_pick, seg_start[None, :], 0), axis=1) - window_start
    inside = (block_pos >= 0) & (block_pos < size_blk * tokens_dev)
    block_id = jnp.where(inside, block_seg, -1)
    block_start = jnp.clip(block_start, 0, 3 * tokens_dev - BLOCK)
    own_pick = block_pick[blocks : 2 * blocks].astype(F32)

    silu_cond, silu_pull = jax.vjp(jax.nn.silu, seg_cond)
    silu_low = silu_cond.astype(BF)
    if fast:
        silu_all = dp_gather(silu_low).reshape(4 * segs, width)
    else:
        silu_all = lax.all_gather(silu_low, "dp", axis=0, tiled=True)
    silu_own = lax.dynamic_slice_in_dim(silu_all.T, own_dev * rows, rows, axis=0)
    partial_mod = dot_tn(silu_own, ada_weight).reshape(size_dp, segs, 6 * width)
    bias_rows = put_slices(
        (query_bias, value_bias, proj_bias, hidden_bias, output_bias, ada_bias),
        own_dev,
        (width, width, width, 4 * width, width, 6 * width),
    )
    bias_rows = jnp.pad(bias_rows, (0, 24 * width - bias_rows.shape[0])).reshape(1, 4, 6 * width)
    partial_mod = jnp.concatenate(
        [partial_mod, jnp.broadcast_to(bias_rows, (size_dp, 4, 6 * width))], axis=1
    )
    if fast:
        by_core = partial_mod.reshape(2, 2, segs + 4, 6 * width)
        sent = lax.dynamic_index_in_dim(by_core, 1 - core, 1, keepdims=False)
        kept = lax.dynamic_index_in_dim(by_core, core, 1, keepdims=False)
        kept = kept + swap(sent, "dp", 1)
        sent = lax.dynamic_index_in_dim(kept, 1 - y, 0, keepdims=False).astype(BF)
        kept = lax.dynamic_index_in_dim(kept, y, 0, keepdims=False)
        row_mod = kept + swap(sent, "dp", 2).astype(F32)
        row_mod, ada_pair = barrier((row_mod, pair_up(ada_weight[None], "dp", core, 1)))
        ada_got = swap(ada_pair, "dp", 2)
        for bit in (1, 2, 4):
            low = row_mod.astype(BF)
            row_mod = low.astype(F32) + swap(low, "blk", bit).astype(F32)
    else:
        row_mod = lax.psum_scatter(partial_mod, "dp", scatter_dimension=0, tiled=True)[0]
        row_mod = lax.psum(row_mod, "blk")
    if fast:
        core_only = core.reshape(1).astype(jnp.int32)
        first_line = gather_line(first, z)
        first_line, second_shard = barrier((first_line, second[: 4 * rows]))
        first_halves = gather_cross(first_line, x, y)
        second_pair = pair_up(second_shard, "blk", z // 2, 4)
        first_halves, second_pair = barrier((first_halves, second_pair))
        first_halves = gather_wide(*first_halves, x, y)
        second_line = pair_up(second_pair, "blk", z % 2, 2).reshape(4, 4 * rows, width)
    else:
        first_all = lax.all_gather(first, everyone, axis=0, tiled=True)
        second_all = lax.all_gather(second, everyone, axis=0, tiled=True)
        groups = first_all.reshape(count, 4, rows, width).transpose(1, 0, 2, 3)
        groups = groups.reshape(4, width, width)
        full_qkv = jnp.concatenate([groups[0], groups[1], groups[2]], axis=1)
        full_proj = groups[3]
        pair = second_all.reshape(count, 8 * rows, width)
        hid = pair[:, : 4 * rows].reshape(count, 4, rows, width).transpose(0, 2, 1, 3)
        full_hidden = hid.reshape(width, 4 * width)
        full_output = pair[:, 4 * rows :].reshape(4 * width, width)
    bias_flat = row_mod[segs:].reshape(-1)
    full_query_bias = bias_flat[:width]
    full_value_bias = bias_flat[width : 2 * width]
    full_proj_bias = bias_flat[2 * width : 3 * width]
    full_hidden_bias = bias_flat[3 * width : 7 * width]
    full_output_bias = bias_flat[7 * width : 8 * width]
    modulation = row_mod[:segs] + bias_flat[8 * width : 14 * width][None, :]
    block_pick = jnp.pad(block_pick.astype(F32), ((0, 16 - 3 * blocks), (0, 0)))
    mods = jnp.dot(block_pick, modulation, precision=HIGHEST)
    own_mods = mods[blocks : blocks + 8]

    big = jnp.broadcast_to(block_big[:, None], (3 * blocks, BLOCK)).reshape(-1) == 1
    flip = halo_flip(fast)
    kept_near, kept_far = halo(kept_patch[0], fast)
    kept_all = jnp.concatenate(
        [
            jnp.where(flip == 0, kept_far, kept_near),
            kept_patch[0],
            jnp.where(flip == 0, kept_near, kept_far),
        ]
    )
    row_pos = jnp.where(big, kept_all // BIG_SIDE, kept_all // SMALL_SIDE)
    col_pos = kept_all - row_pos * jnp.where(big, BIG_SIDE, SMALL_SIDE)
    places = jnp.concatenate(
        [col_pos[None], row_pos[None], jnp.zeros((6, 3 * tokens_dev), jnp.int32)], axis=0
    )
    own_tokens, _ = barrier((tokens[0], kept_near))
    tokens_near, tokens_far = halo(own_tokens, fast, second_pair if fast else None)
    core = core if fast else jnp.int32(0)
    core_arg = jnp.stack([core, flip]).astype(jnp.int32)
    attn_in_all, hidden, attn_in_keep, attn_in_send = attention_input(
        core_arg, (tokens_near, tokens[0], tokens_far), places, place_table(width), mods
    )

    if fast:
        attn_in_all, first_halves, second_line, third_shard, ada_got = barrier(
            (attn_in_all, first_halves, second_line, second[4 * rows :], ada_got)
        )
        first_parts = both_cores(*first_halves)
        second_halves = gather_cross(second_line, x, y)
        third_pair = pair_up(third_shard, "blk", z // 2, 4)
        first_parts, second_halves, third_pair = barrier((first_parts, second_halves, third_pair))
        second_halves = gather_wide(*second_halves, x, y)
        third_line = pair_up(third_pair, "blk", z % 2, 2).reshape(4, 4 * rows, width)
        full_qkv, full_proj = unpack_weight(
            core_only,
            first_parts,
            rows,
            [(0, 0), (0, 1), (0, 2), (1, 0)],
            "unpack_first",
        )
    queries = (dot_nn(attn_in_all, full_qkv[:, :width]) + full_query_bias).astype(BF)
    keys = dot_nn(attn_in_all, full_qkv[:, width : 2 * width]).astype(BF)
    values = (dot_nn(attn_in_all, full_qkv[:, 2 * width :]) + full_value_bias).astype(BF)
    own = slice(tokens_dev, 2 * tokens_dev)
    forward_info = jnp.concatenate(
        [block_start[blocks : 2 * blocks], block_big[blocks : 2 * blocks]]
    ).astype(jnp.int32)
    left_id, own_id, right_id = jnp.split(block_id, 3)
    backward_info = jnp.concatenate(
        [
            jnp.where(flip == 0, right_id, left_id),
            own_id,
            jnp.where(flip == 0, left_id, right_id),
            flip[None],
        ]
    ).astype(jnp.int32)
    if fast:
        queries, second_halves, third_line = barrier((queries, second_halves, third_line))
        second_parts = both_cores(*second_halves)
        third_halves = gather_cross(third_line, x, y)
    attn_low, attended, lse = attend_forward(forward_info, queries, keys, values, HEADS)

    def eight(v):
        return jnp.broadcast_to(v[None, :], (8, v.shape[0]))

    if fast:
        attn_low, second_parts, third_halves = barrier((attn_low, second_parts, third_halves))
        third_halves = gather_wide(*third_halves, x, y)
    branch, after_attn, mlp_in, mlp_keep, low_keep, mlp_low_send = after_attention(
        core_arg, attn_low, full_proj, eight(full_proj_bias), hidden, own_mods
    )
    if fast:
        (full_hidden,) = unpack_weight(
            core_only,
            second_parts,
            rows,
            [(0, 0), (0, 1), (0, 2), (0, 3)],
            "unpack_hidden",
        )
        attn_in_send, mlp_low_send = barrier((attn_in_send, mlp_low_send))
        attn_in_oth, mlp_low_oth = swap(attn_in_send, "dp", 1), swap(mlp_low_send, "dp", 1)
        mlp_in, attn_in_oth, mlp_low_oth = lax.optimization_barrier(
            (mlp_in, attn_in_oth, mlp_low_oth)
        )
    order = jnp.stack([1 - core, 3 - core, core, 2 + core]).astype(jnp.int32)
    act_keep, act_send, slope = feed_forward_up(order, mlp_in, full_hidden, eight(full_hidden_bias))
    if fast:
        act_keep, third_halves = barrier((act_keep, third_halves))
        third_parts = both_cores(*third_halves)
        act_oth = swap(act_send, "dp", 1)
        grad_lower, block_out, lower_sums, full_output = feed_forward_down(
            order,
            act_keep,
            act_send,
            third_parts,
            eight(full_output_bias),
            after_attn,
            cotangent[0],
            own_mods,
            core_only,
        )
    else:
        grad_lower, block_out, lower_sums = feed_forward_down(
            order,
            act_keep,
            act_send,
            full_output,
            eight(full_output_bias),
            after_attn,
            cotangent[0],
            own_mods,
        )

    shape = (tokens_dev, width)
    orders = ["yxz", "xyz"]
    if fast:
        bits = jnp.stack([x, y, z % 2, z // 2]).astype(jnp.int32)

        def step_1(halves):
            return send(halves[0], "dp", 2), send(halves[1], "blk", 1)

        def step_2(halves):
            return send(halves[0], "blk", 1), send(halves[1], "dp", 2)

        def step_3(halves):
            return send(halves, "blk", 2)

        def step_4(halves):
            return send(halves, "blk", 4)

        def half_2(got):
            return add_and_cut(*got)

        def half_3(got):
            return add_and_cut_z(*got)

        half_4 = add_and_cut_last

        def cut(*tasks):
            found = run_together(bits, *tasks)
            return found[0] if len(tasks) == 1 else found

        act_keep, act_oth, grad_lower_oth = barrier((act_keep, act_oth, swap(grad_lower, "dp", 1)))
        third = chip_grads(
            bits,
            [(act_keep, act_oth)],
            [(grad_lower, grad_lower_oth, 0, 0)],
            [(0, 0, 4 * rows, [(0, 2 * rows, 0, 0), (2 * rows, 2 * rows, 1, 0)])],
            orders,
            False,
            shape,
            "grad_output_weight",
        )
        grad_lower, third = barrier((grad_lower, third))
        third = step_1(third)
    grad_upper, grad_after, grad_attn, upper_sums, branch_sums = feed_forward_back(
        grad_lower,
        slope,
        full_hidden,
        full_output,
        full_proj,
        after_attn,
        branch,
        attended,
        lse,
        cotangent[0],
        own_mods,
        HEADS,
    )

    def to_segments(sums):
        return lax.dot_general(
            own_pick, sums[:blocks], (((0,), (0,)), ((), ())), precision=HIGHEST
        )

    def early_message():
        bias = jnp.concatenate(
            [
                branch_sums[blocks, :width],
                upper_sums[0],
                lower_sums[blocks],
                jnp.zeros((2 * width,), F32),
            ]
        )
        return jnp.concatenate(
            [
                to_segments(jnp.concatenate([branch_sums, lower_sums], axis=1)),
                bias.reshape(2, 4 * width),
            ],
            axis=0,
        )

    def late_message(sums):
        return jnp.concatenate([to_segments(sums), sums[blocks : blocks + 1]], axis=0)

    if not fast:
        grad_near, grad_far = halo(grad_attn, fast)
    else:

        early = early_message()
        grad_attn, grad_upper, third, early = barrier((grad_attn, grad_upper, third, early))
        grad_upper_oth = swap(grad_upper, "dp", 1)
        grad_near = swap(grad_attn, "blk", 1)
        early_got = swap_exact(early, 1, 2)
        third = cut(half_2(third))
    grad_q, grad_k_own, grad_v_own = attend_backward_own(
        forward_info, queries, keys, values, grad_attn, HEADS
    )
    if fast:
        mlp_keep, grad_q, grad_near, grad_upper_oth, early, early_got, third = barrier(
            (mlp_keep, grad_q, grad_near, grad_upper_oth, early, early_got, third)
        )
        grad_far = lax.ppermute(grad_near, "blk", halo_hops())
        grad_q_oth = swap(grad_q, "dp", 1)
        third = step_2(third)
        early = early + early_got
        early_got = swap_exact(early, 2, 2)
        second = chip_grads(
            bits,
            [(mlp_keep, mlp_low_oth)],
            [(grad_upper, grad_upper_oth, 0, g) for g in range(4)],
            [(0, g, rows, [(0, rows, g // 2, g % 2 * rows)]) for g in range(4)],
            orders,
            True,
            shape,
            "grad_hidden_weight",
        )
        attn_in_keep, grad_q_oth, second = barrier((attn_in_keep, grad_q_oth, second))
        first = chip_grads(
            bits,
            [(attn_in_keep, attn_in_oth), (low_keep, mlp_low_oth[width // 2 :])],
            [(grad_q, grad_q_oth, 0, 0), (grad_upper, grad_upper_oth, 0, 4)],
            [(0, 0, rows, [(0, rows, 0, 0)]), (1, 1, rows, [(0, rows, 1, 0)])],
            orders,
            True,
            shape,
            "grad_query_weight",
        )

        grad_far, first, second, third, early, early_got = barrier(
            (grad_far, first, second, third, early, early_got)
        )
        second = step_1(second)
        third = step_3(cut(half_3(third)))
        early = early + early_got
        early_got = swap_exact(early, 4, 2)
    grad_kv = attend_backward_other(
        backward_info,
        queries,
        keys,
        values,
        grad_near,
        grad_far,
        grad_k_own,
        grad_v_own,
        HEADS,
    )
    if fast:
        grad_kv, hidden, first, second, third, early, early_got = barrier(
            (grad_kv, hidden, first, second, third, early, early_got)
        )
        second, third = cut(half_2(second), half_4(third))
        hidden, first, second, third = barrier((hidden, first, second, third))
        first = step_1(first)
        second = step_2(second)
        third = step_4(third)
        early_row = early + early_got
    grad_tokens, input_sums = input_gradient(
        (grad_q, grad_kv), full_qkv, hidden, grad_after, own_mods
    )
    if fast:
        attn_in_keep, grad_kv, first, second, third, input_sums, early_row = barrier(
            (attn_in_keep, grad_kv, first, second, third, input_sums, early_row)
        )
        late = late_message(input_sums)
        grad_kv_oth = swap(grad_kv, "dp", 1)
        late_got = swap_exact(late, 1, 1)
        second, first = cut(half_3(second), half_2(first))
        second = step_3(second)
        first = step_2(first)
        third_sum = add(*third)
        last = chip_grads(
            bits,
            [(attn_in_keep, attn_in_oth)],
            [(grad_kv, grad_kv_oth, 0, 0), (grad_kv, grad_kv_oth, 0, 1)],
            [(0, 0, rows, [(0, rows, 0, 0)]), (0, 1, rows, [(0, rows, 1, 0)])],
            orders,
            True,
            shape,
            "grad_key_weight",
        )

        last, first, second, late, late_got, early_row = barrier(
            (last, first, second, late, late_got, early_row)
        )
        last = step_1(last)
        late = late + late_got
        late_got = swap_exact(late, 2, 1)
        second, first = cut(half_4(second), half_3(first))
        second = step_4(second)
        first = step_3(first)

        last, first, second, late, late_got, early_row = barrier(
            (last, first, second, late, late_got, early_row)
        )
        late = late + late_got
        late_got = swap_exact(late, 4, 1)
        last, first = cut(half_2(last), half_4(first))
        last = step_2(last)
        first = step_4(first)
        early_pair = pair_up(early_row[None], "dp", core, 1)
        second_sum = add(*second)

        last, first, late, late_got, early_pair = barrier((last, first, late, late_got, early_pair))
        late_row = late + late_got
        ada_rows = jnp.concatenate(
            [jnp.where(y == 0, ada_pair, ada_got), jnp.where(y == 0, ada_got, ada_pair)], axis=0
        ).reshape(4 * rows, 6 * width)
        own_row = jnp.concatenate([late_row[:segs], early_row[:segs]], axis=1)
        row_high = lax.reduce_precision(own_row, 8, 7)
        row_rest = (own_row - row_high).astype(BF)
        part = dot_nt(ada_rows, row_high.astype(BF)) + dot_nt(ada_rows, row_rest)
        parts = [part] + [swap(part, "blk", bit) for bit in (2, 4, 6)]
        last = step_3(cut(half_3(last)))
        late_pair = pair_up(late_row[None], "dp", core, 1)
        first_sum = add(*first)

        last, parts, late_pair, early_pair = barrier((last, parts, late_pair, early_pair))
        low = [jnp.where(z % 2 == 0, a, b) for a, b in ((parts[0], parts[1]), (parts[2], parts[3]))]
        high = [jnp.where(z % 2 == 0, b, a) for a, b in ((parts[0], parts[1]), (parts[2], parts[3]))]
        line = jnp.stack(
            [
                jnp.where(z // 2 == 0, low[0], low[1]),
                jnp.where(z // 2 == 0, high[0], high[1]),
                jnp.where(z // 2 == 0, low[1], low[0]),
                jnp.where(z // 2 == 0, high[1], high[0]),
            ]
        )
        part = pair_up(line[None], "blk", x, 1)
        last = step_4(cut(half_4(last)))
        late_all = pair_up(late_pair, "dp", y, 2)
        early_all = pair_up(early_pair, "dp", y, 2)
        last_sum = add(*last)

    if not fast:
        early_row, late_row = (
            lax.psum(v, "blk") for v in (early_message(), late_message(input_sums))
        )
        early_all, late_all = (
            lax.all_gather(v, "dp", axis=0, tiled=False) for v in (early_row, late_row)
        )
    mod_all = jnp.concatenate([late_all[:, :segs], early_all[:, :segs]], axis=2)
    mod_all = mod_all.reshape(-1, 6 * width)
    early_bias = jnp.sum(early_all[:, segs:], axis=0).reshape(-1)
    late_bias = jnp.sum(late_all[:, segs:], axis=0).reshape(-1)

    def take(v, n):
        return lax.dynamic_slice_in_dim(v, own_dev * n, n)

    grad_query_bias = take(late_bias[:width], rows)
    grad_value_bias = take(late_bias[width:], rows)
    grad_proj_bias = take(early_bias[:width], rows)
    grad_hidden_bias = take(early_bias[width : 5 * width], 4 * rows)
    grad_output_bias = take(early_bias[5 * width : 6 * width], rows)
    grad_ada_bias = take(jnp.sum(mod_all, axis=0), 6 * rows)
    mod_high = mod_all.astype(BF)
    mod_rest = (mod_all - mod_high.astype(F32)).astype(BF)
    grad_ada_weight = dot_nn(silu_own, mod_high) + dot_nn(silu_own, mod_rest)
    if fast:
        part = part.reshape(2, 4, 4, rows, segs).transpose(4, 2, 1, 0, 3)
        own_silu = part.reshape(segs, width)
    else:
        silu_grad = dot_nt(ada_weight, mod_high) + dot_nt(ada_weight, mod_rest)
        silu_rows = lax.all_gather(silu_grad, everyone, axis=0, tiled=True)
        own_silu = lax.dynamic_slice_in_dim(silu_rows, own_dp * segs, segs, axis=1).T
    grad_seg_cond = silu_pull(own_silu)[0]
    grad_image = lax.dot_general(
        pick_image.astype(F32), grad_seg_cond, (((0,), (0,)), ((), ())), precision=HIGHEST
    )

    if fast:
        grad_qkv_weight = jnp.concatenate(
            [first_sum[:rows], last_sum[:rows], last_sum[rows:]], axis=1
        )
        grad_proj_weight = first_sum[rows:]
        grad_hidden_weight = jnp.concatenate(
            [second_sum[g * rows : (g + 1) * rows] for g in range(4)], axis=1
        )
        grad_output_weight = third_sum
    else:

        def scattered(left_t, right):
            product = dot_nn(left_t, right).astype(BF)
            product = lax.psum_scatter(product, "dp", scatter_dimension=0, tiled=True)
            return lax.psum_scatter(product, "blk", scatter_dimension=0, tiled=True).astype(F32)

        def in_order(keep, send):
            both = jnp.stack([keep.reshape(2, -1, tokens_dev), send.reshape(2, -1, tokens_dev)], axis=1)
            return both.reshape(-1, tokens_dev)

        attn_in_t = in_order(attn_in_keep, attn_in_send)
        mlp_send, low_send = mlp_low_send[: width // 2], mlp_low_send[width // 2 :]
        grad_qkv_weight = scattered(attn_in_t, jnp.concatenate([grad_q, grad_kv], axis=1))
        grad_proj_weight = scattered(in_order(low_keep, low_send), grad_upper[:, 4 * width :])
        grad_hidden_weight = scattered(in_order(mlp_keep, mlp_send), grad_upper[:, : 4 * width])
        act = jnp.stack(
            [act_keep.reshape(2, tokens_dev, width), act_send.reshape(2, tokens_dev, width)], axis=1
        ).reshape(4, tokens_dev, width)
        act_t = act.transpose(0, 2, 1).reshape(4 * width, tokens_dev)
        grad_output_weight = scattered(act_t, grad_lower)
    return (
        block_out[None],
        grad_tokens[None],
        grad_image[None],
        grad_ada_weight,
        grad_ada_bias,
        grad_qkv_weight,
        grad_query_bias,
        grad_value_bias,
        grad_proj_weight,
        grad_proj_bias,
        grad_hidden_weight,
        grad_hidden_bias,
        grad_output_weight,
        grad_output_bias,
    )


def solution(mesh):
    row = P("dp", "blk", None)
    ints = P("dp", "blk")
    image = P("dp", None)
    matrix = P(("dp", "blk"), None)
    vector = P(("dp", "blk"))
    return jax.shard_map(
        per_device,
        mesh=mesh,
        in_specs=(
            row,
            P("dp", None, None),
            row,
            ints,
            ints,
            image,
            image,
            matrix,
            vector,
            matrix,
            vector,
            vector,
            matrix,
            vector,
            matrix,
            vector,
            matrix,
            vector,
        ),
        out_specs=(
            row,
            row,
            P("dp", None, None),
            matrix,
            vector,
            matrix,
            vector,
            vector,
            matrix,
            vector,
            matrix,
            vector,
            matrix,
            vector,
        ),
        check_vma=False,
    )
```
